32 devices in a mesh: dp: 16 (over z, y, x), fsdp: 2 (over core).
Axes of the slice: x: 2, y: 2, z: 4, core: 2. Of those that a mesh axis runs over, the one named last changes fastest.
Arguments:
- tokens: bfloat16 [4096, 1024], P(('dp', 'fsdp')), may hold values from -6 to 6
- dealing: int32 [4096], P(('dp', 'fsdp')), may hold values from 0 to 4095, as said below
- lengths: int32 [32, 1], P(('dp', 'fsdp')), may hold values from 0 to 128, as said below
- norm1_gain: bfloat16 [1024], P(('dp', 'fsdp')), may hold values from 0.099609375 to 1.8984375
- w_query: bfloat16 [1048576], P(('dp', 'fsdp')), may hold values from -0.1875 to 0.1875
- w_key: bfloat16 [1048576], P(('dp', 'fsdp')), may hold values from -0.1875 to 0.1875
- w_value: bfloat16 [1048576], P(('dp', 'fsdp')), may hold values from -0.1875 to 0.1875
- w_out: bfloat16 [1048576], P(('dp', 'fsdp')), may hold values from -1 to 1
- norm2_gain: bfloat16 [1024], P(('dp', 'fsdp')), may hold values from 0.099609375 to 1.8984375
- w_gate: bfloat16 [2818048], P(('dp', 'fsdp')), may hold values from -0.1875 to 0.1875
- w_up: bfloat16 [2818048], P(('dp', 'fsdp')), may hold values from -0.1875 to 0.1875
- w_down: bfloat16 [2818048], P(('dp', 'fsdp')), may hold values from -0.109375 to 0.109375
- cotangent: bfloat16 [4096, 1024], P(('dp', 'fsdp')), may hold values from -6 to 6
Outputs:
- layer_out: bfloat16 [4096, 1024], P(('dp', 'fsdp'))
- input_grad: bfloat16 [4096, 1024], P(('dp', 'fsdp'))
- grad_norm1_gain: float32 [1024], P(('dp', 'fsdp'))
- grad_w_query: float32 [1048576], P(('dp', 'fsdp'))
- grad_w_key: float32 [1048576], P(('dp', 'fsdp'))
- grad_w_value: float32 [1048576], P(('dp', 'fsdp'))
- grad_w_out: float32 [1048576], P(('dp', 'fsdp'))
- grad_norm2_gain: float32 [1024], P(('dp', 'fsdp'))
- grad_w_gate: float32 [2818048], P(('dp', 'fsdp'))
- grad_w_up: float32 [2818048], P(('dp', 'fsdp'))
- grad_w_down: float32 [2818048], P(('dp', 'fsdp'))
The draws below stay inside these ranges and needn't reach their ends.
Inputs may be any that keep to these rules, and one draw needn't show every extreme that they name: dealing is a permutation of the dealt indices. The home device with dp index h and fsdp index f holds exactly the dealt indices of the devices with fsdp index f at local positions h * 8 to (h + 1) * 8 - 1, 8 from each such device, in drawn order. `lengths`: each row lists whole sequences that fill its device: entries are multiples of 128, nonzero ones come first and sum to 128; some device holds one sequence of 128 tokens.
All inputs are finite; a program needn't handle non-finite values.
Results may differ from the reference program's by a relative error of at most 0.012.
The reference program's roundings to bfloat16 on the way count: a program that leaves them out, or rounds other values in their place, can miss the bound.
Values may be sent and summed in bfloat16 or wider, within the bound.
A program may use at most 256 MiB of HBM per device.

```python
import jax
import jax.numpy as jnp
from jax import lax

D = 1024
HEADS = 16
HEAD = 64
FF = 2752
WINDOW = 64
UNIT = 128
TOK_DEV = 128
TOKENS = 4096
N_DP = 16
N_FSDP = 2


def draw_dealing(key, part):
    dev_count = N_DP * N_FSDP
    per_peer = TOK_DEV // N_DP
    device_ids = jnp.arange(dev_count, dtype=jnp.int32)[:, None]
    columns = jnp.arange(TOK_DEV, dtype=jnp.int32)[None, :]
    home_dp = device_ids // N_FSDP
    home_fsdp = device_ids % N_FSDP
    target_dp = columns // per_peer
    within = columns % per_peer
    ordered = (target_dp * N_FSDP + home_fsdp) * TOK_DEV + home_dp * per_peer + within
    row_keys = jax.random.split(key, dev_count)
    shuffled = jax.vmap(lambda row_key, row_vals: jax.random.permutation(row_key, row_vals))(row_keys, ordered)
    return shuffled.reshape(-1).astype(jnp.int32)


def draw_lengths(key, part):
    dev_count = N_DP * N_FSDP
    slot_count = TOK_DEV // UNIT
    cuts = jax.random.randint(key, (dev_count, slot_count - 1), 0, 2).astype(jnp.int32)
    single = jax.random.randint(jax.random.fold_in(key, 7), (), 0, dev_count).astype(jnp.int32)
    device_ids = jnp.arange(dev_count, dtype=jnp.int32)[:, None]
    cuts = jnp.where(device_ids == single, 0, cuts)
    unit_ids = jnp.concatenate([jnp.zeros((dev_count, 1), jnp.int32), jnp.cumsum(cuts, axis=1).astype(jnp.int32)], axis=1)
    matches = (unit_ids[:, :, None] == jnp.arange(slot_count, dtype=jnp.int32)[None, None, :]).astype(jnp.int32)
    return (jnp.sum(matches, axis=1) * UNIT).astype(jnp.int32)


def steps_of(key, shape, pieces, least, high):
    gain = 1.0
    for position, shards_of in pieces:
        steps = jax.random.uniform(jax.random.fold_in(jax.random.fold_in(key, 6), position), (shards_of,), jnp.float32, least / len(pieces), high / len(pieces))
        gain = gain * jnp.repeat(jnp.exp(steps), shape[position] // shards_of).reshape((-1,) + (1,) * (len(shape) - 1 - position))
    return gain


def noise(stream_key, shape, spread, bound, shards=(), kind=jnp.bfloat16):
    factor_of = steps_of(stream_key, shape, shards, -0.22, 0.18) if shards else 1.0
    entries = jax.random.normal(stream_key, shape, jnp.float32) * spread * factor_of
    return jnp.minimum(jnp.maximum(entries, -bound), bound).astype(kind)


def setup_inputs(seed: int = 0) -> dict:
    key_of = jax.random.split(jax.random.key(seed), 14)
    tokens = noise(key_of[0], (TOKENS, D), 1.0, 6.0, ((0, 32),))
    dealing = draw_dealing(jax.random.fold_in(key_of[13], 71), 0)
    lengths = draw_lengths(jax.random.fold_in(key_of[13], 71), 0)
    norm1_gain = jnp.clip(1.0 + 0.18 * jax.random.normal(key_of[3], (D,), jnp.float32), 0.099609375, 1.8984375).astype(jnp.bfloat16)
    w_query = noise(key_of[4], (D * D,), D ** -0.5, 0.1875, ((0, 32),))
    w_key = noise(key_of[5], (D * D,), D ** -0.5, 0.1875, ((0, 32),))
    w_value = noise(key_of[6], (D * D,), D ** -0.5, 0.1875, ((0, 32),))
    w_out = noise(key_of[7], (D * D,), (D // 32) ** -0.5, 1.0, ((0, 32),))
    norm2_gain = jnp.clip(1.0 + 0.18 * jax.random.normal(key_of[8], (D,), jnp.float32), 0.099609375, 1.8984375).astype(jnp.bfloat16)
    w_gate = noise(key_of[9], (D * FF,), D ** -0.5, 0.1875, ((0, 32),))
    w_up = noise(key_of[10], (D * FF,), D ** -0.5, 0.1875, ((0, 32),))
    w_down = noise(key_of[11], (FF * D,), FF ** -0.5, 0.109375, ((0, 32),))
    cotangent = noise(key_of[12], (TOKENS, D), 1.0, 6.0, ((0, 32),))
    return dict(tokens=tokens, dealing=dealing, lengths=lengths, norm1_gain=norm1_gain, w_query=w_query, w_key=w_key, w_value=w_value, w_out=w_out, norm2_gain=norm2_gain, w_gate=w_gate, w_up=w_up, w_down=w_down, cotangent=cotangent)


@jax.custom_vjp
def low(v):
    return lax.optimization_barrier(v.astype(jnp.bfloat16)).astype(jnp.float32)

@jax.custom_vjp
def low_back(v):
    return v

def low_keep(v):
    return (low(v), None)

def low_pass(kept, grad):
    return (grad,)

def back_keep(v):
    return (v, None)

def back_low(kept, grad):
    return (low(grad),)
low.defvjp(low_keep, low_pass)
low_back.defvjp(back_keep, back_low)
EPSILON = 1e-06

def normalize(values, gain_vec):
    meansq = lax.optimization_barrier(jnp.mean(values * values, axis=-1, keepdims=True))
    return values * lax.rsqrt(meansq + EPSILON) * gain_vec

def block_mask(segment):
    block_count = TOK_DEV // WINDOW
    segment = segment.astype(jnp.int32)
    padded = jnp.concatenate([jnp.full((WINDOW,), -1, jnp.int32), segment])
    seg_query = segment.reshape(block_count, WINDOW)
    seg_keys = jnp.concatenate([padded[:-WINDOW].reshape(block_count, WINDOW), seg_query], axis=1)
    offset = jnp.arange(WINDOW)[:, None] - jnp.arange(2 * WINDOW)[None, :] + WINDOW
    inside = (offset >= 0) & (offset < WINDOW)
    return inside[None] & (seg_query[:, :, None] == seg_keys[:, None, :])

def key_blocks(values):
    block_count = TOK_DEV // WINDOW
    padded = jnp.concatenate([jnp.zeros((WINDOW,) + values.shape[1:], values.dtype), values])
    previous = padded[:-WINDOW].reshape((block_count, WINDOW) + values.shape[1:])
    current = values.reshape((block_count, WINDOW) + values.shape[1:])
    return jnp.concatenate([previous, current], axis=1)

def attend(inputs):
    query_act, key_act, value_act, segment = inputs
    block_count = TOK_DEV // WINDOW
    query_blk = query_act.reshape(block_count, WINDOW, HEADS, HEAD)
    key_blk = key_blocks(key_act.reshape(TOK_DEV, HEADS, HEAD))
    value_blk = key_blocks(value_act.reshape(TOK_DEV, HEADS, HEAD))
    scores = jnp.einsum('bahd,bchd->bhac', query_blk, key_blk, precision=lax.Precision.HIGHEST) * HEAD ** (-0.5)
    scores = low_back(scores)
    key_mask = block_mask(segment)[:, None]
    scores = jnp.where(key_mask, scores, -1e+30)
    probs = low(jax.nn.softmax(scores, axis=-1))
    result = jnp.einsum('bhac,bchd->bahd', probs, value_blk, precision=lax.Precision.HIGHEST)
    return result.reshape(TOK_DEV, D)

def forward(params, inputs, segments):
    gain_one, query_w, key_w, value_w, out_w, gain_two, gate_w, up_w, down_w = params
    normed_one = low(normalize(inputs, gain_one))

    def project(weight_mat):
        return low(low_back(jnp.dot(normed_one, weight_mat, precision=lax.Precision.HIGHEST)))
    query_act = project(query_w)
    key_act = project(key_w)
    value_act = project(value_w)
    dev_count = inputs.shape[0] // TOK_DEV
    attended = lax.map(jax.checkpoint(attend), (query_act.reshape(dev_count, TOK_DEV, D), key_act.reshape(dev_count, TOK_DEV, D), value_act.reshape(dev_count, TOK_DEV, D), segments))
    attended = low(low_back(attended.reshape(-1, D)))
    branch = low_back(jnp.dot(attended, out_w, precision=lax.Precision.HIGHEST))
    middle = inputs + branch
    normed_two = low(normalize(middle, gain_two))
    gate_pre = low_back(jnp.dot(normed_two, gate_w, precision=lax.Precision.HIGHEST))
    up_pre = low_back(jnp.dot(normed_two, up_w, precision=lax.Precision.HIGHEST))
    hidden = low(jax.nn.silu(gate_pre) * up_pre)
    return middle + jnp.dot(hidden, down_w, precision=lax.Precision.HIGHEST)

def reference(tokens, dealing, lengths, norm1_gain, w_query, w_key, w_value, w_out, norm2_gain, w_gate, w_up, w_down, cotangent):
    row_count = tokens.shape[0]
    dealing = dealing.astype(jnp.int32)
    dealt_rows = jnp.zeros((row_count, D), jnp.float32).at[dealing].set(tokens.astype(jnp.float32))
    dealt_cot = jnp.zeros((row_count, D), jnp.float32).at[dealing].set(cotangent.astype(jnp.float32))
    bounds = jnp.cumsum(lengths.astype(jnp.int32), axis=1)
    positions = jnp.arange(TOK_DEV, dtype=jnp.int32)
    segments = lax.optimization_barrier(jnp.sum((positions[None, :, None] >= bounds[:, None, :]).astype(jnp.int32), axis=-1)).astype(jnp.int32)
    params = (norm1_gain.astype(jnp.float32), w_query.astype(jnp.float32).reshape(D, D), w_key.astype(jnp.float32).reshape(D, D), w_value.astype(jnp.float32).reshape(D, D), w_out.astype(jnp.float32).reshape(D, D), norm2_gain.astype(jnp.float32), w_gate.astype(jnp.float32).reshape(D, FF), w_up.astype(jnp.float32).reshape(D, FF), w_down.astype(jnp.float32).reshape(FF, D))
    layer_val, pullback = jax.vjp(lambda weights, inputs: forward(weights, inputs, segments), params, dealt_rows)
    weight_grads, input_back = pullback(dealt_cot)
    layer_home = layer_val[dealing].astype(jnp.bfloat16)
    input_home = input_back[dealing].astype(jnp.bfloat16)
    grad_gain_one, grad_query, grad_key, grad_value, grad_out, grad_gain_two, grad_gate, grad_up, grad_down = weight_grads
    return (layer_home, input_home, grad_gain_one, grad_query.reshape(-1), grad_key.reshape(-1), grad_value.reshape(-1), grad_out.reshape(-1), grad_gain_two, grad_gate.reshape(-1), grad_up.reshape(-1), grad_down.reshape(-1))
```

```python
import functools
from types import SimpleNamespace

import jax
import jax.numpy as jnp
from jax import lax
from jax.experimental import pallas as pl
from jax.experimental.pallas import tpu as pltpu
from jax.sharding import PartitionSpec as P

HEAD = 64
WINDOW = 64


EPSILON = 1e-06


def unpack(flat_list, model_width):
    gain_one, query_w, key_w, value_w, out_w, gain_two, gate_w, up_w, down_w = flat_list
    hidden_units = gate_w.shape[0] // model_width
    return (
        gain_one.astype(jnp.float32),
        query_w.reshape(model_width, model_width),
        key_w.reshape(model_width, model_width),
        value_w.reshape(model_width, model_width),
        out_w.reshape(model_width, model_width),
        gain_two.astype(jnp.float32),
        gate_w.reshape(model_width, hidden_units),
        up_w.reshape(model_width, hidden_units),
        down_w.reshape(hidden_units, model_width),
    )


def normalize(values, gain_vec):
    inverse = lax.rsqrt(jnp.mean(values * values, axis=-1, keepdims=True) + EPSILON)
    unit_rows = values * inverse
    return (unit_rows * gain_vec, unit_rows, inverse)


def norm_back(upstream, gain_vec, unit_rows, inverse):
    scaled = upstream * gain_vec
    return inverse * (scaled - unit_rows * jnp.mean(scaled * unit_rows, axis=-1, keepdims=True))


def dot_rows(first_op, second_op):
    return lax.dot_general(
        first_op, second_op, (((0,), (0,)), ((), ())), preferred_element_type=jnp.float32
    )


def dot_back(first_op, second_op):
    return lax.dot_general(
        first_op, second_op, (((1,), (1,)), ((), ())), preferred_element_type=jnp.float32
    )


def flat_piece(entry, count, pieces):
    if entry[0] == "gain":
        vector = entry[1]
        share = vector.shape[0] // pieces
        return vector.reshape(count, share)
    left_op, right_op = (entry[1], entry[2])
    row_total = left_op.shape[1]
    col_total = right_op.shape[1]
    share = row_total * col_total // pieces
    block = dot_rows(left_op, right_op)
    flat = block.reshape(-1)
    return flat.reshape(count, share)


def term_maker(entries, pieces, count):
    return jnp.concatenate([flat_piece(entry, count, pieces) for entry in entries], axis=1)


def split_spans(summed, entries, pieces):
    flat = summed.reshape(-1)
    results = []
    offset = 0
    for entry in entries:
        if entry[0] == "gain":
            share = entry[1].shape[0] // pieces
        else:
            share = entry[1].shape[1] * entry[2].shape[1] // pieces
        results.append(flat[offset : offset + share])
        offset = offset + share
    return results


def block_mask(segment, tok_rows):
    block_count = tok_rows // WINDOW
    padded = jnp.concatenate([jnp.full((WINDOW,), -1, jnp.int32), segment])
    seg_query = segment.reshape(block_count, WINDOW)
    seg_keys = jnp.concatenate([padded[:-WINDOW].reshape(block_count, WINDOW), seg_query], axis=1)
    offset = jnp.arange(WINDOW)[:, None] - jnp.arange(2 * WINDOW)[None, :] + WINDOW
    inside = (offset >= 0) & (offset < WINDOW)
    return inside[None] & (seg_query[:, :, None] == seg_keys[:, None, :])


def key_blocks(values, block_count):
    padded = jnp.concatenate([jnp.zeros((WINDOW,) + values.shape[1:], values.dtype), values])
    previous = padded[:-WINDOW].reshape((block_count, WINDOW) + values.shape[1:])
    current = values.reshape((block_count, WINDOW) + values.shape[1:])
    return jnp.concatenate([previous, current], axis=1)


def fold_keys(key_parts, tok_rows, model_width):
    previous = key_parts[:, :WINDOW]
    current = key_parts[:, WINDOW:]
    shifted = jnp.concatenate([previous[1:], jnp.zeros_like(previous[:1])], axis=0)
    return (current + shifted).reshape(tok_rows, model_width)


def masked_scores(query_blk, key_blk, key_mask):
    scores = jnp.einsum(
        "bahd,bchd->bhac", query_blk, key_blk, preferred_element_type=jnp.float32
    ) * HEAD ** (-0.5)
    return jnp.where(key_mask, scores, -1e30)


def body(
    tokens,
    dealing,
    lengths,
    norm1_gain,
    w_query,
    w_key,
    w_value,
    w_out,
    norm2_gain,
    w_gate,
    w_up,
    w_down,
    cotangent,
):
    tok_rows, model_width = tokens.shape
    dp_count = lax.axis_size("dp")
    fsdp_count = lax.axis_size("fsdp")
    pieces = lax.axis_size(("dp", "fsdp"))
    per_peer = tok_rows // dp_count
    local_pos = dealing % tok_rows
    target_dp = dealing // tok_rows // fsdp_count
    send_slot = target_dp * per_peer + local_pos % per_peer
    sent_tokens = jnp.zeros_like(tokens).at[send_slot].set(tokens)
    sent_cot = jnp.zeros_like(cotangent).at[send_slot].set(cotangent)
    inputs, incoming = (
        lax.all_to_all(sent_tokens, "dp", split_axis=0, concat_axis=0, tiled=True),
        lax.all_to_all(sent_cot, "dp", split_axis=0, concat_axis=0, tiled=True),
    )
    bounds = jnp.cumsum(lengths[0])
    positions = jnp.arange(tok_rows, dtype=jnp.int32)
    segment = jnp.sum((positions[:, None] >= bounds[None, :]).astype(jnp.int32), axis=1)
    block_count = tok_rows // WINDOW
    head_count = model_width // HEAD
    key_mask = block_mask(segment, tok_rows)[:, None]
    flat_weights = (norm1_gain, w_query, w_key, w_value, w_out, norm2_gain, w_gate, w_up, w_down)
    gathered = (
        lax.all_gather(flat_weights[0], ("dp", "fsdp"), axis=0, tiled=True),
        lax.all_gather(flat_weights[1], ("dp", "fsdp"), axis=0, tiled=True),
        lax.all_gather(flat_weights[2], ("dp", "fsdp"), axis=0, tiled=True),
        lax.all_gather(flat_weights[3], ("dp", "fsdp"), axis=0, tiled=True),
        lax.all_gather(flat_weights[4], ("dp", "fsdp"), axis=0, tiled=True),
        lax.all_gather(flat_weights[5], ("dp", "fsdp"), axis=0, tiled=True),
        lax.all_gather(flat_weights[6], ("dp", "fsdp"), axis=0, tiled=True),
        lax.all_gather(flat_weights[7], ("dp", "fsdp"), axis=0, tiled=True),
        lax.all_gather(flat_weights[8], ("dp", "fsdp"), axis=0, tiled=True),
    )
    gain_one, query_w, key_w, value_w, out_w, gain_two, gate_w, up_w, down_w = unpack(
        gathered, model_width
    )
    input_f = inputs.astype(jnp.float32)
    scaled_one, unit_one, inverse_one = normalize(input_f, gain_one)
    normed_one = scaled_one.astype(jnp.bfloat16)
    query_act = jnp.dot(normed_one, query_w, preferred_element_type=jnp.float32).astype(
        jnp.bfloat16
    )
    key_act = jnp.dot(normed_one, key_w, preferred_element_type=jnp.float32).astype(jnp.bfloat16)
    value_act = jnp.dot(normed_one, value_w, preferred_element_type=jnp.float32).astype(
        jnp.bfloat16
    )
    query_blk = query_act.reshape(block_count, WINDOW, head_count, HEAD)
    key_blk = key_blocks(key_act.reshape(tok_rows, head_count, HEAD), block_count)
    value_blk = key_blocks(value_act.reshape(tok_rows, head_count, HEAD), block_count)
    scores = masked_scores(query_blk, key_blk, key_mask)
    row_peak = jnp.max(scores, axis=-1, keepdims=True)
    exp_scores = jnp.exp(scores - row_peak)
    row_total = jnp.sum(exp_scores, axis=-1, keepdims=True)
    log_total = row_peak + jnp.log(row_total)
    probs_low = (exp_scores / row_total).astype(jnp.bfloat16)
    attended = jnp.einsum(
        "bhac,bchd->bahd", probs_low, value_blk, preferred_element_type=jnp.float32
    )
    attended = attended.reshape(tok_rows, model_width).astype(jnp.bfloat16)
    middle = input_f + jnp.dot(attended, out_w, preferred_element_type=jnp.float32)
    scaled_two, unit_two, inverse_two = normalize(middle, gain_two)
    normed_two = scaled_two.astype(jnp.bfloat16)
    gate_pre = jnp.dot(normed_two, gate_w, preferred_element_type=jnp.float32)
    up_pre = jnp.dot(normed_two, up_w, preferred_element_type=jnp.float32)
    sigmoid_gate = jax.nn.sigmoid(gate_pre)
    gate_act = gate_pre * sigmoid_gate
    hidden = (gate_act * up_pre).astype(jnp.bfloat16)
    result = (middle + jnp.dot(hidden, down_w, preferred_element_type=jnp.float32)).astype(
        jnp.bfloat16
    )
    regathered = (
        lax.all_gather(flat_weights[0], ("dp", "fsdp"), axis=0, tiled=True),
        lax.all_gather(flat_weights[1], ("dp", "fsdp"), axis=0, tiled=True),
        lax.all_gather(flat_weights[2], ("dp", "fsdp"), axis=0, tiled=True),
        lax.all_gather(flat_weights[3], ("dp", "fsdp"), axis=0, tiled=True),
        lax.all_gather(flat_weights[4], ("dp", "fsdp"), axis=0, tiled=True),
        lax.all_gather(flat_weights[5], ("dp", "fsdp"), axis=0, tiled=True),
        lax.all_gather(flat_weights[6], ("dp", "fsdp"), axis=0, tiled=True),
        lax.all_gather(flat_weights[7], ("dp", "fsdp"), axis=0, tiled=True),
        lax.all_gather(flat_weights[8], ("dp", "fsdp"), axis=0, tiled=True),
    )
    gain_one, query_w, key_w, value_w, out_w, gain_two, gate_w, up_w, down_w = unpack(
        regathered, model_width
    )
    grad_hidden = dot_back(incoming, down_w)
    grad_gate = (
        grad_hidden * up_pre * sigmoid_gate * (1.0 + gate_pre * (1.0 - sigmoid_gate))
    ).astype(jnp.bfloat16)
    grad_up = (grad_hidden * gate_act).astype(jnp.bfloat16)
    grad_normed_two = dot_back(grad_gate, gate_w) + dot_back(grad_up, up_w)
    grad_gain_two = jnp.sum(grad_normed_two * unit_two, axis=0)
    grad_middle = incoming.astype(jnp.float32) + norm_back(
        grad_normed_two, gain_two, unit_two, inverse_two
    )
    ff_entries = [
        ("gain", grad_gain_two),
        ("mat", normed_two, grad_gate),
        ("mat", normed_two, grad_up),
        ("mat", hidden, incoming),
    ]
    grad_branch = grad_middle.astype(jnp.bfloat16)
    grad_attended = dot_back(grad_branch, out_w).astype(jnp.bfloat16)
    grad_att_blk = grad_attended.reshape(block_count, WINDOW, head_count, HEAD)
    probs = jnp.exp(masked_scores(query_blk, key_blk, key_mask) - log_total)
    grad_probs = jnp.einsum(
        "bahd,bchd->bhac", grad_att_blk, value_blk, preferred_element_type=jnp.float32
    )
    grad_scores = (
        probs * (grad_probs - jnp.sum(grad_probs * probs, axis=-1, keepdims=True))
    ).astype(jnp.bfloat16)
    grad_query = jnp.einsum(
        "bhac,bchd->bahd", grad_scores, key_blk, preferred_element_type=jnp.float32
    ) * HEAD ** (-0.5)
    grad_query = grad_query.reshape(tok_rows, model_width).astype(jnp.bfloat16)
    key_parts = jnp.einsum(
        "bhac,bahd->bchd", grad_scores, query_blk, preferred_element_type=jnp.float32
    ) * HEAD ** (-0.5)
    grad_key = fold_keys(key_parts, tok_rows, model_width).astype(jnp.bfloat16)
    value_parts = jnp.einsum(
        "bhac,bahd->bchd", probs_low, grad_att_blk, preferred_element_type=jnp.float32
    )
    grad_value = fold_keys(value_parts, tok_rows, model_width).astype(jnp.bfloat16)
    grad_normed_one = (
        dot_back(grad_query, query_w) + dot_back(grad_key, key_w) + dot_back(grad_value, value_w)
    )
    grad_gain_one = jnp.sum(grad_normed_one * unit_one, axis=0)
    grad_dealt = (grad_middle + norm_back(grad_normed_one, gain_one, unit_one, inverse_one)).astype(
        jnp.bfloat16
    )
    returned_out, returned_grad = (
        lax.all_to_all(result, "dp", split_axis=0, concat_axis=0, tiled=True),
        lax.all_to_all(grad_dealt, "dp", split_axis=0, concat_axis=0, tiled=True),
    )
    layer_out = returned_out[send_slot]
    input_grad = returned_grad[send_slot]
    attn_entries = [
        ("gain", grad_gain_one),
        ("mat", normed_one, grad_query),
        ("mat", normed_one, grad_key),
        ("mat", normed_one, grad_value),
        ("mat", attended, grad_branch),
    ]
    every_entry = attn_entries + ff_entries
    all_summed = lax.psum_scatter(
        term_maker(every_entry, pieces, lax.axis_size(("dp", "fsdp")) * 1),
        ("dp", "fsdp"),
        scatter_dimension=0,
        tiled=True,
    )
    all_spans = split_spans(all_summed, every_entry, pieces)
    (
        span_gain_one,
        span_query,
        span_key,
        span_value,
        span_out,
        span_gain_two,
        span_gate,
        span_up,
        span_down,
    ) = all_spans
    return (
        layer_out,
        input_grad,
        span_gain_one,
        span_query,
        span_key,
        span_value,
        span_out,
        span_gain_two,
        span_gate,
        span_up,
        span_down,
    )


MESH = pl.DeviceIdType.MESH
TP = 4
CORES = 2
PAD = 96
VMEM_BYTES = 62 * 2**20

QKV, GATE, UP, OUT, DOWN = range(5)
F32 = jnp.float32
BF16 = jnp.bfloat16


def remote(src, dst, send, recv, device):
    return pltpu.make_async_remote_copy(
        src_ref=src, dst_ref=dst, send_sem=send, recv_sem=recv, device_id=device, device_id_type=MESH
    )


def nn(a, b):
    return lax.dot_general(a, b, (((1,), (0,)), ((), ())), preferred_element_type=F32)


def nt(a, b):
    return lax.dot_general(a, b, (((1,), (1,)), ((), ())), preferred_element_type=F32)


def tn(a, b):
    return lax.dot_general(a, b, (((0,), (0,)), ((), ())), preferred_element_type=F32)


def row_of(tile):
    return jnp.concatenate([tile[k : k + 1] for k in range(tile.shape[0])], axis=1)


def tile_of(row):
    return jnp.concatenate(
        [row[:, k * 128 : (k + 1) * 128] for k in range(row.shape[1] // 128)], axis=0
    )


def block_kernel(
    sizes,
    tok,
    cot,
    deal,
    lens,
    gains,
    scol,
    sout,
    sdown,
    lout,
    igrad,
    ocol,
    oout,
    odown,
    ogain,
    b,
    s,
):
    nd, zn, rows, width, hw, fw = sizes
    heads = hw // HEAD
    toks = TP * rows
    per = rows // nd
    dp = lax.axis_index("dp")
    f = lax.axis_index("fsdp")
    other = 1 - f
    z = dp // TP
    c = dp % TP
    sib = (dp, other)
    row_dev = width // (nd * CORES)

    barrier = pltpu.get_barrier_semaphore()
    pl.semaphore_signal(barrier, inc=1, device_id=sib, device_id_type=MESH)

    @pl.loop(1, nd)
    def _(k):
        pl.semaphore_signal(
            barrier, inc=1, device_id=(lax.rem(dp + k, nd), f), device_id_type=MESH
        )

    def all_peers(src, dst, send, recv, start=True):
        @pl.loop(1, nd)
        def _(k):
            to = lax.rem(dp + k, nd)
            remote(src(to), dst.at[dp], send.at[k], recv.at[k], (to, f)).start()

    def all_peers_recv(src, dst, send, recv):
        @pl.loop(1, nd)
        def _(k):
            at = lax.rem(dp + (nd - k), nd)
            remote(src(at), dst.at[at], send.at[k], recv.at[k], (at, f)).wait_recv()

    def all_peers_sent(src, dst, send, recv):
        @pl.loop(1, nd)
        def _(k):
            to = lax.rem(dp + k, nd)
            remote(src(to), dst.at[dp], send.at[k], recv.at[k], (to, f)).wait_send()

    def plane(k):
        cc = lax.rem(c + k, TP)
        return cc, (z * TP + cc, f)

    def gather_start(buf, send, recv):
        for k in range(1, TP):
            _, dev = plane(k)
            remote(buf.at[c], buf.at[c], send.at[k], recv.at[k], dev).start()

    def gather_recv(buf, send, recv):
        for k in range(1, TP):
            cc, dev = plane(TP - k)
            remote(buf.at[c], buf.at[cc], send.at[k], recv.at[k], dev).wait_recv()

    def gather_sent(buf, send, recv):
        for k in range(1, TP):
            _, dev = plane(k)
            remote(buf.at[c], buf.at[c], send.at[k], recv.at[k], dev).wait_send()

    tiles = 4
    tw = width // tiles

    def part(buf, at, j):
        return buf.at[at, :, pl.ds(pl.multiple_of(j * tw, tw), tw)]

    def scatter_tile(src, dst, send, recv, j):
        for k in range(1, TP):
            cc, dev = plane(k)
            remote(part(src, cc, j), part(dst, c, j), send.at[j, k], recv.at[j, k], dev).start()

    def scatter_recv(src, dst, send, recv):
        @pl.loop(0, tiles)
        def _(j):
            for k in range(1, TP):
                cc, dev = plane(TP - k)
                remote(
                    part(src, cc, j), part(dst, cc, j), send.at[j, k], recv.at[j, k], dev
                ).wait_recv()

    def scatter_sent(src, dst, send, recv):
        @pl.loop(0, tiles)
        def _(j):
            for k in range(1, TP):
                cc, dev = plane(k)
                remote(
                    part(src, cc, j), part(dst, c, j), send.at[j, k], recv.at[j, k], dev
                ).wait_send()

    def scatter_sum(src, dst):
        total = src[c].astype(F32)
        for k in range(1, TP):
            total = total + dst[lax.rem(c + k, TP)].astype(F32)
        return total

    def block(piece, at, core):
        if piece == OUT:
            return b.wout.at[at, core]
        if piece == DOWN:
            return b.wdown.at[at, core]
        return b.wcol.at[piece, at, :, core]

    def hop(piece, at, slot, to):
        return remote(
            block(piece, at, f),
            block(piece, at, f),
            s.z_s.at[piece, slot],
            s.z_r.at[piece, at],
            (to * TP + c, f),
        )

    def mirror(piece, at, core):
        return remote(
            block(piece, at, core),
            block(piece, at, core),
            s.b_s.at[piece, at],
            s.b_r.at[piece, at],
            sib,
        )

    def line_start(piece):
        @pl.when(z < zn - 1)
        def _():
            hop(piece, z, 0, z + 1).start()

        @pl.when(z > 0)
        def _():
            hop(piece, z, 1, z - 1).start()

        mirror(piece, z, f).start()

    def line_step(piece, d):
        @pl.when(z >= d)
        def _():
            hop(piece, z - d, 0, z).wait_recv()

            @pl.when(z < zn - 1)
            def _():
                hop(piece, z - d, 2 * d, z + 1).start()

            mirror(piece, z - d, f).start()

        @pl.when(z + d < zn)
        def _():
            hop(piece, z + d, 0, z).wait_recv()

            @pl.when(z > 0)
            def _():
                hop(piece, z + d, 2 * d + 1, z - 1).start()

            mirror(piece, z + d, f).start()

    def line_done(piece):
        for at in range(zn):
            mirror(piece, at, other).wait_recv()

    def line_sent(piece):
        for d in range(zn):

            @pl.when((z >= d) & (z < zn - 1))
            def _():
                hop(piece, z - d, 2 * d, z + 1).wait_send()

            @pl.when((z + d < zn) & (z > 0))
            def _():
                hop(piece, z + d, 2 * d + 1, z - 1).wait_send()

        for at in range(zn):
            mirror(piece, at, f).wait_send()

    def spread(piece, k):
        cc, dev = plane(k)
        return remote(
            scol.at[piece, cc],
            b.wcol.at[piece, z, c, f],
            s.s1_s.at[piece, k],
            s.s1_r.at[piece, k],
            dev,
        )

    def spread_recv(piece):
        for k in range(1, TP):
            cc, dev = plane(TP - k)
            remote(
                scol.at[piece, cc],
                b.wcol.at[piece, z, cc, f],
                s.s1_s.at[piece, k],
                s.s1_r.at[piece, k],
                dev,
            ).wait_recv()

    slot = ((deal[...] >> _log2(rows * CORES)) * per) + (deal[...] & (per - 1))
    pick = (lax.broadcasted_iota(jnp.int32, (rows, rows), 0) == slot).astype(BF16)
    b.pick[...] = pick
    b.tsend[...] = nn(pick, tok[...]).reshape(nd, per, width).astype(BF16)
    b.csend[...] = nn(pick, cot[...]).reshape(nd, per, width).astype(BF16)

    pl.semaphore_wait(barrier, nd)

    all_peers(lambda to: gains, b.grecv, s.g_s, s.g_r)
    all_peers(lambda to: b.tsend.at[to], b.trecv, s.t_s, s.t_r)
    for k in range(1, TP):
        spread(QKV, k).start()
    for piece in (QKV, GATE, UP):
        b.wcol[piece, z, c, f] = scol[piece, c]
    b.wout[z, f] = sout[...]
    b.wdown[z, f] = sdown[...]
    b.trecv[dp] = b.tsend[dp]
    b.crecv[dp] = b.csend[dp]
    b.grecv[dp] = gains[...]
    ri = lax.broadcasted_iota(jnp.int32, (rows, rows), 0)
    ci = lax.broadcasted_iota(jnp.int32, (rows, rows), 1)
    seg_r = jnp.zeros((rows, rows), jnp.int32)
    seg_c = jnp.zeros((rows, rows), jnp.int32)
    bound = jnp.int32(0)
    for k in range(lens.shape[1]):
        bound = bound + lens[0, k]
        seg_r = seg_r + (ri >= bound).astype(jnp.int32)
        seg_c = seg_c + (ci >= bound).astype(jnp.int32)
    allowed = (seg_r == seg_c) & (ri >= ci) & (ri - ci < WINDOW)
    b.mask[c] = allowed.astype(F32).astype(BF16)
    gather_start(b.mask, s.m_s, s.m_r)
    for piece in (GATE, UP):
        for k in range(1, TP):
            spread(piece, k).start()

    all_peers_recv(lambda at: gains, b.grecv, s.g_s, s.g_r)
    gain_sum = jnp.sum(b.grecv[...].astype(F32), axis=0)
    b.gpart[f] = gain_sum.astype(BF16)
    gmirror = remote(b.gpart.at[f], b.gpart.at[f], s.gb_s, s.gb_r, sib)
    gmirror.start()

    spread_recv(QKV)
    line_start(QKV)

    all_peers_recv(lambda at: b.tsend.at[at], b.trecv, s.t_s, s.t_r)
    all_peers(lambda to: b.csend.at[to], b.crecv, s.c_s, s.c_r)
    remote(b.gpart.at[other], b.gpart.at[other], s.gb_s, s.gb_r, sib).wait_recv()
    gain_tile = b.gpart[0].astype(F32) + b.gpart[1].astype(F32)
    gw = width // 128
    b.gain[0:1] = row_of(gain_tile[0:gw])
    b.gain[1:2] = row_of(gain_tile[gw : 2 * gw])

    x = b.trecv[...].astype(F32).reshape(rows, width)
    unit = x * lax.rsqrt(jnp.mean(x * x, axis=1, keepdims=True) + EPSILON)
    b.n1[c] = (unit * b.gain[0:1]).astype(BF16)
    gather_start(b.n1, s.a_s.at[0], s.a_r.at[0])

    line_step(QKV, 1)
    line_start(OUT)
    line_step(QKV, 2)
    line_step(QKV, 3)
    spread_recv(GATE)
    spread_recv(UP)
    line_start(GATE)
    line_step(OUT, 1)
    all_peers_recv(lambda at: b.csend.at[at], b.crecv, s.c_s, s.c_r)
    b.call[c] = b.crecv[...].reshape(rows, width)
    gather_recv(b.n1, s.a_s.at[0], s.a_r.at[0])
    gather_start(b.call, s.a_s.at[1], s.a_r.at[1])
    line_done(QKV)
    n1 = b.n1[...].reshape(toks, width)
    for j in range(3):
        w = b.wcol[QKV, :, :, :, :, j * hw : (j + 1) * hw].reshape(width, hw)
        b.qkv[:, j * hw : (j + 1) * hw] = nn(n1, w).astype(BF16)
    line_step(OUT, 2)
    line_step(GATE, 1)
    line_start(UP)
    gather_recv(b.mask, s.m_s, s.m_r)
    scale = HEAD ** (-0.5)

    @pl.loop(0, TP)
    def _(i):
        at = pl.ds(pl.multiple_of(i * rows, rows), rows)
        blk = b.qkv[at, :]
        allow = b.mask[i].astype(F32) > 0.5
        outs = []
        for h in range(heads):
            q = blk[:, h * HEAD : (h + 1) * HEAD]
            k = blk[:, hw + h * HEAD : hw + (h + 1) * HEAD]
            v = blk[:, 2 * hw + h * HEAD : 2 * hw + (h + 1) * HEAD]
            scores = jnp.where(allow, nt(q, k) * scale, -1e30)
            e = jnp.exp(scores - jnp.max(scores, axis=1, keepdims=True))
            p = e / jnp.sum(e, axis=1, keepdims=True)
            b.probs[i * heads + h] = p
            outs.append(nn(p.astype(BF16), v))
        b.att[at, :] = jnp.concatenate(outs, axis=1).astype(BF16)

    line_step(OUT, 3)
    line_step(GATE, 2)
    line_step(UP, 1)
    line_done(OUT)
    att = b.att[...]

    @pl.loop(0, tiles)
    def _(j):
        cols = pl.ds(pl.multiple_of(j * tw, tw), tw)
        w = b.wout[:, :, :, cols].reshape(hw, tw)
        b.p[0][:, :, cols] = nn(att, w).reshape(TP, rows, tw).astype(BF16)
        scatter_tile(b.p[0], b.q[0], s.r_s.at[0], s.r_r.at[0], j)

    line_step(GATE, 3)
    line_start(DOWN)
    line_step(UP, 2)
    scatter_recv(b.p[0], b.q[0], s.r_s.at[0], s.r_r.at[0])
    middle = b.trecv[...].astype(F32).reshape(rows, width) + scatter_sum(b.p[0], b.q[0])
    b.middle[...] = middle
    unit = middle * lax.rsqrt(jnp.mean(middle * middle, axis=1, keepdims=True) + EPSILON)
    b.n2[c] = (unit * b.gain[1:2]).astype(BF16)
    gather_start(b.n2, s.a_s.at[2], s.a_r.at[2])
    line_step(UP, 3)
    line_step(DOWN, 1)
    line_done(GATE)
    line_done(UP)
    gather_recv(b.n2, s.a_s.at[2], s.a_r.at[2])
    n2 = b.n2[...].reshape(toks, width)
    fb = 256
    for j in range(fw // fb):
        cols = slice(j * fb, (j + 1) * fb)
        gate = nn(n2, b.wcol[GATE, :, :, :, :, cols].reshape(width, fb))
        up = nn(n2, b.wcol[UP, :, :, :, :, cols].reshape(width, fb))
        b.gate[:, cols] = gate
        b.up[:, cols] = up
        b.hid[:, cols] = (gate * jax.nn.sigmoid(gate) * up).astype(BF16)
    line_step(DOWN, 2)

    gather_recv(b.call, s.a_s.at[1], s.a_r.at[1])
    call = b.call[...].reshape(toks, width)

    def presum(piece, src, dst):
        return remote(src, dst, s.p_s.at[piece], s.p_r.at[piece], sib)

    def row_send(piece, src, dst, start):
        for k in range(1, zn):
            zz = lax.rem(z + k, zn)
            cp = remote(
                src.at[zz], dst.at[z], s.w_s.at[piece, k], s.w_r.at[piece, k], (zz * TP + c, f)
            )
            cp.start() if start else cp.wait_send()

    def row_recv(piece, src, dst):
        for k in range(1, zn):
            zz = lax.rem(z + (zn - k), zn)
            remote(
                src.at[zz], dst.at[zz], s.w_s.at[piece, k], s.w_r.at[piece, k], (zz * TP + c, f)
            ).wait_recv()

    for j in range(fw // (4 * PAD)):
        w = tn(b.hid[:, j * 4 * PAD : (j + 1) * 4 * PAD], call)
        b.gdown[2 * j : 2 * j + 2] = w.reshape(2, CORES, PAD, width).astype(BF16)
    presum(DOWN, b.gdown.at[:, other], b.cdown).start()
    line_step(DOWN, 3)
    line_done(DOWN)
    for j in range(fw // (4 * PAD)):
        cols = slice(j * 4 * PAD, (j + 1) * 4 * PAD)
        gh = nt(call, b.wdown[2 * j : 2 * j + 2].reshape(4 * PAD, width))
        gate = b.gate[:, cols]
        sg = jax.nn.sigmoid(gate)
        b.ggate[:, cols] = (gh * b.up[:, cols] * sg * (1.0 + gate * (1.0 - sg))).astype(BF16)
        b.gup[:, cols] = (gh * gate * sg).astype(BF16)

    presum(DOWN, b.gdown.at[:, f], b.cdown).wait_recv()
    for at in range(zn):
        b.sdown[at] = (b.gdown[at, f].astype(F32) + b.cdown[at].astype(F32)).astype(BF16)
    row_send(DOWN, b.sdown, b.rdown, True)
    b.rdown[z] = b.sdown[z]

    @pl.loop(0, tiles)
    def _(j):
        cols = pl.ds(pl.multiple_of(j * tw, tw), tw)
        v = nt(b.ggate[...], b.wcol[GATE, j].reshape(tw, fw))
        v = v + nt(b.gup[...], b.wcol[UP, j].reshape(tw, fw))
        b.p[1][:, :, cols] = v.reshape(TP, rows, tw).astype(BF16)
        scatter_tile(b.p[1], b.q[1], s.r_s.at[1], s.r_r.at[1], j)

    def col_grad(piece, act, grad):
        @pl.loop(0, zn)
        def _(j):
            a = act[:, :, pl.ds(pl.multiple_of(j * tw, tw), tw)].reshape(toks, tw)
            g = tn(a, grad[...])
            b.gcol[piece, j] = g.reshape(TP, CORES, row_dev, fw).astype(BF16)

        presum(piece, b.gcol.at[piece, :, :, other], b.ccol.at[piece]).start()

    def col_send(piece):
        presum(piece, b.gcol.at[piece, :, :, f], b.ccol.at[piece]).wait_recv()

        @pl.loop(0, zn)
        def _(j):
            v = b.gcol[piece, j, :, f].astype(F32) + b.ccol[piece, j].astype(F32)
            b.scol[piece, j] = v.astype(BF16)

        @pl.loop(1, nd)
        def _(k):
            to = lax.rem(dp + k, nd)
            remote(
                b.scol.at[piece, to // TP, to % TP],
                b.rcol.at[piece, z, c],
                s.w_s.at[piece, k],
                s.w_r.at[piece, k],
                (to, f),
            ).start()

        b.rcol[piece, z, c] = b.scol[piece, z, c]

    def col_recv(piece):
        @pl.loop(1, nd)
        def _(k):
            at = lax.rem(dp + (nd - k), nd)
            remote(
                b.scol.at[piece, z, c],
                b.rcol.at[piece, at // TP, at % TP],
                s.w_s.at[piece, k],
                s.w_r.at[piece, k],
                (at, f),
            ).wait_recv()

        total = b.rcol[piece, 0].astype(F32)
        for k in range(1, zn):
            total = total + b.rcol[piece, k].astype(F32)
        ocol[piece] = total

    def col_sent(piece):
        @pl.loop(1, nd)
        def _(k):
            to = lax.rem(dp + k, nd)
            remote(
                b.scol.at[piece, to // TP, to % TP],
                b.rcol.at[piece, z, c],
                s.w_s.at[piece, k],
                s.w_r.at[piece, k],
                (to, f),
            ).wait_send()

    col_grad(GATE, b.n2, b.ggate)
    col_grad(UP, b.n2, b.gup)
    col_send(GATE)

    scatter_recv(b.p[1], b.q[1], s.r_s.at[1], s.r_r.at[1])
    gn = scatter_sum(b.p[1], b.q[1])
    middle = b.middle[...]
    inv = lax.rsqrt(jnp.mean(middle * middle, axis=1, keepdims=True) + EPSILON)
    unit = middle * inv
    b.ggain[1:2] = jnp.sum(gn * unit, axis=0, keepdims=True)
    a = gn * b.gain[1:2]
    gm = b.call[c].astype(F32) + inv * (a - unit * jnp.mean(a * unit, axis=1, keepdims=True))
    b.gmid[...] = gm
    b.gb[c] = gm.astype(BF16)
    gather_start(b.gb, s.a_s.at[3], s.a_r.at[3])
    col_send(UP)

    hid = b.hid[...]

    @pl.loop(0, tiles)
    def _(j):
        cols = pl.ds(pl.multiple_of(j * tw, tw), tw)
        w = b.wdown[:, :, :, cols].reshape(fw, tw)
        b.p[2][:, :, cols] = nn(hid, w).reshape(TP, rows, tw).astype(BF16)
        scatter_tile(b.p[2], b.q[2], s.r_s.at[2], s.r_r.at[2], j)

    gather_recv(b.gb, s.a_s.at[3], s.a_r.at[3])
    gb = b.gb[...].reshape(toks, width)
    b.ga[...] = nt(gb, b.wout[...].reshape(hw, width)).astype(BF16)
    b.gout[...] = tn(b.att[...], gb).reshape(zn, CORES, row_dev, width).astype(BF16)
    presum(OUT, b.gout.at[:, other], b.cout).start()

    @pl.loop(0, TP)
    def _(i):
        at = pl.ds(pl.multiple_of(i * rows, rows), rows)
        blk = b.qkv[at, :]
        gab = b.ga[at, :]
        gq, gk, gv = [], [], []
        for h in range(heads):
            q = blk[:, h * HEAD : (h + 1) * HEAD]
            k = blk[:, hw + h * HEAD : hw + (h + 1) * HEAD]
            v = blk[:, 2 * hw + h * HEAD : 2 * hw + (h + 1) * HEAD]
            ga = gab[:, h * HEAD : (h + 1) * HEAD]
            p = b.probs[i * heads + h]
            gp = nt(ga, v)
            gs = (p * (gp - jnp.sum(p * gp, axis=1, keepdims=True))).astype(BF16)
            gq.append(nn(gs, k) * scale)
            gk.append(tn(gs, q) * scale)
            gv.append(tn(p.astype(BF16), ga))
        b.gqkv[at, :] = jnp.concatenate(gq + gk + gv, axis=1).astype(BF16)

    presum(OUT, b.gout.at[:, f], b.cout).wait_recv()
    for at in range(zn):
        b.sout[at] = (b.gout[at, f].astype(F32) + b.cout[at].astype(F32)).astype(BF16)
    row_send(OUT, b.sout, b.rout, True)
    b.rout[z] = b.sout[z]

    @pl.loop(0, tiles)
    def _(j):
        cols = pl.ds(pl.multiple_of(j * tw, tw), tw)
        v = nt(b.gqkv[...], b.wcol[QKV, j].reshape(tw, fw))
        b.p[3][:, :, cols] = v.reshape(TP, rows, tw).astype(BF16)
        scatter_tile(b.p[3], b.q[3], s.r_s.at[3], s.r_r.at[3], j)

    col_grad(QKV, b.n1, b.gqkv)

    scatter_recv(b.p[2], b.q[2], s.r_s.at[2], s.r_r.at[2])
    res = b.middle[...] + scatter_sum(b.p[2], b.q[2])
    b.lsend[...] = res.reshape(nd, per, width).astype(BF16)
    col_send(QKV)
    all_peers(lambda to: b.lsend.at[to], b.lrecv, s.l_s, s.l_r)
    b.lrecv[dp] = b.lsend[dp]

    scatter_recv(b.p[3], b.q[3], s.r_s.at[3], s.r_r.at[3])
    gn = scatter_sum(b.p[3], b.q[3])
    x = b.trecv[...].astype(F32).reshape(rows, width)
    inv = lax.rsqrt(jnp.mean(x * x, axis=1, keepdims=True) + EPSILON)
    unit = x * inv
    b.ggain[0:1] = jnp.sum(gn * unit, axis=0, keepdims=True)
    a = gn * b.gain[0:1]
    gx = b.gmid[...] + inv * (a - unit * jnp.mean(a * unit, axis=1, keepdims=True))
    b.isend[...] = gx.reshape(nd, per, width).astype(BF16)
    all_peers(lambda to: b.isend.at[to], b.irecv, s.i_s, s.i_r)
    b.irecv[dp] = b.isend[dp]
    b.hsend[...] = jnp.concatenate([tile_of(b.ggain[0:1]), tile_of(b.ggain[1:2])], axis=0)
    all_peers(lambda to: b.hsend, b.hrecv, s.h_s, s.h_r)
    b.hrecv[dp] = b.hsend[...]

    all_peers_recv(lambda at: b.lsend.at[at], b.lrecv, s.l_s, s.l_r)
    pick = b.pick[...]
    lout[...] = tn(pick, b.lrecv[...].reshape(rows, width)).astype(BF16)
    row_recv(DOWN, b.sdown, b.rdown)
    odown[...] = jnp.sum(b.rdown[...].astype(F32), axis=0)
    col_recv(GATE)
    col_recv(UP)
    row_recv(OUT, b.sout, b.rout)
    oout[...] = jnp.sum(b.rout[...].astype(F32), axis=0)
    all_peers_recv(lambda at: b.hsend, b.hrecv, s.h_s, s.h_r)
    b.hpart[f] = jnp.sum(b.hrecv[...], axis=0)
    hmirror = remote(b.hpart.at[f], b.hpart.at[f], s.hb_s, s.hb_r, sib)
    hmirror.start()
    all_peers_recv(lambda at: b.isend.at[at], b.irecv, s.i_s, s.i_r)
    igrad[...] = tn(pick, b.irecv[...].reshape(rows, width)).astype(BF16)
    remote(b.hpart.at[other], b.hpart.at[other], s.hb_s, s.hb_r, sib).wait_recv()
    ogain[...] = b.hpart[0] + b.hpart[1]
    col_recv(QKV)

    gmirror.wait_send()
    hmirror.wait_send()
    all_peers_sent(lambda to: gains, b.grecv, s.g_s, s.g_r)
    all_peers_sent(lambda to: b.tsend.at[to], b.trecv, s.t_s, s.t_r)
    all_peers_sent(lambda to: b.csend.at[to], b.crecv, s.c_s, s.c_r)
    all_peers_sent(lambda to: b.lsend.at[to], b.lrecv, s.l_s, s.l_r)
    all_peers_sent(lambda to: b.isend.at[to], b.irecv, s.i_s, s.i_r)
    all_peers_sent(lambda to: b.hsend, b.hrecv, s.h_s, s.h_r)
    gather_sent(b.mask, s.m_s, s.m_r)
    for i, buf in enumerate((b.n1, b.call, b.n2, b.gb)):
        gather_sent(buf, s.a_s.at[i], s.a_r.at[i])
    for i in range(4):
        scatter_sent(b.p[i], b.q[i], s.r_s.at[i], s.r_r.at[i])
    for piece in (QKV, GATE, UP):
        for k in range(1, TP):
            spread(piece, k).wait_send()
        presum(piece, b.gcol.at[piece, :, :, other], b.ccol.at[piece]).wait_send()
        col_sent(piece)
    presum(OUT, b.gout.at[:, other], b.cout).wait_send()
    presum(DOWN, b.gdown.at[:, other], b.cdown).wait_send()
    row_send(OUT, b.sout, b.rout, False)
    row_send(DOWN, b.sdown, b.rdown, False)
    for piece in (QKV, GATE, UP, OUT, DOWN):
        line_sent(piece)


def _log2(n):
    return n.bit_length() - 1


def kernel_takes(dp_count, core_count, rows, width, hidden):
    pieces = dp_count * core_count
    zn = dp_count // TP
    return (
        core_count == CORES
        and dp_count % TP == 0
        and rows == 128
        and rows % dp_count == 0
        and rows // dp_count == 8
        and width == zn * 256
        and width // HEAD == dp_count
        and width // pieces == HEAD // CORES
        and hidden % pieces == 0
        and hidden // pieces <= PAD
        and PAD * CORES * zn % 256 == 0
        and zn == 4
    )


def planned(
    dp_count,
    tokens,
    dealing,
    lengths,
    norm1_gain,
    w_query,
    w_key,
    w_value,
    w_out,
    norm2_gain,
    w_gate,
    w_up,
    w_down,
    cotangent,
):
    nd = dp_count
    zn = nd // TP
    rows, width = tokens.shape
    pieces = nd * CORES
    row_dev = width // pieces
    hidden = w_gate.shape[0] * pieces // width
    unit = hidden // pieces
    hw = width // TP
    fw = PAD * CORES * zn
    me = lax.axis_index(("dp", "fsdp"))

    def head_cols(w):
        w = w.reshape(row_dev, zn, TP, HEAD)
        return w.transpose(2, 0, 1, 3).reshape(TP, row_dev, hw)

    def hidden_cols(w):
        w = w.reshape(row_dev, zn, TP, CORES, unit)
        w = jnp.pad(w, ((0, 0), (0, 0), (0, 0), (0, 0), (0, PAD - unit)))
        return w.transpose(2, 0, 1, 3, 4).reshape(TP, row_dev, fw)

    scol = jnp.stack(
        [
            jnp.concatenate([head_cols(w_query), head_cols(w_key), head_cols(w_value)], axis=2),
            hidden_cols(w_gate),
            hidden_cols(w_up),
        ]
    )
    sout = w_out.reshape(row_dev, width)
    sdown = jnp.pad(w_down.reshape(unit, width), ((0, PAD - unit), (0, 0)))
    gw = width // 128
    lanes = jnp.arange(128)[None, :]
    tile_rows = jnp.arange(gw)[:, None]
    mine = (tile_rows == me * row_dev // 128) & (lanes // row_dev == me % (128 // row_dev))

    def gain_tile(gain):
        return jnp.where(mine, jnp.tile(gain, 128 // row_dev)[None, :], 0).astype(BF16)

    gains = jnp.concatenate([gain_tile(norm1_gain), gain_tile(norm2_gain)], axis=0)

    toks = TP * rows
    per = rows // nd
    V = pltpu.VMEM
    bufs = dict(
        pick=V((rows, rows), BF16),
        tsend=V((nd, per, width), BF16),
        trecv=V((nd, per, width), BF16),
        csend=V((nd, per, width), BF16),
        crecv=V((nd, per, width), BF16),
        lsend=V((nd, per, width), BF16),
        lrecv=V((nd, per, width), BF16),
        isend=V((nd, per, width), BF16),
        irecv=V((nd, per, width), BF16),
        grecv=V((nd, 2 * gw, 128), BF16),
        gpart=V((CORES, 2 * gw, 128), BF16),
        gain=V((8, width), F32),
        ggain=V((8, width), F32),
        hsend=V((2 * gw, 128), F32),
        hrecv=V((nd, 2 * gw, 128), F32),
        hpart=V((CORES, 2 * gw, 128), F32),
        mask=V((TP, rows, rows), BF16),
        wcol=V((3, zn, TP, CORES, row_dev, fw), BF16),
        wout=V((zn, CORES, row_dev, width), BF16),
        wdown=V((zn, CORES, PAD, width), BF16),
        n1=V((TP, rows, width), BF16),
        n2=V((TP, rows, width), BF16),
        call=V((TP, rows, width), BF16),
        gb=V((TP, rows, width), BF16),
        qkv=V((toks, 3 * hw), BF16),
        probs=V((TP * hw // HEAD, rows, rows), F32),
        att=V((toks, hw), BF16),
        middle=V((rows, width), F32),
        gmid=V((rows, width), F32),
        gate=V((toks, fw), F32),
        up=V((toks, fw), F32),
        hid=V((toks, fw), BF16),
        ggate=V((toks, fw), BF16),
        gup=V((toks, fw), BF16),
        ga=V((toks, hw), BF16),
        gqkv=V((toks, 3 * hw), BF16),
        gcol=V((3, zn, TP, CORES, row_dev, fw), BF16),
        ccol=V((3, zn, TP, row_dev, fw), BF16),
        scol=V((3, zn, TP, row_dev, fw), BF16),
        rcol=V((3, zn, TP, row_dev, fw), BF16),
        gout=V((zn, CORES, row_dev, width), BF16),
        cout=V((zn, row_dev, width), BF16),
        sout=V((zn, row_dev, width), BF16),
        rout=V((zn, row_dev, width), BF16),
        gdown=V((zn, CORES, PAD, width), BF16),
        cdown=V((zn, PAD, width), BF16),
        sdown=V((zn, PAD, width), BF16),
        rdown=V((zn, PAD, width), BF16),
    )
    bufs.update(
        p=[V((TP, rows, width), BF16) for _ in range(4)],
        q=[V((TP, rows, width), BF16) for _ in range(4)],
    )
    S = pltpu.SemaphoreType.DMA
    each = S((nd,))
    sems = dict(
        g_s=each,
        g_r=each,
        t_s=each,
        t_r=each,
        c_s=each,
        c_r=each,
        l_s=each,
        l_r=each,
        i_s=each,
        i_r=each,
        h_s=each,
        h_r=each,
        gb_s=S(()),
        gb_r=S(()),
        hb_s=S(()),
        hb_r=S(()),
        m_s=S((TP,)),
        m_r=S((TP,)),
        s1_s=S((3, TP)),
        s1_r=S((3, TP)),
        z_s=S((5, 2 * zn)),
        z_r=S((5, zn)),
        b_s=S((5, zn)),
        b_r=S((5, zn)),
        a_s=S((4, TP)),
        a_r=S((4, TP)),
        r_s=S((4, 4, TP)),
        r_r=S((4, 4, TP)),
        p_s=S((5,)),
        p_r=S((5,)),
        w_s=S((5, nd)),
        w_r=S((5, nd)),
    )
    n_io = 8 + 6
    spaces, shape_of = jax.tree.flatten((bufs, sems))

    def entry(*refs):
        io, rest = refs[:n_io], refs[n_io:]
        b, s = jax.tree.unflatten(shape_of, rest)
        block_kernel((nd, zn, rows, width, hw, fw), *io, SimpleNamespace(**b), SimpleNamespace(**s))

    vm = pl.BlockSpec(memory_space=pltpu.VMEM)
    sm = pl.BlockSpec(memory_space=pltpu.SMEM)
    lout, igrad, ocol, oout, odown, ogain = pl.pallas_call(
        entry,
        out_shape=(
            jax.ShapeDtypeStruct((rows, width), BF16),
            jax.ShapeDtypeStruct((rows, width), BF16),
            jax.ShapeDtypeStruct((3, TP, row_dev, fw), F32),
            jax.ShapeDtypeStruct((row_dev, width), F32),
            jax.ShapeDtypeStruct((PAD, width), F32),
            jax.ShapeDtypeStruct((2 * gw, 128), F32),
        ),
        in_specs=[vm, vm, vm, sm, vm, vm, vm, vm],
        out_specs=(vm,) * 6,
        scratch_shapes=spaces,
        compiler_params=pltpu.CompilerParams(
            collective_id=0, has_side_effects=True, vmem_limit_bytes=VMEM_BYTES
        ),
        name="block_fwd_bwd",
    )(tokens, cotangent, dealing.reshape(1, rows), lengths, gains, scol, sout, sdown)

    def head_rows(g):
        g = g.reshape(TP, row_dev, zn, HEAD)
        return g.transpose(1, 2, 0, 3).reshape(-1)

    def hidden_rows(g):
        g = g.reshape(TP, row_dev, zn, CORES, PAD)[..., :unit]
        return g.transpose(1, 2, 0, 3, 4).reshape(-1)

    def my_gain(tile):
        return lax.dynamic_slice(tile.reshape(-1), (me * row_dev,), (row_dev,))

    return (
        lout,
        igrad,
        my_gain(ogain[:gw]),
        head_rows(ocol[0, :, :, :hw]),
        head_rows(ocol[0, :, :, hw : 2 * hw]),
        head_rows(ocol[0, :, :, 2 * hw :]),
        oout.reshape(-1),
        my_gain(ogain[gw:]),
        hidden_rows(ocol[1]),
        hidden_rows(ocol[2]),
        odown[:unit].reshape(-1),
    )


def dispatch(dp_count, core_count, *args):
    tokens, w_gate = args[0], args[9]
    rows, width = tokens.shape
    hidden = w_gate.shape[0] * dp_count * core_count // width
    if kernel_takes(dp_count, core_count, rows, width, hidden):
        return planned(dp_count, *args)
    return body(*args)


def solution(mesh):
    in_specs = (
        P(("dp", "fsdp"), None),
        P(("dp", "fsdp")),
        P(("dp", "fsdp"), None),
        P(("dp", "fsdp")),
        P(("dp", "fsdp")),
        P(("dp", "fsdp")),
        P(("dp", "fsdp")),
        P(("dp", "fsdp")),
        P(("dp", "fsdp")),
        P(("dp", "fsdp")),
        P(("dp", "fsdp")),
        P(("dp", "fsdp")),
        P(("dp", "fsdp"), None),
    )
    out_specs = (
        P(("dp", "fsdp"), None),
        P(("dp", "fsdp"), None),
        P(("dp", "fsdp")),
        P(("dp", "fsdp")),
        P(("dp", "fsdp")),
        P(("dp", "fsdp")),
        P(("dp", "fsdp")),
        P(("dp", "fsdp")),
        P(("dp", "fsdp")),
        P(("dp", "fsdp")),
        P(("dp", "fsdp")),
    )
    return jax.shard_map(
        functools.partial(dispatch, mesh.shape["dp"], mesh.shape["fsdp"]),
         mesh=mesh, in_specs=in_specs, out_specs=out_specs, check_vma=False)
```

```python
import functools
from types import SimpleNamespace

import jax
import jax.numpy as jnp
from jax import lax
from jax.experimental import pallas as pl
from jax.experimental.pallas import tpu as pltpu
from jax.sharding import PartitionSpec as P

HEAD = 64
WINDOW = 64


EPSILON = 1e-06


def unpack(flat_list, model_width):
    gain_one, query_w, key_w, value_w, out_w, gain_two, gate_w, up_w, down_w = flat_list
    hidden_units = gate_w.shape[0] // model_width
    return (
        gain_one.astype(jnp.float32),
        query_w.reshape(model_width, model_width),
        key_w.reshape(model_width, model_width),
        value_w.reshape(model_width, model_width),
        out_w.reshape(model_width, model_width),
        gain_two.astype(jnp.float32),
        gate_w.reshape(model_width, hidden_units),
        up_w.reshape(model_width, hidden_units),
        down_w.reshape(hidden_units, model_width),
    )


def normalize(values, gain_vec):
    inverse = lax.rsqrt(jnp.mean(values * values, axis=-1, keepdims=True) + EPSILON)
    unit_rows = values * inverse
    return (unit_rows * gain_vec, unit_rows, inverse)


def norm_back(upstream, gain_vec, unit_rows, inverse):
    scaled = upstream * gain_vec
    return inverse * (scaled - unit_rows * jnp.mean(scaled * unit_rows, axis=-1, keepdims=True))


def dot_rows(first_op, second_op):
    return lax.dot_general(
        first_op, second_op, (((0,), (0,)), ((), ())), preferred_element_type=jnp.float32
    )


def dot_back(first_op, second_op):
    return lax.dot_general(
        first_op, second_op, (((1,), (1,)), ((), ())), preferred_element_type=jnp.float32
    )


def flat_piece(entry, count, pieces):
    if entry[0] == "gain":
        vector = entry[1]
        share = vector.shape[0] // pieces
        return vector.reshape(count, share)
    left_op, right_op = (entry[1], entry[2])
    row_total = left_op.shape[1]
    col_total = right_op.shape[1]
    share = row_total * col_total // pieces
    block = dot_rows(left_op, right_op)
    flat = block.reshape(-1)
    return flat.reshape(count, share)


def term_maker(entries, pieces, count):
    return jnp.concatenate([flat_piece(entry, count, pieces) for entry in entries], axis=1)


def split_spans(summed, entries, pieces):
    flat = summed.reshape(-1)
    results = []
    offset = 0
    for entry in entries:
        if entry[0] == "gain":
            share = entry[1].shape[0] // pieces
        else:
            share = entry[1].shape[1] * entry[2].shape[1] // pieces
        results.append(flat[offset : offset + share])
        offset = offset + share
    return results


def block_mask(segment, tok_rows):
    block_count = tok_rows // WINDOW
    padded = jnp.concatenate([jnp.full((WINDOW,), -1, jnp.int32), segment])
    seg_query = segment.reshape(block_count, WINDOW)
    seg_keys = jnp.concatenate([padded[:-WINDOW].reshape(block_count, WINDOW), seg_query], axis=1)
    offset = jnp.arange(WINDOW)[:, None] - jnp.arange(2 * WINDOW)[None, :] + WINDOW
    inside = (offset >= 0) & (offset < WINDOW)
    return inside[None] & (seg_query[:, :, None] == seg_keys[:, None, :])


def key_blocks(values, block_count):
    padded = jnp.concatenate([jnp.zeros((WINDOW,) + values.shape[1:], values.dtype), values])
    previous = padded[:-WINDOW].reshape((block_count, WINDOW) + values.shape[1:])
    current = values.reshape((block_count, WINDOW) + values.shape[1:])
    return jnp.concatenate([previous, current], axis=1)


def fold_keys(key_parts, tok_rows, model_width):
    previous = key_parts[:, :WINDOW]
    current = key_parts[:, WINDOW:]
    shifted = jnp.concatenate([previous[1:], jnp.zeros_like(previous[:1])], axis=0)
    return (current + shifted).reshape(tok_rows, model_width)


def masked_scores(query_blk, key_blk, key_mask):
    scores = jnp.einsum(
        "bahd,bchd->bhac", query_blk, key_blk, preferred_element_type=jnp.float32
    ) * HEAD ** (-0.5)
    return jnp.where(key_mask, scores, -1e30)


def body(
    tokens,
    dealing,
    lengths,
    norm1_gain,
    w_query,
    w_key,
    w_value,
    w_out,
    norm2_gain,
    w_gate,
    w_up,
    w_down,
    cotangent,
):
    tok_rows, model_width = tokens.shape
    dp_count = lax.axis_size("dp")
    fsdp_count = lax.axis_size("fsdp")
    pieces = lax.axis_size(("dp", "fsdp"))
    per_peer = tok_rows // dp_count
    local_pos = dealing % tok_rows
    target_dp = dealing // tok_rows // fsdp_count
    send_slot = target_dp * per_peer + local_pos % per_peer
    sent_tokens = jnp.zeros_like(tokens).at[send_slot].set(tokens)
    sent_cot = jnp.zeros_like(cotangent).at[send_slot].set(cotangent)
    inputs, incoming = (
        lax.all_to_all(sent_tokens, "dp", split_axis=0, concat_axis=0, tiled=True),
        lax.all_to_all(sent_cot, "dp", split_axis=0, concat_axis=0, tiled=True),
    )
    bounds = jnp.cumsum(lengths[0])
    positions = jnp.arange(tok_rows, dtype=jnp.int32)
    segment = jnp.sum((positions[:, None] >= bounds[None, :]).astype(jnp.int32), axis=1)
    block_count = tok_rows // WINDOW
    head_count = model_width // HEAD
    key_mask = block_mask(segment, tok_rows)[:, None]
    flat_weights = (norm1_gain, w_query, w_key, w_value, w_out, norm2_gain, w_gate, w_up, w_down)
    gathered = (
        lax.all_gather(flat_weights[0], ("dp", "fsdp"), axis=0, tiled=True),
        lax.all_gather(flat_weights[1], ("dp", "fsdp"), axis=0, tiled=True),
        lax.all_gather(flat_weights[2], ("dp", "fsdp"), axis=0, tiled=True),
        lax.all_gather(flat_weights[3], ("dp", "fsdp"), axis=0, tiled=True),
        lax.all_gather(flat_weights[4], ("dp", "fsdp"), axis=0, tiled=True),
        lax.all_gather(flat_weights[5], ("dp", "fsdp"), axis=0, tiled=True),
        lax.all_gather(flat_weights[6], ("dp", "fsdp"), axis=0, tiled=True),
        lax.all_gather(flat_weights[7], ("dp", "fsdp"), axis=0, tiled=True),
        lax.all_gather(flat_weights[8], ("dp", "fsdp"), axis=0, tiled=True),
    )
    gain_one, query_w, key_w, value_w, out_w, gain_two, gate_w, up_w, down_w = unpack(
        gathered, model_width
    )
    input_f = inputs.astype(jnp.float32)
    scaled_one, unit_one, inverse_one = normalize(input_f, gain_one)
    normed_one = scaled_one.astype(jnp.bfloat16)
    query_act = jnp.dot(normed_one, query_w, preferred_element_type=jnp.float32).astype(
        jnp.bfloat16
    )
    key_act = jnp.dot(normed_one, key_w, preferred_element_type=jnp.float32).astype(jnp.bfloat16)
    value_act = jnp.dot(normed_one, value_w, preferred_element_type=jnp.float32).astype(
        jnp.bfloat16
    )
    query_blk = query_act.reshape(block_count, WINDOW, head_count, HEAD)
    key_blk = key_blocks(key_act.reshape(tok_rows, head_count, HEAD), block_count)
    value_blk = key_blocks(value_act.reshape(tok_rows, head_count, HEAD), block_count)
    scores = masked_scores(query_blk, key_blk, key_mask)
    row_peak = jnp.max(scores, axis=-1, keepdims=True)
    exp_scores = jnp.exp(scores - row_peak)
    row_total = jnp.sum(exp_scores, axis=-1, keepdims=True)
    log_total = row_peak + jnp.log(row_total)
    probs_low = (exp_scores / row_total).astype(jnp.bfloat16)
    attended = jnp.einsum(
        "bhac,bchd->bahd", probs_low, value_blk, preferred_element_type=jnp.float32
    )
    attended = attended.reshape(tok_rows, model_width).astype(jnp.bfloat16)
    middle = input_f + jnp.dot(attended, out_w, preferred_element_type=jnp.float32)
    scaled_two, unit_two, inverse_two = normalize(middle, gain_two)
    normed_two = scaled_two.astype(jnp.bfloat16)
    gate_pre = jnp.dot(normed_two, gate_w, preferred_element_type=jnp.float32)
    up_pre = jnp.dot(normed_two, up_w, preferred_element_type=jnp.float32)
    sigmoid_gate = jax.nn.sigmoid(gate_pre)
    gate_act = gate_pre * sigmoid_gate
    hidden = (gate_act * up_pre).astype(jnp.bfloat16)
    result = (middle + jnp.dot(hidden, down_w, preferred_element_type=jnp.float32)).astype(
        jnp.bfloat16
    )
    regathered = (
        lax.all_gather(flat_weights[0], ("dp", "fsdp"), axis=0, tiled=True),
        lax.all_gather(flat_weights[1], ("dp", "fsdp"), axis=0, tiled=True),
        lax.all_gather(flat_weights[2], ("dp", "fsdp"), axis=0, tiled=True),
        lax.all_gather(flat_weights[3], ("dp", "fsdp"), axis=0, tiled=True),
        lax.all_gather(flat_weights[4], ("dp", "fsdp"), axis=0, tiled=True),
        lax.all_gather(flat_weights[5], ("dp", "fsdp"), axis=0, tiled=True),
        lax.all_gather(flat_weights[6], ("dp", "fsdp"), axis=0, tiled=True),
        lax.all_gather(flat_weights[7], ("dp", "fsdp"), axis=0, tiled=True),
        lax.all_gather(flat_weights[8], ("dp", "fsdp"), axis=0, tiled=True),
    )
    gain_one, query_w, key_w, value_w, out_w, gain_two, gate_w, up_w, down_w = unpack(
        regathered, model_width
    )
    grad_hidden = dot_back(incoming, down_w)
    grad_gate = (
        grad_hidden * up_pre * sigmoid_gate * (1.0 + gate_pre * (1.0 - sigmoid_gate))
    ).astype(jnp.bfloat16)
    grad_up = (grad_hidden * gate_act).astype(jnp.bfloat16)
    grad_normed_two = dot_back(grad_gate, gate_w) + dot_back(grad_up, up_w)
    grad_gain_two = jnp.sum(grad_normed_two * unit_two, axis=0)
    grad_middle = incoming.astype(jnp.float32) + norm_back(
        grad_normed_two, gain_two, unit_two, inverse_two
    )
    ff_entries = [
        ("gain", grad_gain_two),
        ("mat", normed_two, grad_gate),
        ("mat", normed_two, grad_up),
        ("mat", hidden, incoming),
    ]
    grad_branch = grad_middle.astype(jnp.bfloat16)
    grad_attended = dot_back(grad_branch, out_w).astype(jnp.bfloat16)
    grad_att_blk = grad_attended.reshape(block_count, WINDOW, head_count, HEAD)
    probs = jnp.exp(masked_scores(query_blk, key_blk, key_mask) - log_total)
    grad_probs = jnp.einsum(
        "bahd,bchd->bhac", grad_att_blk, value_blk, preferred_element_type=jnp.float32
    )
    grad_scores = (
        probs * (grad_probs - jnp.sum(grad_probs * probs, axis=-1, keepdims=True))
    ).astype(jnp.bfloat16)
    grad_query = jnp.einsum(
        "bhac,bchd->bahd", grad_scores, key_blk, preferred_element_type=jnp.float32
    ) * HEAD ** (-0.5)
    grad_query = grad_query.reshape(tok_rows, model_width).astype(jnp.bfloat16)
    key_parts = jnp.einsum(
        "bhac,bahd->bchd", grad_scores, query_blk, preferred_element_type=jnp.float32
    ) * HEAD ** (-0.5)
    grad_key = fold_keys(key_parts, tok_rows, model_width).astype(jnp.bfloat16)
    value_parts = jnp.einsum(
        "bhac,bahd->bchd", probs_low, grad_att_blk, preferred_element_type=jnp.float32
    )
    grad_value = fold_keys(value_parts, tok_rows, model_width).astype(jnp.bfloat16)
    grad_normed_one = (
        dot_back(grad_query, query_w) + dot_back(grad_key, key_w) + dot_back(grad_value, value_w)
    )
    grad_gain_one = jnp.sum(grad_normed_one * unit_one, axis=0)
    grad_dealt = (grad_middle + norm_back(grad_normed_one, gain_one, unit_one, inverse_one)).astype(
        jnp.bfloat16
    )
    returned_out, returned_grad = (
        lax.all_to_all(result, "dp", split_axis=0, concat_axis=0, tiled=True),
        lax.all_to_all(grad_dealt, "dp", split_axis=0, concat_axis=0, tiled=True),
    )
    layer_out = returned_out[send_slot]
    input_grad = returned_grad[send_slot]
    attn_entries = [
        ("gain", grad_gain_one),
        ("mat", normed_one, grad_query),
        ("mat", normed_one, grad_key),
        ("mat", normed_one, grad_value),
        ("mat", attended, grad_branch),
    ]
    every_entry = attn_entries + ff_entries
    all_summed = lax.psum_scatter(
        term_maker(every_entry, pieces, lax.axis_size(("dp", "fsdp")) * 1),
        ("dp", "fsdp"),
        scatter_dimension=0,
        tiled=True,
    )
    all_spans = split_spans(all_summed, every_entry, pieces)
    (
        span_gain_one,
        span_query,
        span_key,
        span_value,
        span_out,
        span_gain_two,
        span_gate,
        span_up,
        span_down,
    ) = all_spans
    return (
        layer_out,
        input_grad,
        span_gain_one,
        span_query,
        span_key,
        span_value,
        span_out,
        span_gain_two,
        span_gate,
        span_up,
        span_down,
    )


MESH = pl.DeviceIdType.MESH
TP = 4
CORES = 2
PAD = 96
VMEM_BYTES = 62 * 2**20

QKV, GATE, UP, OUT, DOWN = range(5)
F32 = jnp.float32
BF16 = jnp.bfloat16


def remote(src, dst, send, recv, device):
    return pltpu.make_async_remote_copy(
        src_ref=src, dst_ref=dst, send_sem=send, recv_sem=recv, device_id=device, device_id_type=MESH
    )


def nn(a, b):
    return lax.dot_general(a, b, (((1,), (0,)), ((), ())), preferred_element_type=F32)


def nt(a, b):
    return lax.dot_general(a, b, (((1,), (1,)), ((), ())), preferred_element_type=F32)


def tn(a, b):
    return lax.dot_general(a, b, (((0,), (0,)), ((), ())), preferred_element_type=F32)


def row_of(tile):
    return jnp.concatenate([tile[k : k + 1] for k in range(tile.shape[0])], axis=1)


def tile_of(row):
    return jnp.concatenate(
        [row[:, k * 128 : (k + 1) * 128] for k in range(row.shape[1] // 128)], axis=0
    )


def block_kernel(
    sizes,
    tok,
    cot,
    deal,
    lens,
    gain1,
    gain2,
    wq,
    wk,
    wv,
    wo,
    wg,
    wu,
    wd,
    lout,
    igrad,
    ogain1,
    oq,
    ok,
    ov,
    oo,
    ogain2,
    og,
    ou,
    od,
    b,
    s,
):
    nd, zn, rows, width, hw, fw, share = sizes
    scol = b.own
    gains = b.gown
    heads = hw // HEAD
    toks = TP * rows
    per = rows // nd
    dp = lax.axis_index("dp")
    f = lax.axis_index("fsdp")
    other = 1 - f
    z = dp // TP
    c = dp % TP
    sib = (dp, other)
    row_dev = width // (nd * CORES)

    barrier = pltpu.get_barrier_semaphore()
    pl.semaphore_signal(barrier, inc=1, device_id=sib, device_id_type=MESH)

    @pl.loop(1, nd)
    def _(k):
        pl.semaphore_signal(
            barrier, inc=1, device_id=(lax.rem(dp + k, nd), f), device_id_type=MESH
        )

    me = dp * CORES + f
    chunks = share * CORES * TP * zn // 64
    lane = lax.broadcasted_iota(jnp.int32, (1, 128), 1)

    def turned(v, by):
        return pltpu.roll(v, by % 128, 1) if by % 128 else v

    def heads_in(w, t):
        n = w.shape[0]
        b.flat[:n] = w[...].astype(F32)
        per_row = width // 128
        cols = [b.flat[pl.ds(j, row_dev, stride=per_row), :] for j in range(per_row)]
        for cc in range(TP):
            for u in range(hw // 128):
                left, right = cols[4 * u + cc // 2], cols[4 * u + 2 + cc // 2]
                tile = jnp.where(
                    lane < HEAD, turned(left, HEAD * (cc % 2)), turned(right, HEAD * (1 - cc % 2))
                )
                at = t * hw + u * 128
                scol[QKV, cc, :, at : at + 128] = tile.astype(BF16)

    def heads_out(o, t):
        per_row = width // 128
        for j in range(per_row):
            cc, h = 2 * (j % 2), j // 2
            at = t * hw + (h // 2) * 128
            left = b.rcol[QKV, cc, :, at : at + 128].astype(F32)
            right = b.rcol[QKV, cc + 1, :, at : at + 128].astype(F32)
            tile = jnp.where(
                lane < HEAD, turned(left, HEAD * (h % 2)), turned(right, HEAD * (1 - h % 2))
            )
            o[pl.ds(j, row_dev, stride=per_row), :] = tile

    def spans(cc, odd):
        total = share * CORES * TP * zn
        for k in range(CORES * zn):
            src = total * odd + share * (CORES * TP * (k // CORES) + CORES * cc + k % CORES)
            dst, left = PAD * k, share
            while left:
                n = min(left, 128 - src % 128, 128 - dst % 128)
                yield src, dst, n
                src, dst, left = src + n, dst + n, left - n

    def hidden_in(w, piece):
        n = w.shape[0]
        b.flat[:n] = w[...].astype(F32)
        for cc in range(TP):
            for odd in range(2):
                tiles_of = [jnp.zeros((row_dev // 2, 128), F32) for _ in range(fw // 128)]
                for src, dst, ln in spans(cc, odd):
                    v = b.flat[pl.ds(src // 128, row_dev // 2, stride=chunks), :]
                    at = dst % 128
                    keep = (lane >= at) & (lane < at + ln)
                    tiles_of[dst // 128] = jnp.where(
                        keep, turned(v, dst - src), tiles_of[dst // 128]
                    )
                for u, v in enumerate(tiles_of):
                    b.pairs[u, pl.ds(odd, row_dev // 2, stride=2), :] = v
            for u in range(fw // 128):
                scol[piece, cc, :, u * 128 : (u + 1) * 128] = b.pairs[u].astype(BF16)

    def hidden_out(o, piece):
        todo = [[] for _ in range(chunks)]
        for cc in range(TP):
            for u in range(fw // 128):
                b.wide[cc, u] = b.rcol[piece, cc, :, u * 128 : (u + 1) * 128].astype(F32)
            for odd in range(2):
                for src, dst, ln in spans(cc, odd):
                    todo[src // 128].append((src, dst, ln, cc, odd))
        for j in range(chunks):
            tile = jnp.zeros((row_dev // 2, 128), F32)
            for src, dst, ln, cc, odd in todo[j]:
                v = b.wide[cc, dst // 128, pl.ds(odd, row_dev // 2, stride=2), :]
                at = src % 128
                keep = (lane >= at) & (lane < at + ln)
                tile = jnp.where(keep, turned(v, src - dst), tile)
            o[pl.ds(j, row_dev // 2, stride=chunks), :] = tile

    def rows_in(w, out, n):
        count = w.shape[0]
        per_row = width // 128
        b.flat[:count] = w[...].astype(F32)
        if count < n * per_row:
            b.flat[count : n * per_row] = jnp.zeros((n * per_row - count, 128), F32)
        for j in range(per_row):
            out[:, j * 128 : (j + 1) * 128] = b.flat[pl.ds(j, n, stride=per_row), :].astype(BF16)

    def rows_out(o, v):
        per_row = width // 128
        n = o.shape[0] // per_row
        for j in range(per_row):
            o[pl.ds(j, n, stride=per_row), :] = v[:n, j * 128 : (j + 1) * 128]

    def all_peers(src, dst, send, recv, start=True):
        @pl.loop(1, nd)
        def _(k):
            to = lax.rem(dp + k, nd)
            remote(src(to), dst.at[dp], send.at[k], recv.at[k], (to, f)).start()

    def all_peers_recv(src, dst, send, recv):
        @pl.loop(1, nd)
        def _(k):
            at = lax.rem(dp + (nd - k), nd)
            remote(src(at), dst.at[at], send.at[k], recv.at[k], (at, f)).wait_recv()

    def all_peers_sent(src, dst, send, recv):
        @pl.loop(1, nd)
        def _(k):
            to = lax.rem(dp + k, nd)
            remote(src(to), dst.at[dp], send.at[k], recv.at[k], (to, f)).wait_send()

    cx = c % 2
    cy = c // 2

    def plane(k):
        xx = 1 - cx if k % 2 else cx
        yy = 1 - cy if k // 2 else cy
        cc = yy * 2 + xx
        return cc, (z * TP + cc, f)

    def gather_start(buf, send, recv):
        for k in range(1, TP):
            _, dev = plane(k)
            remote(buf.at[c], buf.at[c], send.at[k], recv.at[k], dev).start()

    def gather_recv(buf, send, recv):
        for k in range(1, TP):
            cc, dev = plane(k)
            remote(buf.at[c], buf.at[cc], send.at[k], recv.at[k], dev).wait_recv()

    def gather_sent(buf, send, recv):
        for k in range(1, TP):
            _, dev = plane(k)
            remote(buf.at[c], buf.at[c], send.at[k], recv.at[k], dev).wait_send()

    tiles = 4
    tw = width // tiles

    def gather_one(buf, k, send, recv):
        cc, dev = plane(k)
        remote(buf.at[c], buf.at[cc], send.at[k], recv.at[k], dev).wait_recv()

    def swap(src, dst, send, recv, k):
        cc, dev = plane(k)
        return remote(src.at[cc], dst.at[c], send.at[k], recv.at[k], dev)

    def swap_recv(src, dst, send, recv, k):
        cc, dev = plane(k)
        remote(src.at[cc], dst.at[cc], send.at[k], recv.at[k], dev).wait_recv()

    half = rows // 2
    low, high = pl.ds(0, half), pl.ds(half, half)

    def relay(buf, send, recv, k):
        at = (plane(2)[0], c, c, plane(1)[0])[k]
        ref = (buf.at[at, high], buf.at[at], buf.at[at], buf.at[at, low])[k]
        return remote(ref, ref, send.at[k], recv.at[k], plane((1, 1, 2, 2)[k])[1])

    def relay_wait(buf, send, recv, k):
        at = plane((3, 1, 2, 3)[k])[0]
        ref = (buf.at[at, high], buf.at[at], buf.at[at], buf.at[at, low])[k]
        remote(ref, ref, send.at[k], recv.at[k], plane((1, 1, 2, 2)[k])[1]).wait_recv()

    def relay_start(buf, send, recv):
        relay(buf, send, recv, 1).start()
        relay(buf, send, recv, 2).start()

    def relay_pass(buf, send, recv):
        relay_wait(buf, send, recv, 1)
        relay(buf, send, recv, 3).start()
        relay_wait(buf, send, recv, 2)
        relay(buf, send, recv, 0).start()

    def relay_done(buf, send, recv):
        relay_wait(buf, send, recv, 3)
        relay_wait(buf, send, recv, 0)

    def halves(src, land, send, recv, k):
        at = plane(3)[0]
        part = src.at[at, low] if k else src.at[at, high]
        return remote(part, land.at[k // 3], send.at[k], recv.at[k], plane(1 if k else 2)[1])

    def side(src, dst, send, recv, k):
        cc, dev = plane(k)
        return remote(src.at[cc], dst.at[k - 1], send.at[k], recv.at[k], dev)

    def reduce_start(src, land, send, recv):
        halves(src, land, send, recv, 3).start()
        halves(src, land, send, recv, 0).start()

    def reduce_side(src, dst, land, send, recv, k):
        cc = plane(k)[0]
        if k == 1:
            halves(src, land, send, recv, 0).wait_recv()
            src[cc, half:] = (src[cc, half:].astype(F32) + land[0].astype(F32)).astype(BF16)
        else:
            halves(src, land, send, recv, 3).wait_recv()
            src[cc, :half] = (src[cc, :half].astype(F32) + land[1].astype(F32)).astype(BF16)
        side(src, dst, send, recv, k).start()

    def reduce_sum(src, dst, send, recv):
        total = src[c].astype(F32)
        for k in (1, 2):
            side(src, dst, send, recv, k).wait_recv()
            total = total + dst[k - 1].astype(F32)
        return total

    def block(piece, at, core):
        if piece == OUT:
            return b.wout.at[c, at, core]
        if piece == DOWN:
            return b.wdown.at[at, core]
        return b.wcol.at[piece, at, :, core]

    def hop(piece, at, slot, to):
        return remote(
            block(piece, at, f),
            block(piece, at, f),
            s.z_s.at[piece, slot],
            s.z_r.at[piece, at],
            (to * TP + c, f),
        )

    def mirror(piece, at, core):
        return remote(
            block(piece, at, core),
            block(piece, at, core),
            s.b_s.at[piece, at],
            s.b_r.at[piece, at],
            sib,
        )

    def line_start(piece):
        @pl.when(z < zn - 1)
        def _():
            hop(piece, z, 0, z + 1).start()

        @pl.when(z > 0)
        def _():
            hop(piece, z, 1, z - 1).start()

        mirror(piece, z, f).start()

    def line_step(piece, d):
        @pl.when(z >= d)
        def _():
            hop(piece, z - d, 0, z).wait_recv()

            @pl.when(z < zn - 1)
            def _():
                hop(piece, z - d, 2 * d, z + 1).start()

            mirror(piece, z - d, f).start()

        @pl.when(z + d < zn)
        def _():
            hop(piece, z + d, 0, z).wait_recv()

            @pl.when(z > 0)
            def _():
                hop(piece, z + d, 2 * d + 1, z - 1).start()

            mirror(piece, z + d, f).start()

    def line_done(piece):
        for at in range(zn):
            mirror(piece, at, other).wait_recv()

    def line_sent(piece):
        for d in range(zn):

            @pl.when((z >= d) & (z < zn - 1))
            def _():
                hop(piece, z - d, 2 * d, z + 1).wait_send()

            @pl.when((z + d < zn) & (z > 0))
            def _():
                hop(piece, z + d, 2 * d + 1, z - 1).wait_send()

        for at in range(zn):
            mirror(piece, at, f).wait_send()

    def spread(piece, k):
        cc, dev = plane(k)
        return remote(
            scol.at[piece, cc],
            b.wcol.at[piece, z, c, f],
            s.s1_s.at[piece, k],
            s.s1_r.at[piece, k],
            dev,
        )

    def spread_recv(piece):
        for k in range(1, TP):
            cc, dev = plane(k)
            remote(
                scol.at[piece, cc],
                b.wcol.at[piece, z, cc, f],
                s.s1_s.at[piece, k],
                s.s1_r.at[piece, k],
                dev,
            ).wait_recv()

    slot = ((deal[...] >> _log2(rows * CORES)) * per) + (deal[...] & (per - 1))
    pick = (lax.broadcasted_iota(jnp.int32, (rows, rows), 0) == slot).astype(BF16)
    b.pick[...] = pick
    b.tsend[...] = nn(pick, tok[...]).reshape(nd, per, width).astype(BF16)
    b.csend[...] = nn(pick, cot[...]).reshape(nd, per, width).astype(BF16)

    gw = width // 128
    heads_in(wq, 0)
    heads_in(wk, 1)
    heads_in(wv, 2)
    spot = lax.broadcasted_iota(jnp.int32, (gw, 128), 0) == (me * row_dev) // 128
    spot = spot & ((lane // row_dev) == me % (128 // row_dev))

    def gain_tile(gain):
        g = gain[...].astype(F32)
        return jnp.where(spot, jnp.concatenate([g] * (128 // row_dev), axis=1), 0.0)

    gains[...] = jnp.concatenate([gain_tile(gain1), gain_tile(gain2)], axis=0).astype(BF16)
    pl.semaphore_wait(barrier, nd)

    all_peers(lambda to: gains, b.grecv, s.g_s, s.g_r)
    all_peers(lambda to: b.tsend.at[to], b.trecv, s.t_s, s.t_r)
    for k in range(1, TP):
        spread(QKV, k).start()
    b.wcol[QKV, z, c, f] = scol[QKV, c]
    b.trecv[dp] = b.tsend[dp]
    b.crecv[dp] = b.csend[dp]
    b.grecv[dp] = gains[...]
    ri = lax.broadcasted_iota(jnp.int32, (rows, rows), 0)
    ci = lax.broadcasted_iota(jnp.int32, (rows, rows), 1)
    seg_r = jnp.zeros((rows, rows), jnp.int32)
    seg_c = jnp.zeros((rows, rows), jnp.int32)
    bound = jnp.int32(0)
    for k in range(lens.shape[1]):
        bound = bound + lens[0, k]
        seg_r = seg_r + (ri >= bound).astype(jnp.int32)
        seg_c = seg_c + (ci >= bound).astype(jnp.int32)
    allowed = (seg_r == seg_c) & (ri >= ci) & (ri - ci < WINDOW)
    b.mask[c] = allowed.astype(F32).astype(BF16)
    gather_start(b.mask, s.m_s, s.m_r)
    rows_in(wo, b.wout.at[c, z, f], row_dev)

    all_peers_recv(lambda at: gains, b.grecv, s.g_s, s.g_r)
    gain_sum = jnp.sum(b.grecv[...].astype(F32), axis=0)
    b.gpart[f] = gain_sum.astype(BF16)
    gmirror = remote(b.gpart.at[f], b.gpart.at[f], s.gb_s, s.gb_r, sib)
    gmirror.start()

    spread_recv(QKV)
    line_start(QKV)
    for piece, w in ((GATE, wg), (UP, wu)):
        hidden_in(w, piece)
        for k in range(1, TP):
            spread(piece, k).start()
        b.wcol[piece, z, c, f] = scol[piece, c]
    rows_in(wd, b.wdown.at[z, f], PAD)

    all_peers_recv(lambda at: b.tsend.at[at], b.trecv, s.t_s, s.t_r)
    all_peers(lambda to: b.csend.at[to], b.crecv, s.c_s, s.c_r)
    remote(b.gpart.at[other], b.gpart.at[other], s.gb_s, s.gb_r, sib).wait_recv()
    gain_tile = b.gpart[0].astype(F32) + b.gpart[1].astype(F32)
    b.gain[0:1] = row_of(gain_tile[0:gw])
    b.gain[1:2] = row_of(gain_tile[gw : 2 * gw])

    x = b.trecv[...].astype(F32).reshape(rows, width)
    unit = x * lax.rsqrt(jnp.mean(x * x, axis=1, keepdims=True) + EPSILON)
    b.n1[c] = (unit * b.gain[0:1]).astype(BF16)
    gather_start(b.n1, s.a_s.at[0], s.a_r.at[0])

    line_step(QKV, 1)
    line_start(OUT)
    line_step(QKV, 2)
    spread_recv(GATE)
    spread_recv(UP)
    line_start(GATE)
    line_step(QKV, 3)
    line_step(OUT, 1)
    gather_recv(b.mask, s.m_s, s.m_r)
    line_done(QKV)
    scale = HEAD ** (-0.5)

    def out_rows(cc, core):
        return b.wout.at[cc, :, core]

    def out_send(k):
        _, dev = plane(k)
        return remote(out_rows(c, f), out_rows(c, f), s.o_s.at[k], s.o_r.at[k], dev)

    def out_mirror(k, core):
        rows_of = out_rows(plane(k)[0], core)
        return remote(rows_of, rows_of, s.om_s.at[k], s.om_r.at[k], sib)

    def attend(k):
        i = plane(k)[0]
        if k:
            gather_one(b.n1, k, s.a_s.at[0], s.a_r.at[0])
        w = b.wcol[QKV].reshape(width, fw)
        b.qkv[i] = nn(b.n1[i], w).astype(BF16)
        blk = b.qkv[i]
        allow = b.mask[i].astype(F32) > 0.5
        outs = []
        for h in range(heads):
            q = blk[:, h * HEAD : (h + 1) * HEAD]
            key = blk[:, hw + h * HEAD : hw + (h + 1) * HEAD]
            v = blk[:, 2 * hw + h * HEAD : 2 * hw + (h + 1) * HEAD]
            scores = jnp.where(allow, nt(q, key) * scale, -1e30)
            e = jnp.exp(scores - jnp.max(scores, axis=1, keepdims=True))
            p = e / jnp.sum(e, axis=1, keepdims=True)
            b.probs[i, h] = p
            outs.append(nn(p.astype(BF16), v))
        b.att[i] = jnp.concatenate(outs, axis=1).astype(BF16)
        if k:
            swap(b.att, b.attall, s.x_s.at[0], s.x_r.at[0], k).start()
        else:
            b.attall[c] = b.att[c]

    attend(0)
    line_step(OUT, 2)
    attend(1)
    line_step(OUT, 3)
    for k in range(1, TP):
        out_send(k).start()
    line_start(UP)
    attend(2)
    line_step(GATE, 1)
    attend(3)
    all_peers_recv(lambda at: b.csend.at[at], b.crecv, s.c_s, s.c_r)
    b.call[c] = b.crecv[...].reshape(rows, width)
    line_step(GATE, 2)
    for k in range(1, TP):
        cc, dev = plane(k)
        remote(out_rows(c, f), out_rows(cc, f), s.o_s.at[k], s.o_r.at[k], dev).wait_recv()
        out_mirror(k, f).start()
    gather_start(b.call, s.a_s.at[1], s.a_r.at[1])
    line_done(OUT)
    for k in range(1, TP):
        out_mirror(k, other).wait_recv()
        swap_recv(b.att, b.attall, s.x_s.at[0], s.x_r.at[0], k)
    middle = b.trecv[...].astype(F32).reshape(rows, width)
    for i in range(TP):
        middle = middle + nn(b.attall[i], b.wout[i].reshape(hw, width))
    b.middle[...] = middle
    unit = middle * lax.rsqrt(jnp.mean(middle * middle, axis=1, keepdims=True) + EPSILON)
    b.n2[c] = (unit * b.gain[1:2]).astype(BF16)
    gather_start(b.n2, s.a_s.at[2], s.a_r.at[2])
    line_step(GATE, 3)
    line_step(UP, 1)
    line_start(DOWN)
    line_step(UP, 2)
    line_step(UP, 3)
    line_done(GATE)
    line_done(UP)

    def feed(k):
        i = plane(k)[0]
        if k:
            gather_one(b.n2, k, s.a_s.at[2], s.a_r.at[2])
        gate = nn(b.n2[i], b.wcol[GATE].reshape(width, fw))
        up = nn(b.n2[i], b.wcol[UP].reshape(width, fw))
        b.gate[i] = gate
        b.up[i] = up
        b.hid[i] = (gate * jax.nn.sigmoid(gate) * up).astype(BF16)

    feed(0)
    feed(1)
    feed(2)
    feed(3)
    line_step(DOWN, 1)

    def presum(piece, src, dst):
        return remote(src, dst, s.p_s.at[piece], s.p_r.at[piece], sib)

    def part_of(piece):
        if piece == OUT:
            return b.gout.at[:, f], b.cout, b.sout, b.eout
        if piece == DOWN:
            return b.gdown.at[:, f], b.cdown, b.sdown, b.edown
        return b.gcol.at[piece, :, :, f], b.ccol.at[piece], b.scol.at[piece], b.ecol.at[piece]

    def half_of(piece):
        if piece == OUT:
            return b.gout.at[:, other]
        if piece == DOWN:
            return b.gdown.at[:, other]
        return b.gcol.at[piece, :, :, other]

    edge = (z == 0) | (z == zn - 1)

    def travel(piece, at, slot, send, to):
        _, _, part, land = part_of(piece)
        return remote(
            part.at[at], land.at[slot], s.e_s.at[piece, send], s.e_r.at[piece, slot], (to * TP + c, f)
        )

    inner = 1 + z // (zn - 1)
    end = (z - 1) * (zn - 1)

    def edge_send(piece, k):
        at, slot = ((zn - 1 - z, 3), (zn - 1 - inner, 2), (inner, 0))[k]
        return travel(piece, at, slot, slot, inner)

    def inner_send(piece, k):
        to, slot = ((end, 0), (zn - 1 - end, 1), (zn - 1 - z, 1))[k]
        return travel(piece, to, slot, k, to)

    def sum_start(piece):
        mine, came, part, _ = part_of(piece)
        presum(piece, half_of(piece), came).wait_recv()

        @pl.loop(0, zn)
        def _(j):
            part[j] = (mine[j].astype(F32) + came[j].astype(F32)).astype(BF16)

        @pl.when(edge)
        def _():
            for k in range(3):
                edge_send(piece, k).start()

        @pl.when(jnp.logical_not(edge))
        def _():
            inner_send(piece, 0).start()

    def sum_middle(piece):
        _, _, part, land = part_of(piece)

        @pl.when(jnp.logical_not(edge))
        def _():
            for k, slot, at in ((1, 3, zn - 1 - end), (2, 2, zn - 1 - z)):
                travel(piece, at, slot, slot, z).wait_recv()
                part[at] = (part[at].astype(F32) + land[slot].astype(F32)).astype(BF16)
                inner_send(piece, k).start()

    def sum_end(piece):
        _, _, part, land = part_of(piece)
        for slot in (0, 1):
            travel(piece, z, slot, slot, z).wait_recv()
        return part[z].astype(F32) + land[0].astype(F32) + land[1].astype(F32)

    def sum_sent(piece):
        @pl.when(edge)
        def _():
            for k in range(3):
                edge_send(piece, k).wait_send()

        @pl.when(jnp.logical_not(edge))
        def _():
            for k in range(3):
                inner_send(piece, k).wait_send()

        presum(piece, half_of(piece), part_of(piece)[1]).wait_send()

    def col_grad(piece, act, grad):
        @pl.loop(0, zn)
        def _(j):
            a = act[:, :, pl.ds(pl.multiple_of(j * tw, tw), tw)].reshape(toks, tw)
            g = tn(a, grad[...].reshape(toks, fw))
            b.gcol[piece, j] = g.reshape(TP, CORES, row_dev, fw).astype(BF16)

        presum(piece, half_of(piece), b.ccol.at[piece]).start()

    def home(piece, k):
        cc, dev = plane(k)
        return remote(
            b.tcol.at[piece, cc], b.rcol.at[piece, c], s.h2_s.at[piece, k], s.h2_r.at[piece, k], dev
        )

    def col_end(piece):
        b.tcol[piece] = sum_end(piece).astype(BF16)
        for k in range(1, TP):
            home(piece, k).start()
        b.rcol[piece, c] = b.tcol[piece, c]

    def my_gain(tile):
        row = jnp.sum(jnp.where(spot, tile, 0.0), axis=0, keepdims=True)
        total = row[:, :row_dev]
        for k in range(1, 128 // row_dev):
            total = total + row[:, k * row_dev : (k + 1) * row_dev]
        return total

    def col_recv(piece):
        for k in range(1, TP):
            cc, dev = plane(k)
            remote(
                b.tcol.at[piece, cc], b.rcol.at[piece, cc], s.h2_s.at[piece, k], s.h2_r.at[piece, k], dev
            ).wait_recv()

    gather_recv(b.call, s.a_s.at[1], s.a_r.at[1])
    call = b.call[...].reshape(toks, width)
    span = 4 * PAD
    for j in range(fw // span):
        w = tn(b.hid[:, :, j * span : (j + 1) * span].reshape(toks, span), call)
        b.gdown[2 * j : 2 * j + 2] = w.reshape(2, CORES, PAD, width).astype(BF16)
    presum(DOWN, half_of(DOWN), b.cdown).start()
    line_step(DOWN, 2)
    sum_start(DOWN)
    line_step(DOWN, 3)
    line_done(DOWN)

    def feed_back(k):
        i = plane(k)[0]
        gh = nt(b.call[i], b.wdown[...].reshape(fw, width))
        gate = b.gate[i]
        sg = jax.nn.sigmoid(gate)
        b.ggate[i] = (gh * b.up[i] * sg * (1.0 + gate * (1.0 - sg))).astype(BF16)
        b.gup[i] = (gh * gate * sg).astype(BF16)
        v = nt(b.ggate[i], b.wcol[GATE].reshape(width, fw))
        v = v + nt(b.gup[i], b.wcol[UP].reshape(width, fw))
        b.p[1][i] = v.astype(BF16)

    red1 = (b.p[1], b.q[1], b.land.at[1], s.x_s.at[1], s.x_r.at[1])
    red0 = (b.p[0], b.q[0], b.land.at[0], s.x_s.at[3], s.x_r.at[3])
    red2 = (b.p[2], b.q[2], b.land.at[2], s.x_s.at[4], s.x_r.at[4])

    def red_start(red):
        reduce_start(red[0], red[2], red[3], red[4])

    def red_sum(red):
        return reduce_sum(red[0], red[1], red[3], red[4])

    feed_back(3)
    red_start(red1)
    feed_back(1)
    reduce_side(*red1, 1)
    feed_back(2)
    reduce_side(*red1, 2)
    feed_back(0)
    col_grad(GATE, b.n2, b.ggate)
    sum_middle(DOWN)
    col_grad(UP, b.n2, b.gup)
    sum_start(GATE)

    def feed_out(k):
        i = plane(k)[0]
        b.p[0][i] = nn(b.hid[i], b.wdown[...].reshape(fw, width)).astype(BF16)

    for k in (3, 1, 2, 0):
        feed_out(k)
    sum_start(UP)

    gn = red_sum(red1)
    red_start(red0)
    middle = b.middle[...]
    inv = lax.rsqrt(jnp.mean(middle * middle, axis=1, keepdims=True) + EPSILON)
    unit = middle * inv
    b.ggain[1:2] = jnp.sum(gn * unit, axis=0, keepdims=True)
    a = gn * b.gain[1:2]
    gm = b.call[c].astype(F32) + inv * (a - unit * jnp.mean(a * unit, axis=1, keepdims=True))
    b.gmid[...] = gm
    gb = gm.astype(BF16)
    b.gb[c] = gb
    for k in (3, 1, 2, 0):
        i = plane(k)[0]
        b.gasend[i] = nt(gb, b.wout[i].reshape(hw, width)).astype(BF16)
        if k:
            swap(b.gasend, b.ga, s.x_s.at[2], s.x_r.at[2], k).start()
        else:
            b.ga[c] = b.gasend[c]
    reduce_side(*red0, 1)
    reduce_side(*red0, 2)
    sum_middle(GATE)

    def attend_back(k):
        i = plane(k)[0]
        if k:
            swap_recv(b.gasend, b.ga, s.x_s.at[2], s.x_r.at[2], k)
        blk = b.qkv[i]
        gab = b.ga[i]
        gq, gk, gv = [], [], []
        for h in range(heads):
            q = blk[:, h * HEAD : (h + 1) * HEAD]
            key = blk[:, hw + h * HEAD : hw + (h + 1) * HEAD]
            v = blk[:, 2 * hw + h * HEAD : 2 * hw + (h + 1) * HEAD]
            ga = gab[:, h * HEAD : (h + 1) * HEAD]
            p = b.probs[i, h]
            gp = nt(ga, v)
            gs = (p * (gp - jnp.sum(p * gp, axis=1, keepdims=True))).astype(BF16)
            gq.append(nn(gs, key) * scale)
            gk.append(tn(gs, q) * scale)
            gv.append(tn(p.astype(BF16), ga))
        b.gqkv[i] = jnp.concatenate(gq + gk + gv, axis=1).astype(BF16)
        b.p[2][i] = nt(b.gqkv[i], b.wcol[QKV].reshape(width, fw)).astype(BF16)

    attend_back(3)
    red_start(red2)
    relay_start(b.gb, s.a_s.at[3], s.a_r.at[3])
    attend_back(1)
    reduce_side(*red2, 1)
    attend_back(2)
    reduce_side(*red2, 2)
    attend_back(0)
    col_grad(QKV, b.n1, b.gqkv)
    sum_middle(UP)
    sum_start(QKV)
    relay_pass(b.gb, s.a_s.at[3], s.a_r.at[3])
    rows_out(od, sum_end(DOWN))

    res = b.middle[...] + red_sum(red0)
    b.lsend[...] = res.reshape(nd, per, width).astype(BF16)
    all_peers(lambda to: b.lsend.at[to], b.lrecv, s.l_s, s.l_r)
    b.lrecv[dp] = b.lsend[dp]

    gn = red_sum(red2)
    x = b.trecv[...].astype(F32).reshape(rows, width)
    inv = lax.rsqrt(jnp.mean(x * x, axis=1, keepdims=True) + EPSILON)
    unit = x * inv
    b.ggain[0:1] = jnp.sum(gn * unit, axis=0, keepdims=True)
    a = gn * b.gain[0:1]
    gx = b.gmid[...] + inv * (a - unit * jnp.mean(a * unit, axis=1, keepdims=True))
    b.isend[...] = gx.reshape(nd, per, width).astype(BF16)
    all_peers(lambda to: b.isend.at[to], b.irecv, s.i_s, s.i_r)
    b.irecv[dp] = b.isend[dp]
    b.hsend[...] = jnp.concatenate([tile_of(b.ggain[0:1]), tile_of(b.ggain[1:2])], axis=0)
    all_peers(lambda to: b.hsend, b.hrecv, s.h_s, s.h_r)
    b.hrecv[dp] = b.hsend[...]

    relay_done(b.gb, s.a_s.at[3], s.a_r.at[3])
    gb_all = b.gb[...].reshape(toks, width)
    b.gout[...] = (
        tn(b.att[...].reshape(toks, hw), gb_all).reshape(zn, CORES, row_dev, width).astype(BF16)
    )
    presum(OUT, half_of(OUT), b.cout).start()
    sum_middle(QKV)
    sum_start(OUT)

    col_end(GATE)
    all_peers_recv(lambda at: b.lsend.at[at], b.lrecv, s.l_s, s.l_r)
    pick = b.pick[...]
    lout[...] = tn(pick, b.lrecv[...].reshape(rows, width)).astype(BF16)
    sum_middle(OUT)
    col_end(UP)
    all_peers_recv(lambda at: b.hsend, b.hrecv, s.h_s, s.h_r)
    b.hpart[f] = jnp.sum(b.hrecv[...], axis=0)
    hmirror = remote(b.hpart.at[f], b.hpart.at[f], s.hb_s, s.hb_r, sib)
    hmirror.start()
    all_peers_recv(lambda at: b.isend.at[at], b.irecv, s.i_s, s.i_r)
    igrad[...] = tn(pick, b.irecv[...].reshape(rows, width)).astype(BF16)
    remote(b.hpart.at[other], b.hpart.at[other], s.hb_s, s.hb_r, sib).wait_recv()
    gain_sum = b.hpart[0] + b.hpart[1]
    ogain1[...] = my_gain(gain_sum[:gw])
    ogain2[...] = my_gain(gain_sum[gw:])
    col_recv(GATE)
    hidden_out(og, GATE)
    col_end(QKV)
    col_recv(UP)
    hidden_out(ou, UP)
    rows_out(oo, sum_end(OUT))
    col_recv(QKV)
    heads_out(oq, 0)
    heads_out(ok, 1)
    heads_out(ov, 2)

    gmirror.wait_send()
    hmirror.wait_send()
    all_peers_sent(lambda to: gains, b.grecv, s.g_s, s.g_r)
    all_peers_sent(lambda to: b.tsend.at[to], b.trecv, s.t_s, s.t_r)
    all_peers_sent(lambda to: b.csend.at[to], b.crecv, s.c_s, s.c_r)
    all_peers_sent(lambda to: b.lsend.at[to], b.lrecv, s.l_s, s.l_r)
    all_peers_sent(lambda to: b.isend.at[to], b.irecv, s.i_s, s.i_r)
    all_peers_sent(lambda to: b.hsend, b.hrecv, s.h_s, s.h_r)
    gather_sent(b.mask, s.m_s, s.m_r)
    for i, buf in enumerate((b.n1, b.call, b.n2)):
        gather_sent(buf, s.a_s.at[i], s.a_r.at[i])
    for k in range(TP):
        relay(b.gb, s.a_s.at[3], s.a_r.at[3], k).wait_send()
    for src, dst, land, send, recv in (red0, red1, red2):
        for k in (3, 0):
            halves(src, land, send, recv, k).wait_send()
        for k in (1, 2):
            side(src, dst, send, recv, k).wait_send()
    for k in range(1, TP):
        swap(b.att, b.attall, s.x_s.at[0], s.x_r.at[0], k).wait_send()
        swap(b.gasend, b.ga, s.x_s.at[2], s.x_r.at[2], k).wait_send()
        out_send(k).wait_send()
        out_mirror(k, f).wait_send()
        for piece in (QKV, GATE, UP):
            spread(piece, k).wait_send()
            home(piece, k).wait_send()
    for piece in (QKV, GATE, UP, OUT, DOWN):
        line_sent(piece)
        sum_sent(piece)


def _log2(n):
    return n.bit_length() - 1


def kernel_takes(dp_count, core_count, rows, width, hidden):
    pieces = dp_count * core_count
    zn = dp_count // TP
    return (
        core_count == CORES
        and dp_count % TP == 0
        and rows == 128
        and rows % dp_count == 0
        and rows // dp_count == 8
        and width == zn * 256
        and width // HEAD == dp_count
        and width // pieces == HEAD // CORES
        and hidden % pieces == 0
        and hidden // pieces <= PAD
        and PAD * CORES * zn % 256 == 0
        and zn == 4
    )


def planned(
    dp_count,
    tokens,
    dealing,
    lengths,
    norm1_gain,
    w_query,
    w_key,
    w_value,
    w_out,
    norm2_gain,
    w_gate,
    w_up,
    w_down,
    cotangent,
):
    nd = dp_count
    zn = nd // TP
    rows, width = tokens.shape
    pieces = nd * CORES
    row_dev = width // pieces
    hidden = w_gate.shape[0] * pieces // width
    unit = hidden // pieces
    hw = width // TP
    fw = PAD * CORES * zn
    gw = width // 128
    toks = TP * rows
    per = rows // nd
    V = pltpu.VMEM
    bufs = dict(
        pick=V((rows, rows), BF16),
        own=V((3, TP, row_dev, fw), BF16),
        gown=V((2 * gw, 128), BF16),
        flat=V((PAD * width // 128, 128), F32),
        pairs=V((fw // 128, row_dev, 128), F32),
        wide=V((TP, fw // 128, row_dev, 128), F32),
        tsend=V((nd, per, width), BF16),
        trecv=V((nd, per, width), BF16),
        csend=V((nd, per, width), BF16),
        crecv=V((nd, per, width), BF16),
        lsend=V((nd, per, width), BF16),
        lrecv=V((nd, per, width), BF16),
        isend=V((nd, per, width), BF16),
        irecv=V((nd, per, width), BF16),
        grecv=V((nd, 2 * gw, 128), BF16),
        gpart=V((CORES, 2 * gw, 128), BF16),
        gain=V((8, width), F32),
        ggain=V((8, width), F32),
        hsend=V((2 * gw, 128), F32),
        hrecv=V((nd, 2 * gw, 128), F32),
        hpart=V((CORES, 2 * gw, 128), F32),
        mask=V((TP, rows, rows), BF16),
        wcol=V((3, zn, TP, CORES, row_dev, fw), BF16),
        wout=V((TP, zn, CORES, row_dev, width), BF16),
        wdown=V((zn, CORES, PAD, width), BF16),
        n1=V((TP, rows, width), BF16),
        n2=V((TP, rows, width), BF16),
        call=V((TP, rows, width), BF16),
        gb=V((TP, rows, width), BF16),
        qkv=V((TP, rows, 3 * hw), BF16),
        probs=V((TP, hw // HEAD, rows, rows), F32),
        att=V((TP, rows, hw), BF16),
        attall=V((TP, rows, hw), BF16),
        gasend=V((TP, rows, hw), BF16),
        middle=V((rows, width), F32),
        gmid=V((rows, width), F32),
        gate=V((TP, rows, fw), F32),
        up=V((TP, rows, fw), F32),
        hid=V((TP, rows, fw), BF16),
        ggate=V((TP, rows, fw), BF16),
        gup=V((TP, rows, fw), BF16),
        ga=V((TP, rows, hw), BF16),
        gqkv=V((TP, rows, 3 * hw), BF16),
        gcol=V((3, zn, TP, CORES, row_dev, fw), BF16),
        ccol=V((3, zn, TP, row_dev, fw), BF16),
        scol=V((3, zn, TP, row_dev, fw), BF16),
        ecol=V((3, 4, TP, row_dev, fw), BF16),
        tcol=V((3, TP, row_dev, fw), BF16),
        rcol=V((3, TP, row_dev, fw), BF16),
        gout=V((zn, CORES, row_dev, width), BF16),
        cout=V((zn, row_dev, width), BF16),
        sout=V((zn, row_dev, width), BF16),
        eout=V((4, row_dev, width), BF16),
        gdown=V((zn, CORES, PAD, width), BF16),
        cdown=V((zn, PAD, width), BF16),
        sdown=V((zn, PAD, width), BF16),
        edown=V((4, PAD, width), BF16),
    )
    bufs.update(
        p=[V((TP, rows, width), BF16) for _ in range(3)],
        q=[V((2, rows, width), BF16) for _ in range(3)],
        land=V((3, 2, rows // 2, width), BF16),
    )
    S = pltpu.SemaphoreType.DMA
    each = S((nd,))
    sems = dict(
        g_s=each,
        g_r=each,
        t_s=each,
        t_r=each,
        c_s=each,
        c_r=each,
        l_s=each,
        l_r=each,
        i_s=each,
        i_r=each,
        h_s=each,
        h_r=each,
        gb_s=S(()),
        gb_r=S(()),
        hb_s=S(()),
        hb_r=S(()),
        m_s=S((TP,)),
        m_r=S((TP,)),
        s1_s=S((3, TP)),
        s1_r=S((3, TP)),
        z_s=S((5, 2 * zn)),
        z_r=S((5, zn)),
        b_s=S((5, zn)),
        b_r=S((5, zn)),
        a_s=S((4, TP)),
        a_r=S((4, TP)),
        o_s=S((TP,)),
        o_r=S((TP,)),
        om_s=S((TP,)),
        om_r=S((TP,)),
        x_s=S((5, TP)),
        x_r=S((5, TP)),
        p_s=S((5,)),
        p_r=S((5,)),
        e_s=S((5, 4)),
        e_r=S((5, 4)),
        h2_s=S((3, TP)),
        h2_r=S((3, TP)),
    )
    n_io = 13 + 11
    spaces, shape_of = jax.tree.flatten((bufs, sems))

    def entry(*refs):
        io, rest = refs[:n_io], refs[n_io:]
        b, s = jax.tree.unflatten(shape_of, rest)
        block_kernel((nd, zn, rows, width, hw, fw, unit), *io, SimpleNamespace(**b), SimpleNamespace(**s))

    vm = pl.BlockSpec(memory_space=pltpu.VMEM)
    sm = pl.BlockSpec(memory_space=pltpu.SMEM)
    head_span = jax.ShapeDtypeStruct((row_dev * width // 128, 128), F32)
    hidden_span = jax.ShapeDtypeStruct((unit * width // 128, 128), F32)
    gain_span = jax.ShapeDtypeStruct((1, row_dev), F32)
    row_block = jax.ShapeDtypeStruct((rows, width), BF16)

    def lanes(v):
        return v.reshape(-1, 128)

    outs = pl.pallas_call(
        entry,
        out_shape=(row_block, row_block, gain_span)
        + (head_span,) * 4
        + (gain_span,)
        + (hidden_span,) * 3,
        in_specs=[vm, vm, vm, sm] + [vm] * 9,
        out_specs=(vm,) * 11,
        scratch_shapes=spaces,
        compiler_params=pltpu.CompilerParams(
            collective_id=0, has_side_effects=True, vmem_limit_bytes=VMEM_BYTES
        ),
        name="block_fwd_bwd",
    )(
        tokens,
        cotangent,
        dealing.reshape(1, rows),
        lengths,
        norm1_gain.reshape(1, row_dev),
        norm2_gain.reshape(1, row_dev),
        lanes(w_query),
        lanes(w_key),
        lanes(w_value),
        lanes(w_out),
        lanes(w_gate),
        lanes(w_up),
        lanes(w_down),
    )
    whole = pl.BlockSpec(memory_space=pl.ANY)

    def hand_over(*refs):
        n = len(refs) // 2
        copies = [pltpu.make_async_copy(refs[i], refs[n + i], refs[-1].at[i]) for i in range(n)]
        for cp in copies:
            cp.start()
        for cp in copies:
            cp.wait()

    outs = pl.pallas_call(
        hand_over,
        out_shape=tuple(jax.ShapeDtypeStruct(v.shape, v.dtype) for v in outs),
        in_specs=[vm] * len(outs),
        out_specs=(whole,) * len(outs),
        scratch_shapes=[S((len(outs),))],
        name="hand_over",
    )(*outs)
    return tuple(outs[:2]) + tuple(v.reshape(-1) for v in outs[2:])


def dispatch(dp_count, core_count, *args):
    tokens, w_gate = args[0], args[9]
    rows, width = tokens.shape
    hidden = w_gate.shape[0] * dp_count * core_count // width
    if kernel_takes(dp_count, core_count, rows, width, hidden):
        return planned(dp_count, *args)
    return body(*args)


def solution(mesh):
    in_specs = (
        P(("dp", "fsdp"), None),
        P(("dp", "fsdp")),
        P(("dp", "fsdp"), None),
        P(("dp", "fsdp")),
        P(("dp", "fsdp")),
        P(("dp", "fsdp")),
        P(("dp", "fsdp")),
        P(("dp", "fsdp")),
        P(("dp", "fsdp")),
        P(("dp", "fsdp")),
        P(("dp", "fsdp")),
        P(("dp", "fsdp")),
        P(("dp", "fsdp"), None),
    )
    out_specs = (
        P(("dp", "fsdp"), None),
        P(("dp", "fsdp"), None),
        P(("dp", "fsdp")),
        P(("dp", "fsdp")),
        P(("dp", "fsdp")),
        P(("dp", "fsdp")),
        P(("dp", "fsdp")),
        P(("dp", "fsdp")),
        P(("dp", "fsdp")),
        P(("dp", "fsdp")),
        P(("dp", "fsdp")),
    )
    return jax.shard_map(
        functools.partial(dispatch, mesh.shape["dp"], mesh.shape["fsdp"]),
         mesh=mesh, in_specs=in_specs, out_specs=out_specs, check_vma=False)
```

```python
import functools
from types import SimpleNamespace

import jax
import jax.numpy as jnp
from jax import lax
from jax.experimental import pallas as pl
from jax.experimental.pallas import tpu as pltpu
from jax.sharding import PartitionSpec as P

HEAD = 64
WINDOW = 64


EPSILON = 1e-06


def unpack(flat_list, model_width):
    gain_one, query_w, key_w, value_w, out_w, gain_two, gate_w, up_w, down_w = flat_list
    hidden_units = gate_w.shape[0] // model_width
    return (
        gain_one.astype(jnp.float32),
        query_w.reshape(model_width, model_width),
        key_w.reshape(model_width, model_width),
        value_w.reshape(model_width, model_width),
        out_w.reshape(model_width, model_width),
        gain_two.astype(jnp.float32),
        gate_w.reshape(model_width, hidden_units),
        up_w.reshape(model_width, hidden_units),
        down_w.reshape(hidden_units, model_width),
    )


def normalize(values, gain_vec):
    inverse = lax.rsqrt(jnp.mean(values * values, axis=-1, keepdims=True) + EPSILON)
    unit_rows = values * inverse
    return (unit_rows * gain_vec, unit_rows, inverse)


def norm_back(upstream, gain_vec, unit_rows, inverse):
    scaled = upstream * gain_vec
    return inverse * (scaled - unit_rows * jnp.mean(scaled * unit_rows, axis=-1, keepdims=True))


def dot_rows(first_op, second_op):
    return lax.dot_general(
        first_op, second_op, (((0,), (0,)), ((), ())), preferred_element_type=jnp.float32
    )


def dot_back(first_op, second_op):
    return lax.dot_general(
        first_op, second_op, (((1,), (1,)), ((), ())), preferred_element_type=jnp.float32
    )


def flat_piece(entry, count, pieces):
    if entry[0] == "gain":
        vector = entry[1]
        share = vector.shape[0] // pieces
        return vector.reshape(count, share)
    left_op, right_op = (entry[1], entry[2])
    row_total = left_op.shape[1]
    col_total = right_op.shape[1]
    share = row_total * col_total // pieces
    block = dot_rows(left_op, right_op)
    flat = block.reshape(-1)
    return flat.reshape(count, share)


def term_maker(entries, pieces, count):
    return jnp.concatenate([flat_piece(entry, count, pieces) for entry in entries], axis=1)


def split_spans(summed, entries, pieces):
    flat = summed.reshape(-1)
    results = []
    offset = 0
    for entry in entries:
        if entry[0] == "gain":
            share = entry[1].shape[0] // pieces
        else:
            share = entry[1].shape[1] * entry[2].shape[1] // pieces
        results.append(flat[offset : offset + share])
        offset = offset + share
    return results


def block_mask(segment, tok_rows):
    block_count = tok_rows // WINDOW
    padded = jnp.concatenate([jnp.full((WINDOW,), -1, jnp.int32), segment])
    seg_query = segment.reshape(block_count, WINDOW)
    seg_keys = jnp.concatenate([padded[:-WINDOW].reshape(block_count, WINDOW), seg_query], axis=1)
    offset = jnp.arange(WINDOW)[:, None] - jnp.arange(2 * WINDOW)[None, :] + WINDOW
    inside = (offset >= 0) & (offset < WINDOW)
    return inside[None] & (seg_query[:, :, None] == seg_keys[:, None, :])


def key_blocks(values, block_count):
    padded = jnp.concatenate([jnp.zeros((WINDOW,) + values.shape[1:], values.dtype), values])
    previous = padded[:-WINDOW].reshape((block_count, WINDOW) + values.shape[1:])
    current = values.reshape((block_count, WINDOW) + values.shape[1:])
    return jnp.concatenate([previous, current], axis=1)


def fold_keys(key_parts, tok_rows, model_width):
    previous = key_parts[:, :WINDOW]
    current = key_parts[:, WINDOW:]
    shifted = jnp.concatenate([previous[1:], jnp.zeros_like(previous[:1])], axis=0)
    return (current + shifted).reshape(tok_rows, model_width)


def masked_scores(query_blk, key_blk, key_mask):
    scores = jnp.einsum(
        "bahd,bchd->bhac", query_blk, key_blk, preferred_element_type=jnp.float32
    ) * HEAD ** (-0.5)
    return jnp.where(key_mask, scores, -1e30)


def body(
    tokens,
    dealing,
    lengths,
    norm1_gain,
    w_query,
    w_key,
    w_value,
    w_out,
    norm2_gain,
    w_gate,
    w_up,
    w_down,
    cotangent,
):
    tok_rows, model_width = tokens.shape
    dp_count = lax.axis_size("dp")
    fsdp_count = lax.axis_size("fsdp")
    pieces = lax.axis_size(("dp", "fsdp"))
    per_peer = tok_rows // dp_count
    local_pos = dealing % tok_rows
    target_dp = dealing // tok_rows // fsdp_count
    send_slot = target_dp * per_peer + local_pos % per_peer
    sent_tokens = jnp.zeros_like(tokens).at[send_slot].set(tokens)
    sent_cot = jnp.zeros_like(cotangent).at[send_slot].set(cotangent)
    inputs, incoming = (
        lax.all_to_all(sent_tokens, "dp", split_axis=0, concat_axis=0, tiled=True),
        lax.all_to_all(sent_cot, "dp", split_axis=0, concat_axis=0, tiled=True),
    )
    bounds = jnp.cumsum(lengths[0])
    positions = jnp.arange(tok_rows, dtype=jnp.int32)
    segment = jnp.sum((positions[:, None] >= bounds[None, :]).astype(jnp.int32), axis=1)
    block_count = tok_rows // WINDOW
    head_count = model_width // HEAD
    key_mask = block_mask(segment, tok_rows)[:, None]
    flat_weights = (norm1_gain, w_query, w_key, w_value, w_out, norm2_gain, w_gate, w_up, w_down)
    gathered = (
        lax.all_gather(flat_weights[0], ("dp", "fsdp"), axis=0, tiled=True),
        lax.all_gather(flat_weights[1], ("dp", "fsdp"), axis=0, tiled=True),
        lax.all_gather(flat_weights[2], ("dp", "fsdp"), axis=0, tiled=True),
        lax.all_gather(flat_weights[3], ("dp", "fsdp"), axis=0, tiled=True),
        lax.all_gather(flat_weights[4], ("dp", "fsdp"), axis=0, tiled=True),
        lax.all_gather(flat_weights[5], ("dp", "fsdp"), axis=0, tiled=True),
        lax.all_gather(flat_weights[6], ("dp", "fsdp"), axis=0, tiled=True),
        lax.all_gather(flat_weights[7], ("dp", "fsdp"), axis=0, tiled=True),
        lax.all_gather(flat_weights[8], ("dp", "fsdp"), axis=0, tiled=True),
    )
    gain_one, query_w, key_w, value_w, out_w, gain_two, gate_w, up_w, down_w = unpack(
        gathered, model_width
    )
    input_f = inputs.astype(jnp.float32)
    scaled_one, unit_one, inverse_one = normalize(input_f, gain_one)
    normed_one = scaled_one.astype(jnp.bfloat16)
    query_act = jnp.dot(normed_one, query_w, preferred_element_type=jnp.float32).astype(
        jnp.bfloat16
    )
    key_act = jnp.dot(normed_one, key_w, preferred_element_type=jnp.float32).astype(jnp.bfloat16)
    value_act = jnp.dot(normed_one, value_w, preferred_element_type=jnp.float32).astype(
        jnp.bfloat16
    )
    query_blk = query_act.reshape(block_count, WINDOW, head_count, HEAD)
    key_blk = key_blocks(key_act.reshape(tok_rows, head_count, HEAD), block_count)
    value_blk = key_blocks(value_act.reshape(tok_rows, head_count, HEAD), block_count)
    scores = masked_scores(query_blk, key_blk, key_mask)
    row_peak = jnp.max(scores, axis=-1, keepdims=True)
    exp_scores = jnp.exp(scores - row_peak)
    row_total = jnp.sum(exp_scores, axis=-1, keepdims=True)
    log_total = row_peak + jnp.log(row_total)
    probs_low = (exp_scores / row_total).astype(jnp.bfloat16)
    attended = jnp.einsum(
        "bhac,bchd->bahd", probs_low, value_blk, preferred_element_type=jnp.float32
    )
    attended = attended.reshape(tok_rows, model_width).astype(jnp.bfloat16)
    middle = input_f + jnp.dot(attended, out_w, preferred_element_type=jnp.float32)
    scaled_two, unit_two, inverse_two = normalize(middle, gain_two)
    normed_two = scaled_two.astype(jnp.bfloat16)
    gate_pre = jnp.dot(normed_two, gate_w, preferred_element_type=jnp.float32)
    up_pre = jnp.dot(normed_two, up_w, preferred_element_type=jnp.float32)
    sigmoid_gate = jax.nn.sigmoid(gate_pre)
    gate_act = gate_pre * sigmoid_gate
    hidden = (gate_act * up_pre).astype(jnp.bfloat16)
    result = (middle + jnp.dot(hidden, down_w, preferred_element_type=jnp.float32)).astype(
        jnp.bfloat16
    )
    regathered = (
        lax.all_gather(flat_weights[0], ("dp", "fsdp"), axis=0, tiled=True),
        lax.all_gather(flat_weights[1], ("dp", "fsdp"), axis=0, tiled=True),
        lax.all_gather(flat_weights[2], ("dp", "fsdp"), axis=0, tiled=True),
        lax.all_gather(flat_weights[3], ("dp", "fsdp"), axis=0, tiled=True),
        lax.all_gather(flat_weights[4], ("dp", "fsdp"), axis=0, tiled=True),
        lax.all_gather(flat_weights[5], ("dp", "fsdp"), axis=0, tiled=True),
        lax.all_gather(flat_weights[6], ("dp", "fsdp"), axis=0, tiled=True),
        lax.all_gather(flat_weights[7], ("dp", "fsdp"), axis=0, tiled=True),
        lax.all_gather(flat_weights[8], ("dp", "fsdp"), axis=0, tiled=True),
    )
    gain_one, query_w, key_w, value_w, out_w, gain_two, gate_w, up_w, down_w = unpack(
        regathered, model_width
    )
    grad_hidden = dot_back(incoming, down_w)
    grad_gate = (
        grad_hidden * up_pre * sigmoid_gate * (1.0 + gate_pre * (1.0 - sigmoid_gate))
    ).astype(jnp.bfloat16)
    grad_up = (grad_hidden * gate_act).astype(jnp.bfloat16)
    grad_normed_two = dot_back(grad_gate, gate_w) + dot_back(grad_up, up_w)
    grad_gain_two = jnp.sum(grad_normed_two * unit_two, axis=0)
    grad_middle = incoming.astype(jnp.float32) + norm_back(
        grad_normed_two, gain_two, unit_two, inverse_two
    )
    ff_entries = [
        ("gain", grad_gain_two),
        ("mat", normed_two, grad_gate),
        ("mat", normed_two, grad_up),
        ("mat", hidden, incoming),
    ]
    grad_branch = grad_middle.astype(jnp.bfloat16)
    grad_attended = dot_back(grad_branch, out_w).astype(jnp.bfloat16)
    grad_att_blk = grad_attended.reshape(block_count, WINDOW, head_count, HEAD)
    probs = jnp.exp(masked_scores(query_blk, key_blk, key_mask) - log_total)
    grad_probs = jnp.einsum(
        "bahd,bchd->bhac", grad_att_blk, value_blk, preferred_element_type=jnp.float32
    )
    grad_scores = (
        probs * (grad_probs - jnp.sum(grad_probs * probs, axis=-1, keepdims=True))
    ).astype(jnp.bfloat16)
    grad_query = jnp.einsum(
        "bhac,bchd->bahd", grad_scores, key_blk, preferred_element_type=jnp.float32
    ) * HEAD ** (-0.5)
    grad_query = grad_query.reshape(tok_rows, model_width).astype(jnp.bfloat16)
    key_parts = jnp.einsum(
        "bhac,bahd->bchd", grad_scores, query_blk, preferred_element_type=jnp.float32
    ) * HEAD ** (-0.5)
    grad_key = fold_keys(key_parts, tok_rows, model_width).astype(jnp.bfloat16)
    value_parts = jnp.einsum(
        "bhac,bahd->bchd", probs_low, grad_att_blk, preferred_element_type=jnp.float32
    )
    grad_value = fold_keys(value_parts, tok_rows, model_width).astype(jnp.bfloat16)
    grad_normed_one = (
        dot_back(grad_query, query_w) + dot_back(grad_key, key_w) + dot_back(grad_value, value_w)
    )
    grad_gain_one = jnp.sum(grad_normed_one * unit_one, axis=0)
    grad_dealt = (grad_middle + norm_back(grad_normed_one, gain_one, unit_one, inverse_one)).astype(
        jnp.bfloat16
    )
    returned_out, returned_grad = (
        lax.all_to_all(result, "dp", split_axis=0, concat_axis=0, tiled=True),
        lax.all_to_all(grad_dealt, "dp", split_axis=0, concat_axis=0, tiled=True),
    )
    layer_out = returned_out[send_slot]
    input_grad = returned_grad[send_slot]
    attn_entries = [
        ("gain", grad_gain_one),
        ("mat", normed_one, grad_query),
        ("mat", normed_one, grad_key),
        ("mat", normed_one, grad_value),
        ("mat", attended, grad_branch),
    ]
    every_entry = attn_entries + ff_entries
    all_summed = lax.psum_scatter(
        term_maker(every_entry, pieces, lax.axis_size(("dp", "fsdp")) * 1),
        ("dp", "fsdp"),
        scatter_dimension=0,
        tiled=True,
    )
    all_spans = split_spans(all_summed, every_entry, pieces)
    (
        span_gain_one,
        span_query,
        span_key,
        span_value,
        span_out,
        span_gain_two,
        span_gate,
        span_up,
        span_down,
    ) = all_spans
    return (
        layer_out,
        input_grad,
        span_gain_one,
        span_query,
        span_key,
        span_value,
        span_out,
        span_gain_two,
        span_gate,
        span_up,
        span_down,
    )


MESH = pl.DeviceIdType.MESH
TP = 4
CORES = 2
PAD = 96
VMEM_BYTES = 62 * 2**20

QKV, GATE, UP, OUT, DOWN = range(5)
F32 = jnp.float32
BF16 = jnp.bfloat16


def remote(src, dst, send, recv, device):
    return pltpu.make_async_remote_copy(
        src_ref=src, dst_ref=dst, send_sem=send, recv_sem=recv, device_id=device, device_id_type=MESH
    )


def nn(a, b):
    return lax.dot_general(a, b, (((1,), (0,)), ((), ())), preferred_element_type=F32)


def nt(a, b):
    return lax.dot_general(a, b, (((1,), (1,)), ((), ())), preferred_element_type=F32)


def tn(a, b):
    return lax.dot_general(a, b, (((0,), (0,)), ((), ())), preferred_element_type=F32)


def row_of(tile):
    return jnp.concatenate([tile[k : k + 1] for k in range(tile.shape[0])], axis=1)


def tile_of(row):
    return jnp.concatenate(
        [row[:, k * 128 : (k + 1) * 128] for k in range(row.shape[1] // 128)], axis=0
    )


def block_kernel(
    sizes,
    tok,
    cot,
    deal,
    lens,
    gain1,
    gain2,
    wq,
    wk,
    wv,
    wo,
    wg,
    wu,
    wd,
    lout,
    igrad,
    ogain1,
    oq,
    ok,
    ov,
    oo,
    ogain2,
    og,
    ou,
    od,
    b,
    s,
):
    nd, zn, rows, width, hw, fw, share = sizes
    scol = b.own
    gains = b.gown
    heads = hw // HEAD
    toks = TP * rows
    per = rows // nd
    dp = lax.axis_index("dp")
    f = lax.axis_index("fsdp")
    other = 1 - f
    z = dp // TP
    c = dp % TP
    sib = (dp, other)
    row_dev = width // (nd * CORES)

    barrier = pltpu.get_barrier_semaphore()
    pl.semaphore_signal(barrier, inc=1, device_id=sib, device_id_type=MESH)

    @pl.loop(1, nd)
    def _(k):
        pl.semaphore_signal(
            barrier, inc=1, device_id=(lax.rem(dp + k, nd), f), device_id_type=MESH
        )

    me = dp * CORES + f
    chunks = share * CORES * TP * zn // 64
    lane = lax.broadcasted_iota(jnp.int32, (1, 128), 1)

    def turned(v, by):
        return pltpu.roll(v, by % 128, 1) if by % 128 else v

    def heads_in(w, t):
        n = w.shape[0]
        b.flat[:n] = w[...].astype(F32)
        per_row = width // 128
        cols = [b.flat[pl.ds(j, row_dev, stride=per_row), :] for j in range(per_row)]
        for cc in range(TP):
            for u in range(hw // 128):
                left, right = cols[4 * u + cc // 2], cols[4 * u + 2 + cc // 2]
                tile = jnp.where(
                    lane < HEAD, turned(left, HEAD * (cc % 2)), turned(right, HEAD * (1 - cc % 2))
                )
                at = t * hw + u * 128
                scol[QKV, cc, :, at : at + 128] = tile.astype(BF16)

    def heads_out(o, t):
        per_row = width // 128
        for j in range(per_row):
            cc, h = 2 * (j % 2), j // 2
            at = t * hw + (h // 2) * 128
            left = b.rcol[QKV, cc, :, at : at + 128].astype(F32)
            right = b.rcol[QKV, cc + 1, :, at : at + 128].astype(F32)
            tile = jnp.where(
                lane < HEAD, turned(left, HEAD * (h % 2)), turned(right, HEAD * (1 - h % 2))
            )
            o[pl.ds(j, row_dev, stride=per_row), :] = tile

    def spans(cc, odd):
        total = share * CORES * TP * zn
        for k in range(CORES * zn):
            src = total * odd + share * (CORES * TP * (k // CORES) + CORES * cc + k % CORES)
            dst, left = PAD * k, share
            while left:
                n = min(left, 128 - src % 128, 128 - dst % 128)
                yield src, dst, n
                src, dst, left = src + n, dst + n, left - n

    def hidden_in(w, piece):
        n = w.shape[0]
        b.flat[:n] = w[...].astype(F32)
        for cc in range(TP):
            for odd in range(2):
                tiles_of = [jnp.zeros((row_dev // 2, 128), F32) for _ in range(fw // 128)]
                for src, dst, ln in spans(cc, odd):
                    v = b.flat[pl.ds(src // 128, row_dev // 2, stride=chunks), :]
                    at = dst % 128
                    keep = (lane >= at) & (lane < at + ln)
                    tiles_of[dst // 128] = jnp.where(
                        keep, turned(v, dst - src), tiles_of[dst // 128]
                    )
                for u, v in enumerate(tiles_of):
                    b.pairs[u, pl.ds(odd, row_dev // 2, stride=2), :] = v
            for u in range(fw // 128):
                scol[piece, cc, :, u * 128 : (u + 1) * 128] = b.pairs[u].astype(BF16)

    def hidden_out(o, piece):
        todo = [[] for _ in range(chunks)]
        for cc in range(TP):
            for u in range(fw // 128):
                b.wide[cc, u] = b.rcol[piece, cc, :, u * 128 : (u + 1) * 128].astype(F32)
            for odd in range(2):
                for src, dst, ln in spans(cc, odd):
                    todo[src // 128].append((src, dst, ln, cc, odd))
        for j in range(chunks):
            tile = jnp.zeros((row_dev // 2, 128), F32)
            for src, dst, ln, cc, odd in todo[j]:
                v = b.wide[cc, dst // 128, pl.ds(odd, row_dev // 2, stride=2), :]
                at = src % 128
                keep = (lane >= at) & (lane < at + ln)
                tile = jnp.where(keep, turned(v, src - dst), tile)
            o[pl.ds(j, row_dev // 2, stride=chunks), :] = tile

    def rows_in(w, out, n):
        count = w.shape[0]
        per_row = width // 128
        b.flat[:count] = w[...].astype(F32)
        if count < n * per_row:
            b.flat[count : n * per_row] = jnp.zeros((n * per_row - count, 128), F32)
        for j in range(per_row):
            out[:, j * 128 : (j + 1) * 128] = b.flat[pl.ds(j, n, stride=per_row), :].astype(BF16)

    def rows_out(o, v):
        per_row = width // 128
        n = o.shape[0] // per_row
        for j in range(per_row):
            o[pl.ds(j, n, stride=per_row), :] = v[:n, j * 128 : (j + 1) * 128]

    def all_peers(src, dst, send, recv, start=True):
        @pl.loop(1, nd)
        def _(k):
            to = lax.rem(dp + k, nd)
            remote(src(to), dst.at[dp], send.at[k], recv.at[k], (to, f)).start()

    def all_peers_recv(src, dst, send, recv):
        @pl.loop(1, nd)
        def _(k):
            at = lax.rem(dp + (nd - k), nd)
            remote(src(at), dst.at[at], send.at[k], recv.at[k], (at, f)).wait_recv()

    def all_peers_sent(src, dst, send, recv):
        @pl.loop(1, nd)
        def _(k):
            to = lax.rem(dp + k, nd)
            remote(src(to), dst.at[dp], send.at[k], recv.at[k], (to, f)).wait_send()

    cx = c % 2
    cy = c // 2

    def plane(k):
        xx = 1 - cx if k % 2 else cx
        yy = 1 - cy if k // 2 else cy
        cc = yy * 2 + xx
        return cc, (z * TP + cc, f)

    def gather_start(buf, send, recv):
        for k in range(1, TP):
            _, dev = plane(k)
            remote(buf.at[c], buf.at[c], send.at[k], recv.at[k], dev).start()

    def gather_recv(buf, send, recv):
        for k in range(1, TP):
            cc, dev = plane(k)
            remote(buf.at[c], buf.at[cc], send.at[k], recv.at[k], dev).wait_recv()

    def gather_sent(buf, send, recv):
        for k in range(1, TP):
            _, dev = plane(k)
            remote(buf.at[c], buf.at[c], send.at[k], recv.at[k], dev).wait_send()

    tiles = 4
    tw = width // tiles

    def swap(src, dst, send, recv, k):
        cc, dev = plane(k)
        return remote(src.at[cc], dst.at[c], send.at[k], recv.at[k], dev)

    def swap_recv(src, dst, send, recv, k):
        cc, dev = plane(k)
        remote(src.at[cc], dst.at[cc], send.at[k], recv.at[k], dev).wait_recv()

    half = rows // 2
    low, high = pl.ds(0, half), pl.ds(half, half)

    def rows_part(buf):
        def get(at, part):
            return buf.at[at] if part is None else buf.at[at, (low, high)[part]]

        return get

    def relay_refs(get, send, recv, k, at):
        ref = get(at, (1, None, None, 0)[k])
        return remote(ref, ref, send.at[k], recv.at[k], plane((1, 1, 2, 2)[k])[1])

    def relay(get, send, recv, k):
        return relay_refs(get, send, recv, k, (plane(2)[0], c, c, plane(1)[0])[k])

    def relay_wait(get, send, recv, k):
        relay_refs(get, send, recv, k, plane((3, 1, 2, 3)[k])[0]).wait_recv()

    def relay_start(get, send, recv):
        relay(get, send, recv, 1).start()
        relay(get, send, recv, 2).start()

    def relay_pass(get, send, recv):
        relay_wait(get, send, recv, 1)
        relay(get, send, recv, 3).start()
        relay_wait(get, send, recv, 2)
        relay(get, send, recv, 0).start()

    def relay_done(get, send, recv):
        relay_wait(get, send, recv, 3)
        relay_wait(get, send, recv, 0)

    def halves(src, land, send, recv, k):
        at = plane(3)[0]
        part = src.at[at, low] if k else src.at[at, high]
        return remote(part, land.at[k // 3], send.at[k], recv.at[k], plane(1 if k else 2)[1])

    def side(src, dst, send, recv, k):
        cc, dev = plane(k)
        return remote(src.at[cc], dst.at[k - 1], send.at[k], recv.at[k], dev)

    def reduce_start(src, land, send, recv):
        halves(src, land, send, recv, 3).start()
        halves(src, land, send, recv, 0).start()

    def reduce_side(src, dst, land, send, recv, k):
        cc = plane(k)[0]
        if k == 1:
            halves(src, land, send, recv, 0).wait_recv()
            src[cc, half:] = (src[cc, half:].astype(F32) + land[0].astype(F32)).astype(BF16)
        else:
            halves(src, land, send, recv, 3).wait_recv()
            src[cc, :half] = (src[cc, :half].astype(F32) + land[1].astype(F32)).astype(BF16)
        side(src, dst, send, recv, k).start()

    def reduce_sum(src, dst, send, recv):
        total = src[c].astype(F32)
        for k in (1, 2):
            side(src, dst, send, recv, k).wait_recv()
            total = total + dst[k - 1].astype(F32)
        return total

    def block(piece, at, core):
        if piece == OUT:
            return b.wout.at[c, at, core]
        if piece == DOWN:
            return b.wdown.at[at, core]
        return b.wcol.at[piece, at, :, core]

    def hop(piece, at, slot, to):
        return remote(
            block(piece, at, f),
            block(piece, at, f),
            s.z_s.at[piece, slot],
            s.z_r.at[piece, at],
            (to * TP + c, f),
        )

    def mirror(piece, at, core):
        return remote(
            block(piece, at, core),
            block(piece, at, core),
            s.b_s.at[piece, at],
            s.b_r.at[piece, at],
            sib,
        )

    own_hops = ((1, 0), (-1, 1), (2, 2), (-2, 3))

    def reaches(by):
        return z + by < zn if by > 0 else z + by >= 0

    def line_start(piece):
        for by, slot in own_hops:

            @pl.when(reaches(by))
            def _():
                hop(piece, z, slot, z + by).start()

        mirror(piece, z, f).start()

    def line_pass(piece):
        for at_z, at, slot, to in ((zn - 2, 0, 4, zn - 1), (1, zn - 1, 5, 0)):

            @pl.when(z == at_z)
            def _():
                hop(piece, at, slot, z).wait_recv()
                hop(piece, at, slot, to).start()

    def line_take(piece):
        for d in range(1, zn):
            for by, passer in ((-d, zn - 2), (d, 1)):

                @pl.when(reaches(by) & ((z != passer) if d == zn - 2 else True))
                def _():
                    hop(piece, z + by, 0, z).wait_recv()

                @pl.when(reaches(by))
                def _():
                    mirror(piece, z + by, f).start()

    def line_done(piece):
        for at in range(zn):
            mirror(piece, at, other).wait_recv()

    def line_sent(piece):
        for by, slot in own_hops:

            @pl.when(reaches(by))
            def _():
                hop(piece, z, slot, z + by).wait_send()

        for at_z, at, slot, to in ((zn - 2, 0, 4, zn - 1), (1, zn - 1, 5, 0)):

            @pl.when(z == at_z)
            def _():
                hop(piece, at, slot, to).wait_send()

        for at in range(zn):
            mirror(piece, at, f).wait_send()

    def spread(piece, k):
        cc, dev = plane(k)
        return remote(
            scol.at[piece, cc],
            b.wcol.at[piece, z, c, f],
            s.s1_s.at[piece, k],
            s.s1_r.at[piece, k],
            dev,
        )

    def spread_recv(piece):
        for k in range(1, TP):
            cc, dev = plane(k)
            remote(
                scol.at[piece, cc],
                b.wcol.at[piece, z, cc, f],
                s.s1_s.at[piece, k],
                s.s1_r.at[piece, k],
                dev,
            ).wait_recv()

    slot = ((deal[...] >> _log2(rows * CORES)) * per) + (deal[...] & (per - 1))
    pick = (lax.broadcasted_iota(jnp.int32, (rows, rows), 0) == slot).astype(BF16)
    b.pick[...] = pick
    b.tsend[...] = nn(pick, tok[...]).reshape(nd, per, width).astype(BF16)
    b.csend[...] = nn(pick, cot[...]).reshape(nd, per, width).astype(BF16)

    gw = width // 128
    heads_in(wq, 0)
    heads_in(wk, 1)
    heads_in(wv, 2)
    spot = lax.broadcasted_iota(jnp.int32, (gw, 128), 0) == (me * row_dev) // 128
    spot = spot & ((lane // row_dev) == me % (128 // row_dev))

    def gain_tile(gain):
        g = gain[...].astype(F32)
        return jnp.where(spot, jnp.concatenate([g] * (128 // row_dev), axis=1), 0.0)

    gains[...] = jnp.concatenate([gain_tile(gain1), gain_tile(gain2)], axis=0).astype(BF16)
    pl.semaphore_wait(barrier, nd)

    all_peers(lambda to: gains, b.grecv, s.g_s, s.g_r)
    all_peers(lambda to: b.tsend.at[to], b.trecv, s.t_s, s.t_r)
    for k in range(1, TP):
        spread(QKV, k).start()
    b.wcol[QKV, z, c, f] = scol[QKV, c]
    b.trecv[dp] = b.tsend[dp]
    b.crecv[dp] = b.csend[dp]
    b.grecv[dp] = gains[...]
    ri = lax.broadcasted_iota(jnp.int32, (rows, rows), 0)
    ci = lax.broadcasted_iota(jnp.int32, (rows, rows), 1)
    seg_r = jnp.zeros((rows, rows), jnp.int32)
    seg_c = jnp.zeros((rows, rows), jnp.int32)
    bound = jnp.int32(0)
    for k in range(lens.shape[1]):
        bound = bound + lens[0, k]
        seg_r = seg_r + (ri >= bound).astype(jnp.int32)
        seg_c = seg_c + (ci >= bound).astype(jnp.int32)
    allowed = (seg_r == seg_c) & (ri >= ci) & (ri - ci < WINDOW)
    b.mask[c] = allowed.astype(F32).astype(BF16)
    gather_start(b.mask, s.m_s, s.m_r)
    rows_in(wo, b.wout.at[c, z, f], row_dev)

    all_peers_recv(lambda at: gains, b.grecv, s.g_s, s.g_r)
    gain_sum = jnp.sum(b.grecv[...].astype(F32), axis=0)
    b.gpart[f] = gain_sum.astype(BF16)
    gmirror = remote(b.gpart.at[f], b.gpart.at[f], s.gb_s, s.gb_r, sib)
    gmirror.start()

    spread_recv(QKV)
    line_start(QKV)
    line_start(OUT)
    for piece, w in ((GATE, wg), (UP, wu)):
        hidden_in(w, piece)
        for k in range(1, TP):
            spread(piece, k).start()
        b.wcol[piece, z, c, f] = scol[piece, c]
    rows_in(wd, b.wdown.at[z, f], PAD)

    all_peers_recv(lambda at: b.tsend.at[at], b.trecv, s.t_s, s.t_r)
    all_peers(lambda to: b.csend.at[to], b.crecv, s.c_s, s.c_r)
    remote(b.gpart.at[other], b.gpart.at[other], s.gb_s, s.gb_r, sib).wait_recv()
    gain_tile = b.gpart[0].astype(F32) + b.gpart[1].astype(F32)
    b.gain[0:1] = row_of(gain_tile[0:gw])
    b.gain[1:2] = row_of(gain_tile[gw : 2 * gw])

    x = b.trecv[...].astype(F32).reshape(rows, width)
    unit = x * lax.rsqrt(jnp.mean(x * x, axis=1, keepdims=True) + EPSILON)
    b.n1[c] = (unit * b.gain[0:1]).astype(BF16)
    n1_way = (rows_part(b.n1), s.a_s.at[0], s.a_r.at[0])
    call_way = (rows_part(b.call), s.a_s.at[1], s.a_r.at[1])
    n2_way = (rows_part(b.n2), s.a_s.at[2], s.a_r.at[2])
    gb_way = (rows_part(b.gb), s.a_s.at[3], s.a_r.at[3])
    relay_start(*n1_way)
    line_pass(QKV)
    spread_recv(GATE)
    line_start(GATE)
    relay_pass(*n1_way)
    spread_recv(UP)
    line_pass(OUT)
    line_take(QKV)
    gather_recv(b.mask, s.m_s, s.m_r)
    line_start(UP)
    line_done(QKV)
    scale = HEAD ** (-0.5)

    def out_part(at, part):
        return b.wout.at[at, :, f] if part is None else b.wout.at[at, pl.ds(part * (zn // 2), zn // 2), f]

    out_way = (out_part, s.o_s, s.o_r)

    def out_mirror(k, core):
        rows_of = b.wout.at[plane(k)[0], :, core]
        return remote(rows_of, rows_of, s.om_s.at[k], s.om_r.at[k], sib)

    def attend(k):
        i = plane(k)[0]
        if k == 3:
            relay_done(*n1_way)
        w = b.wcol[QKV].reshape(width, fw)
        b.qkv[i] = nn(b.n1[i], w).astype(BF16)
        blk = b.qkv[i]
        allow = b.mask[i].astype(F32) > 0.5
        outs = []
        for h in range(heads):
            q = blk[:, h * HEAD : (h + 1) * HEAD]
            key = blk[:, hw + h * HEAD : hw + (h + 1) * HEAD]
            v = blk[:, 2 * hw + h * HEAD : 2 * hw + (h + 1) * HEAD]
            scores = jnp.where(allow, nt(q, key) * scale, -1e30)
            e = jnp.exp(scores - jnp.max(scores, axis=1, keepdims=True))
            p = e / jnp.sum(e, axis=1, keepdims=True)
            b.probs[i, h] = p
            outs.append(nn(p.astype(BF16), v))
        b.att[i] = jnp.concatenate(outs, axis=1).astype(BF16)
        if k:
            swap(b.att, b.attall, s.x_s.at[0], s.x_r.at[0], k).start()
        else:
            b.attall[c] = b.att[c]

    attend(1)
    line_take(OUT)
    relay_start(*out_way)
    attend(2)
    attend(3)
    line_pass(GATE)
    attend(0)
    line_start(DOWN)
    relay_pass(*out_way)
    all_peers_recv(lambda at: b.csend.at[at], b.crecv, s.c_s, s.c_r)
    b.call[c] = b.crecv[...].reshape(rows, width)
    for k in (1, 2):
        out_mirror(k, f).start()
    line_done(OUT)
    line_pass(UP)
    relay_done(*out_way)
    out_mirror(3, f).start()
    for k in range(1, TP):
        swap_recv(b.att, b.attall, s.x_s.at[0], s.x_r.at[0], k)
        out_mirror(k, other).wait_recv()
    middle = b.trecv[...].astype(F32).reshape(rows, width)
    for i in range(TP):
        middle = middle + nn(b.attall[i], b.wout[i].reshape(hw, width))
    b.middle[...] = middle
    unit = middle * lax.rsqrt(jnp.mean(middle * middle, axis=1, keepdims=True) + EPSILON)
    b.n2[c] = (unit * b.gain[1:2]).astype(BF16)
    relay_start(*n2_way)
    line_take(GATE)
    relay_pass(*n2_way)
    relay_start(*call_way)
    line_take(UP)
    line_done(GATE)
    line_done(UP)

    def feed(k):
        i = plane(k)[0]
        if k == 3:
            relay_done(*n2_way)
        gate = nn(b.n2[i], b.wcol[GATE].reshape(width, fw))
        up = nn(b.n2[i], b.wcol[UP].reshape(width, fw))
        b.gate[i] = gate
        b.up[i] = up
        b.hid[i] = (gate * jax.nn.sigmoid(gate) * up).astype(BF16)

    feed(0)
    feed(1)
    feed(2)
    relay_pass(*call_way)
    feed(3)
    line_pass(DOWN)

    def presum(piece, src, dst):
        return remote(src, dst, s.p_s.at[piece], s.p_r.at[piece], sib)

    def part_of(piece):
        if piece == OUT:
            return b.gout.at[:, f], b.cout, b.sout, b.eout
        if piece == DOWN:
            return b.gdown.at[:, f], b.cdown, b.sdown, b.edown
        return b.gcol.at[piece, :, :, f], b.ccol.at[piece], b.scol.at[piece], b.ecol.at[piece]

    def half_of(piece):
        if piece == OUT:
            return b.gout.at[:, other]
        if piece == DOWN:
            return b.gdown.at[:, other]
        return b.gcol.at[piece, :, :, other]

    edge = (z == 0) | (z == zn - 1)

    def travel(piece, at, slot, send, to):
        _, _, part, land = part_of(piece)
        return remote(
            part.at[at], land.at[slot], s.e_s.at[piece, send], s.e_r.at[piece, slot], (to * TP + c, f)
        )

    inner = 1 + z // (zn - 1)
    end = (z - 1) * (zn - 1)

    def edge_send(piece, k):
        at, slot = ((zn - 1 - z, 3), (zn - 1 - inner, 2), (inner, 0))[k]
        return travel(piece, at, slot, slot, inner)

    def inner_send(piece, k):
        to, slot = ((end, 0), (zn - 1 - end, 1), (zn - 1 - z, 1))[k]
        return travel(piece, to, slot, k, to)

    def sum_start(piece):
        mine, came, part, _ = part_of(piece)
        presum(piece, half_of(piece), came).wait_recv()

        @pl.loop(0, zn)
        def _(j):
            part[j] = (mine[j].astype(F32) + came[j].astype(F32)).astype(BF16)

        @pl.when(edge)
        def _():
            for k in range(3):
                edge_send(piece, k).start()

        @pl.when(jnp.logical_not(edge))
        def _():
            inner_send(piece, 0).start()

    def sum_middle(piece):
        _, _, part, land = part_of(piece)

        @pl.when(jnp.logical_not(edge))
        def _():
            for k, slot, at in ((1, 3, zn - 1 - end), (2, 2, zn - 1 - z)):
                travel(piece, at, slot, slot, z).wait_recv()
                part[at] = (part[at].astype(F32) + land[slot].astype(F32)).astype(BF16)
                inner_send(piece, k).start()

    def sum_end(piece):
        _, _, part, land = part_of(piece)
        for slot in (0, 1):
            travel(piece, z, slot, slot, z).wait_recv()
        return part[z].astype(F32) + land[0].astype(F32) + land[1].astype(F32)

    def sum_sent(piece):
        @pl.when(edge)
        def _():
            for k in range(3):
                edge_send(piece, k).wait_send()

        @pl.when(jnp.logical_not(edge))
        def _():
            for k in range(3):
                inner_send(piece, k).wait_send()

        presum(piece, half_of(piece), part_of(piece)[1]).wait_send()

    def col_grad(piece, act, grad):
        @pl.loop(0, zn)
        def _(j):
            a = act[:, :, pl.ds(pl.multiple_of(j * tw, tw), tw)].reshape(toks, tw)
            g = tn(a, grad[...].reshape(toks, fw))
            b.gcol[piece, j] = g.reshape(TP, CORES, row_dev, fw).astype(BF16)

        presum(piece, half_of(piece), b.ccol.at[piece]).start()

    def home(piece, k):
        cc, dev = plane(k)
        return remote(
            b.tcol.at[piece, cc], b.rcol.at[piece, c], s.h2_s.at[piece, k], s.h2_r.at[piece, k], dev
        )

    def col_end(piece):
        b.tcol[piece] = sum_end(piece).astype(BF16)
        for k in range(1, TP):
            home(piece, k).start()
        b.rcol[piece, c] = b.tcol[piece, c]

    def my_gain(tile):
        row = jnp.sum(jnp.where(spot, tile, 0.0), axis=0, keepdims=True)
        total = row[:, :row_dev]
        for k in range(1, 128 // row_dev):
            total = total + row[:, k * row_dev : (k + 1) * row_dev]
        return total

    def col_recv(piece):
        for k in range(1, TP):
            cc, dev = plane(k)
            remote(
                b.tcol.at[piece, cc], b.rcol.at[piece, cc], s.h2_s.at[piece, k], s.h2_r.at[piece, k], dev
            ).wait_recv()

    relay_done(*call_way)
    call = b.call[...].reshape(toks, width)
    span = 4 * PAD
    for j in range(fw // span):
        w = tn(b.hid[:, :, j * span : (j + 1) * span].reshape(toks, span), call)
        b.gdown[2 * j : 2 * j + 2] = w.reshape(2, CORES, PAD, width).astype(BF16)
    presum(DOWN, half_of(DOWN), b.cdown).start()
    sum_start(DOWN)
    line_take(DOWN)
    line_done(DOWN)

    def feed_back(k):
        i = plane(k)[0]
        gh = nt(b.call[i], b.wdown[...].reshape(fw, width))
        gate = b.gate[i]
        sg = jax.nn.sigmoid(gate)
        b.ggate[i] = (gh * b.up[i] * sg * (1.0 + gate * (1.0 - sg))).astype(BF16)
        b.gup[i] = (gh * gate * sg).astype(BF16)
        v = nt(b.ggate[i], b.wcol[GATE].reshape(width, fw))
        v = v + nt(b.gup[i], b.wcol[UP].reshape(width, fw))
        b.p[1][i] = v.astype(BF16)

    red1 = (b.p[1], b.q[1], b.land.at[1], s.x_s.at[1], s.x_r.at[1])
    red0 = (b.p[0], b.q[0], b.land.at[0], s.x_s.at[3], s.x_r.at[3])
    red2 = (b.p[2], b.q[2], b.land.at[2], s.x_s.at[4], s.x_r.at[4])

    def red_start(red):
        reduce_start(red[0], red[2], red[3], red[4])

    def red_sum(red):
        return reduce_sum(red[0], red[1], red[3], red[4])

    feed_back(3)
    red_start(red1)
    feed_back(1)
    reduce_side(*red1, 1)
    feed_back(2)
    reduce_side(*red1, 2)
    feed_back(0)
    col_grad(GATE, b.n2, b.ggate)
    sum_middle(DOWN)
    col_grad(UP, b.n2, b.gup)
    sum_start(GATE)

    def feed_out(k):
        i = plane(k)[0]
        b.p[0][i] = nn(b.hid[i], b.wdown[...].reshape(fw, width)).astype(BF16)

    for k in (3, 1, 2, 0):
        feed_out(k)
    sum_start(UP)

    gn = red_sum(red1)
    red_start(red0)
    middle = b.middle[...]
    inv = lax.rsqrt(jnp.mean(middle * middle, axis=1, keepdims=True) + EPSILON)
    unit = middle * inv
    b.ggain[1:2] = jnp.sum(gn * unit, axis=0, keepdims=True)
    a = gn * b.gain[1:2]
    gm = b.call[c].astype(F32) + inv * (a - unit * jnp.mean(a * unit, axis=1, keepdims=True))
    b.gmid[...] = gm
    gb = gm.astype(BF16)
    b.gb[c] = gb
    for k in (3, 1, 2, 0):
        i = plane(k)[0]
        b.gasend[i] = nt(gb, b.wout[i].reshape(hw, width)).astype(BF16)
        if k:
            swap(b.gasend, b.ga, s.x_s.at[2], s.x_r.at[2], k).start()
        else:
            b.ga[c] = b.gasend[c]
    reduce_side(*red0, 1)
    reduce_side(*red0, 2)
    sum_middle(GATE)

    def attend_back(k):
        i = plane(k)[0]
        if k:
            swap_recv(b.gasend, b.ga, s.x_s.at[2], s.x_r.at[2], k)
        blk = b.qkv[i]
        gab = b.ga[i]
        gq, gk, gv = [], [], []
        for h in range(heads):
            q = blk[:, h * HEAD : (h + 1) * HEAD]
            key = blk[:, hw + h * HEAD : hw + (h + 1) * HEAD]
            v = blk[:, 2 * hw + h * HEAD : 2 * hw + (h + 1) * HEAD]
            ga = gab[:, h * HEAD : (h + 1) * HEAD]
            p = b.probs[i, h]
            gp = nt(ga, v)
            gs = (p * (gp - jnp.sum(p * gp, axis=1, keepdims=True))).astype(BF16)
            gq.append(nn(gs, key) * scale)
            gk.append(tn(gs, q) * scale)
            gv.append(tn(p.astype(BF16), ga))
        b.gqkv[i] = jnp.concatenate(gq + gk + gv, axis=1).astype(BF16)
        b.p[2][i] = nt(b.gqkv[i], b.wcol[QKV].reshape(width, fw)).astype(BF16)

    attend_back(3)
    red_start(red2)
    relay_start(*gb_way)
    attend_back(1)
    reduce_side(*red2, 1)
    attend_back(2)
    reduce_side(*red2, 2)
    attend_back(0)
    col_grad(QKV, b.n1, b.gqkv)
    sum_middle(UP)
    sum_start(QKV)
    relay_pass(*gb_way)
    rows_out(od, sum_end(DOWN))

    res = b.middle[...] + red_sum(red0)
    b.lsend[...] = res.reshape(nd, per, width).astype(BF16)
    all_peers(lambda to: b.lsend.at[to], b.lrecv, s.l_s, s.l_r)
    b.lrecv[dp] = b.lsend[dp]

    gn = red_sum(red2)
    x = b.trecv[...].astype(F32).reshape(rows, width)
    inv = lax.rsqrt(jnp.mean(x * x, axis=1, keepdims=True) + EPSILON)
    unit = x * inv
    b.ggain[0:1] = jnp.sum(gn * unit, axis=0, keepdims=True)
    a = gn * b.gain[0:1]
    gx = b.gmid[...] + inv * (a - unit * jnp.mean(a * unit, axis=1, keepdims=True))
    b.isend[...] = gx.reshape(nd, per, width).astype(BF16)
    all_peers(lambda to: b.isend.at[to], b.irecv, s.i_s, s.i_r)
    b.irecv[dp] = b.isend[dp]
    b.hsend[...] = jnp.concatenate([tile_of(b.ggain[0:1]), tile_of(b.ggain[1:2])], axis=0)
    all_peers(lambda to: b.hsend, b.hrecv, s.h_s, s.h_r)
    b.hrecv[dp] = b.hsend[...]

    relay_done(*gb_way)
    gb_all = b.gb[...].reshape(toks, width)
    b.gout[...] = (
        tn(b.att[...].reshape(toks, hw), gb_all).reshape(zn, CORES, row_dev, width).astype(BF16)
    )
    presum(OUT, half_of(OUT), b.cout).start()
    sum_middle(QKV)
    sum_start(OUT)

    col_end(GATE)
    all_peers_recv(lambda at: b.lsend.at[at], b.lrecv, s.l_s, s.l_r)
    pick = b.pick[...]
    lout[...] = tn(pick, b.lrecv[...].reshape(rows, width)).astype(BF16)
    sum_middle(OUT)
    col_end(UP)
    all_peers_recv(lambda at: b.hsend, b.hrecv, s.h_s, s.h_r)
    b.hpart[f] = jnp.sum(b.hrecv[...], axis=0)
    hmirror = remote(b.hpart.at[f], b.hpart.at[f], s.hb_s, s.hb_r, sib)
    hmirror.start()
    all_peers_recv(lambda at: b.isend.at[at], b.irecv, s.i_s, s.i_r)
    igrad[...] = tn(pick, b.irecv[...].reshape(rows, width)).astype(BF16)
    remote(b.hpart.at[other], b.hpart.at[other], s.hb_s, s.hb_r, sib).wait_recv()
    gain_sum = b.hpart[0] + b.hpart[1]
    ogain1[...] = my_gain(gain_sum[:gw])
    ogain2[...] = my_gain(gain_sum[gw:])
    col_recv(GATE)
    hidden_out(og, GATE)
    col_end(QKV)
    col_recv(UP)
    hidden_out(ou, UP)
    rows_out(oo, sum_end(OUT))
    col_recv(QKV)
    heads_out(oq, 0)
    heads_out(ok, 1)
    heads_out(ov, 2)

    gmirror.wait_send()
    hmirror.wait_send()
    all_peers_sent(lambda to: gains, b.grecv, s.g_s, s.g_r)
    all_peers_sent(lambda to: b.tsend.at[to], b.trecv, s.t_s, s.t_r)
    all_peers_sent(lambda to: b.csend.at[to], b.crecv, s.c_s, s.c_r)
    all_peers_sent(lambda to: b.lsend.at[to], b.lrecv, s.l_s, s.l_r)
    all_peers_sent(lambda to: b.isend.at[to], b.irecv, s.i_s, s.i_r)
    all_peers_sent(lambda to: b.hsend, b.hrecv, s.h_s, s.h_r)
    gather_sent(b.mask, s.m_s, s.m_r)
    for k in range(TP):
        for way in (n1_way, call_way, n2_way, gb_way, out_way):
            relay(*way, k).wait_send()
    for src, dst, land, send, recv in (red0, red1, red2):
        for k in (3, 0):
            halves(src, land, send, recv, k).wait_send()
        for k in (1, 2):
            side(src, dst, send, recv, k).wait_send()
    for k in range(1, TP):
        swap(b.att, b.attall, s.x_s.at[0], s.x_r.at[0], k).wait_send()
        swap(b.gasend, b.ga, s.x_s.at[2], s.x_r.at[2], k).wait_send()
        out_mirror(k, f).wait_send()
        for piece in (QKV, GATE, UP):
            spread(piece, k).wait_send()
            home(piece, k).wait_send()
    for piece in (QKV, GATE, UP, OUT, DOWN):
        line_sent(piece)
        sum_sent(piece)


def _log2(n):
    return n.bit_length() - 1


def kernel_takes(dp_count, core_count, rows, width, hidden):
    pieces = dp_count * core_count
    zn = dp_count // TP
    return (
        core_count == CORES
        and dp_count % TP == 0
        and rows == 128
        and rows % dp_count == 0
        and rows // dp_count == 8
        and width == zn * 256
        and width // HEAD == dp_count
        and width // pieces == HEAD // CORES
        and hidden % pieces == 0
        and hidden // pieces <= PAD
        and PAD * CORES * zn % 256 == 0
        and zn == 4
    )


def planned(
    dp_count,
    tokens,
    dealing,
    lengths,
    norm1_gain,
    w_query,
    w_key,
    w_value,
    w_out,
    norm2_gain,
    w_gate,
    w_up,
    w_down,
    cotangent,
):
    nd = dp_count
    zn = nd // TP
    rows, width = tokens.shape
    pieces = nd * CORES
    row_dev = width // pieces
    hidden = w_gate.shape[0] * pieces // width
    unit = hidden // pieces
    hw = width // TP
    fw = PAD * CORES * zn
    gw = width // 128
    toks = TP * rows
    per = rows // nd
    V = pltpu.VMEM
    bufs = dict(
        pick=V((rows, rows), BF16),
        own=V((3, TP, row_dev, fw), BF16),
        gown=V((2 * gw, 128), BF16),
        flat=V((PAD * width // 128, 128), F32),
        pairs=V((fw // 128, row_dev, 128), F32),
        wide=V((TP, fw // 128, row_dev, 128), F32),
        tsend=V((nd, per, width), BF16),
        trecv=V((nd, per, width), BF16),
        csend=V((nd, per, width), BF16),
        crecv=V((nd, per, width), BF16),
        lsend=V((nd, per, width), BF16),
        lrecv=V((nd, per, width), BF16),
        isend=V((nd, per, width), BF16),
        irecv=V((nd, per, width), BF16),
        grecv=V((nd, 2 * gw, 128), BF16),
        gpart=V((CORES, 2 * gw, 128), BF16),
        gain=V((8, width), F32),
        ggain=V((8, width), F32),
        hsend=V((2 * gw, 128), F32),
        hrecv=V((nd, 2 * gw, 128), F32),
        hpart=V((CORES, 2 * gw, 128), F32),
        mask=V((TP, rows, rows), BF16),
        wcol=V((3, zn, TP, CORES, row_dev, fw), BF16),
        wout=V((TP, zn, CORES, row_dev, width), BF16),
        wdown=V((zn, CORES, PAD, width), BF16),
        n1=V((TP, rows, width), BF16),
        n2=V((TP, rows, width), BF16),
        call=V((TP, rows, width), BF16),
        gb=V((TP, rows, width), BF16),
        qkv=V((TP, rows, 3 * hw), BF16),
        probs=V((TP, hw // HEAD, rows, rows), F32),
        att=V((TP, rows, hw), BF16),
        attall=V((TP, rows, hw), BF16),
        gasend=V((TP, rows, hw), BF16),
        middle=V((rows, width), F32),
        gmid=V((rows, width), F32),
        gate=V((TP, rows, fw), F32),
        up=V((TP, rows, fw), F32),
        hid=V((TP, rows, fw), BF16),
        ggate=V((TP, rows, fw), BF16),
        gup=V((TP, rows, fw), BF16),
        ga=V((TP, rows, hw), BF16),
        gqkv=V((TP, rows, 3 * hw), BF16),
        gcol=V((3, zn, TP, CORES, row_dev, fw), BF16),
        ccol=V((3, zn, TP, row_dev, fw), BF16),
        scol=V((3, zn, TP, row_dev, fw), BF16),
        ecol=V((3, 4, TP, row_dev, fw), BF16),
        tcol=V((3, TP, row_dev, fw), BF16),
        rcol=V((3, TP, row_dev, fw), BF16),
        gout=V((zn, CORES, row_dev, width), BF16),
        cout=V((zn, row_dev, width), BF16),
        sout=V((zn, row_dev, width), BF16),
        eout=V((4, row_dev, width), BF16),
        gdown=V((zn, CORES, PAD, width), BF16),
        cdown=V((zn, PAD, width), BF16),
        sdown=V((zn, PAD, width), BF16),
        edown=V((4, PAD, width), BF16),
    )
    bufs.update(
        p=[V((TP, rows, width), BF16) for _ in range(3)],
        q=[V((2, rows, width), BF16) for _ in range(3)],
        land=V((3, 2, rows // 2, width), BF16),
    )
    S = pltpu.SemaphoreType.DMA
    each = S((nd,))
    sems = dict(
        g_s=each,
        g_r=each,
        t_s=each,
        t_r=each,
        c_s=each,
        c_r=each,
        l_s=each,
        l_r=each,
        i_s=each,
        i_r=each,
        h_s=each,
        h_r=each,
        gb_s=S(()),
        gb_r=S(()),
        hb_s=S(()),
        hb_r=S(()),
        m_s=S((TP,)),
        m_r=S((TP,)),
        s1_s=S((3, TP)),
        s1_r=S((3, TP)),
        z_s=S((5, 2 * zn)),
        z_r=S((5, zn)),
        b_s=S((5, zn)),
        b_r=S((5, zn)),
        a_s=S((4, TP)),
        a_r=S((4, TP)),
        o_s=S((TP,)),
        o_r=S((TP,)),
        om_s=S((TP,)),
        om_r=S((TP,)),
        x_s=S((5, TP)),
        x_r=S((5, TP)),
        p_s=S((5,)),
        p_r=S((5,)),
        e_s=S((5, 4)),
        e_r=S((5, 4)),
        h2_s=S((3, TP)),
        h2_r=S((3, TP)),
    )
    n_io = 13 + 11
    spaces, shape_of = jax.tree.flatten((bufs, sems))

    def entry(*refs):
        io, rest = refs[:n_io], refs[n_io:]
        b, s = jax.tree.unflatten(shape_of, rest)
        block_kernel((nd, zn, rows, width, hw, fw, unit), *io, SimpleNamespace(**b), SimpleNamespace(**s))

    vm = pl.BlockSpec(memory_space=pltpu.VMEM)
    sm = pl.BlockSpec(memory_space=pltpu.SMEM)
    head_span = jax.ShapeDtypeStruct((row_dev * width // 128, 128), F32)
    hidden_span = jax.ShapeDtypeStruct((unit * width // 128, 128), F32)
    gain_span = jax.ShapeDtypeStruct((1, row_dev), F32)
    row_block = jax.ShapeDtypeStruct((rows, width), BF16)

    def lanes(v):
        return v.reshape(-1, 128)

    outs = pl.pallas_call(
        entry,
        out_shape=(row_block, row_block, gain_span)
        + (head_span,) * 4
        + (gain_span,)
        + (hidden_span,) * 3,
        in_specs=[vm, vm, vm, sm] + [vm] * 9,
        out_specs=(vm,) * 11,
        scratch_shapes=spaces,
        compiler_params=pltpu.CompilerParams(
            collective_id=0, has_side_effects=True, vmem_limit_bytes=VMEM_BYTES
        ),
        name="block_fwd_bwd",
    )(
        tokens,
        cotangent,
        dealing.reshape(1, rows),
        lengths,
        norm1_gain.reshape(1, row_dev),
        norm2_gain.reshape(1, row_dev),
        lanes(w_query),
        lanes(w_key),
        lanes(w_value),
        lanes(w_out),
        lanes(w_gate),
        lanes(w_up),
        lanes(w_down),
    )
    whole = pl.BlockSpec(memory_space=pl.ANY)

    def hand_over(*refs):
        n = len(refs) // 2
        copies = [pltpu.make_async_copy(refs[i], refs[n + i], refs[-1].at[i]) for i in range(n)]
        for cp in copies:
            cp.start()
        for cp in copies:
            cp.wait()

    outs = pl.pallas_call(
        hand_over,
        out_shape=tuple(jax.ShapeDtypeStruct(v.shape, v.dtype) for v in outs),
        in_specs=[vm] * len(outs),
        out_specs=(whole,) * len(outs),
        scratch_shapes=[S((len(outs),))],
        name="hand_over",
    )(*outs)
    return tuple(outs[:2]) + tuple(v.reshape(-1) for v in outs[2:])


def dispatch(dp_count, core_count, *args):
    tokens, w_gate = args[0], args[9]
    rows, width = tokens.shape
    hidden = w_gate.shape[0] * dp_count * core_count // width
    if kernel_takes(dp_count, core_count, rows, width, hidden):
        return planned(dp_count, *args)
    return body(*args)


def solution(mesh):
    in_specs = (
        P(("dp", "fsdp"), None),
        P(("dp", "fsdp")),
        P(("dp", "fsdp"), None),
        P(("dp", "fsdp")),
        P(("dp", "fsdp")),
        P(("dp", "fsdp")),
        P(("dp", "fsdp")),
        P(("dp", "fsdp")),
        P(("dp", "fsdp")),
        P(("dp", "fsdp")),
        P(("dp", "fsdp")),
        P(("dp", "fsdp")),
        P(("dp", "fsdp"), None),
    )
    out_specs = (
        P(("dp", "fsdp"), None),
        P(("dp", "fsdp"), None),
        P(("dp", "fsdp")),
        P(("dp", "fsdp")),
        P(("dp", "fsdp")),
        P(("dp", "fsdp")),
        P(("dp", "fsdp")),
        P(("dp", "fsdp")),
        P(("dp", "fsdp")),
        P(("dp", "fsdp")),
        P(("dp", "fsdp")),
    )
    return jax.shard_map(
        functools.partial(dispatch, mesh.shape["dp"], mesh.shape["fsdp"]),
         mesh=mesh, in_specs=in_specs, out_specs=out_specs, check_vma=False)
```

```python
import functools
from types import SimpleNamespace

import jax
import jax.numpy as jnp
from jax import lax
from jax.experimental import pallas as pl
from jax.experimental.pallas import tpu as pltpu
from jax.sharding import PartitionSpec as P

HEAD = 64
WINDOW = 64


EPSILON = 1e-06


def unpack(flat_list, model_width):
    gain_one, query_w, key_w, value_w, out_w, gain_two, gate_w, up_w, down_w = flat_list
    hidden_units = gate_w.shape[0] // model_width
    return (
        gain_one.astype(jnp.float32),
        query_w.reshape(model_width, model_width),
        key_w.reshape(model_width, model_width),
        value_w.reshape(model_width, model_width),
        out_w.reshape(model_width, model_width),
        gain_two.astype(jnp.float32),
        gate_w.reshape(model_width, hidden_units),
        up_w.reshape(model_width, hidden_units),
        down_w.reshape(hidden_units, model_width),
    )


def normalize(values, gain_vec):
    inverse = lax.rsqrt(jnp.mean(values * values, axis=-1, keepdims=True) + EPSILON)
    unit_rows = values * inverse
    return (unit_rows * gain_vec, unit_rows, inverse)


def norm_back(upstream, gain_vec, unit_rows, inverse):
    scaled = upstream * gain_vec
    return inverse * (scaled - unit_rows * jnp.mean(scaled * unit_rows, axis=-1, keepdims=True))


def dot_rows(first_op, second_op):
    return lax.dot_general(
        first_op, second_op, (((0,), (0,)), ((), ())), preferred_element_type=jnp.float32
    )


def dot_back(first_op, second_op):
    return lax.dot_general(
        first_op, second_op, (((1,), (1,)), ((), ())), preferred_element_type=jnp.float32
    )


def flat_piece(entry, count, pieces):
    if entry[0] == "gain":
        vector = entry[1]
        share = vector.shape[0] // pieces
        return vector.reshape(count, share)
    left_op, right_op = (entry[1], entry[2])
    row_total = left_op.shape[1]
    col_total = right_op.shape[1]
    share = row_total * col_total // pieces
    block = dot_rows(left_op, right_op)
    flat = block.reshape(-1)
    return flat.reshape(count, share)


def term_maker(entries, pieces, count):
    return jnp.concatenate([flat_piece(entry, count, pieces) for entry in entries], axis=1)


def split_spans(summed, entries, pieces):
    flat = summed.reshape(-1)
    results = []
    offset = 0
    for entry in entries:
        if entry[0] == "gain":
            share = entry[1].shape[0] // pieces
        else:
            share = entry[1].shape[1] * entry[2].shape[1] // pieces
        results.append(flat[offset : offset + share])
        offset = offset + share
    return results


def block_mask(segment, tok_rows):
    block_count = tok_rows // WINDOW
    padded = jnp.concatenate([jnp.full((WINDOW,), -1, jnp.int32), segment])
    seg_query = segment.reshape(block_count, WINDOW)
    seg_keys = jnp.concatenate([padded[:-WINDOW].reshape(block_count, WINDOW), seg_query], axis=1)
    offset = jnp.arange(WINDOW)[:, None] - jnp.arange(2 * WINDOW)[None, :] + WINDOW
    inside = (offset >= 0) & (offset < WINDOW)
    return inside[None] & (seg_query[:, :, None] == seg_keys[:, None, :])


def key_blocks(values, block_count):
    padded = jnp.concatenate([jnp.zeros((WINDOW,) + values.shape[1:], values.dtype), values])
    previous = padded[:-WINDOW].reshape((block_count, WINDOW) + values.shape[1:])
    current = values.reshape((block_count, WINDOW) + values.shape[1:])
    return jnp.concatenate([previous, current], axis=1)


def fold_keys(key_parts, tok_rows, model_width):
    previous = key_parts[:, :WINDOW]
    current = key_parts[:, WINDOW:]
    shifted = jnp.concatenate([previous[1:], jnp.zeros_like(previous[:1])], axis=0)
    return (current + shifted).reshape(tok_rows, model_width)


def masked_scores(query_blk, key_blk, key_mask):
    scores = jnp.einsum(
        "bahd,bchd->bhac", query_blk, key_blk, preferred_element_type=jnp.float32
    ) * HEAD ** (-0.5)
    return jnp.where(key_mask, scores, -1e30)


def body(
    tokens,
    dealing,
    lengths,
    norm1_gain,
    w_query,
    w_key,
    w_value,
    w_out,
    norm2_gain,
    w_gate,
    w_up,
    w_down,
    cotangent,
):
    tok_rows, model_width = tokens.shape
    dp_count = lax.axis_size("dp")
    fsdp_count = lax.axis_size("fsdp")
    pieces = lax.axis_size(("dp", "fsdp"))
    per_peer = tok_rows // dp_count
    local_pos = dealing % tok_rows
    target_dp = dealing // tok_rows // fsdp_count
    send_slot = target_dp * per_peer + local_pos % per_peer
    sent_tokens = jnp.zeros_like(tokens).at[send_slot].set(tokens)
    sent_cot = jnp.zeros_like(cotangent).at[send_slot].set(cotangent)
    inputs, incoming = (
        lax.all_to_all(sent_tokens, "dp", split_axis=0, concat_axis=0, tiled=True),
        lax.all_to_all(sent_cot, "dp", split_axis=0, concat_axis=0, tiled=True),
    )
    bounds = jnp.cumsum(lengths[0])
    positions = jnp.arange(tok_rows, dtype=jnp.int32)
    segment = jnp.sum((positions[:, None] >= bounds[None, :]).astype(jnp.int32), axis=1)
    block_count = tok_rows // WINDOW
    head_count = model_width // HEAD
    key_mask = block_mask(segment, tok_rows)[:, None]
    flat_weights = (norm1_gain, w_query, w_key, w_value, w_out, norm2_gain, w_gate, w_up, w_down)
    gathered = (
        lax.all_gather(flat_weights[0], ("dp", "fsdp"), axis=0, tiled=True),
        lax.all_gather(flat_weights[1], ("dp", "fsdp"), axis=0, tiled=True),
        lax.all_gather(flat_weights[2], ("dp", "fsdp"), axis=0, tiled=True),
        lax.all_gather(flat_weights[3], ("dp", "fsdp"), axis=0, tiled=True),
        lax.all_gather(flat_weights[4], ("dp", "fsdp"), axis=0, tiled=True),
        lax.all_gather(flat_weights[5], ("dp", "fsdp"), axis=0, tiled=True),
        lax.all_gather(flat_weights[6], ("dp", "fsdp"), axis=0, tiled=True),
        lax.all_gather(flat_weights[7], ("dp", "fsdp"), axis=0, tiled=True),
        lax.all_gather(flat_weights[8], ("dp", "fsdp"), axis=0, tiled=True),
    )
    gain_one, query_w, key_w, value_w, out_w, gain_two, gate_w, up_w, down_w = unpack(
        gathered, model_width
    )
    input_f = inputs.astype(jnp.float32)
    scaled_one, unit_one, inverse_one = normalize(input_f, gain_one)
    normed_one = scaled_one.astype(jnp.bfloat16)
    query_act = jnp.dot(normed_one, query_w, preferred_element_type=jnp.float32).astype(
        jnp.bfloat16
    )
    key_act = jnp.dot(normed_one, key_w, preferred_element_type=jnp.float32).astype(jnp.bfloat16)
    value_act = jnp.dot(normed_one, value_w, preferred_element_type=jnp.float32).astype(
        jnp.bfloat16
    )
    query_blk = query_act.reshape(block_count, WINDOW, head_count, HEAD)
    key_blk = key_blocks(key_act.reshape(tok_rows, head_count, HEAD), block_count)
    value_blk = key_blocks(value_act.reshape(tok_rows, head_count, HEAD), block_count)
    scores = masked_scores(query_blk, key_blk, key_mask)
    row_peak = jnp.max(scores, axis=-1, keepdims=True)
    exp_scores = jnp.exp(scores - row_peak)
    row_total = jnp.sum(exp_scores, axis=-1, keepdims=True)
    log_total = row_peak + jnp.log(row_total)
    probs_low = (exp_scores / row_total).astype(jnp.bfloat16)
    attended = jnp.einsum(
        "bhac,bchd->bahd", probs_low, value_blk, preferred_element_type=jnp.float32
    )
    attended = attended.reshape(tok_rows, model_width).astype(jnp.bfloat16)
    middle = input_f + jnp.dot(attended, out_w, preferred_element_type=jnp.float32)
    scaled_two, unit_two, inverse_two = normalize(middle, gain_two)
    normed_two = scaled_two.astype(jnp.bfloat16)
    gate_pre = jnp.dot(normed_two, gate_w, preferred_element_type=jnp.float32)
    up_pre = jnp.dot(normed_two, up_w, preferred_element_type=jnp.float32)
    sigmoid_gate = jax.nn.sigmoid(gate_pre)
    gate_act = gate_pre * sigmoid_gate
    hidden = (gate_act * up_pre).astype(jnp.bfloat16)
    result = (middle + jnp.dot(hidden, down_w, preferred_element_type=jnp.float32)).astype(
        jnp.bfloat16
    )
    regathered = (
        lax.all_gather(flat_weights[0], ("dp", "fsdp"), axis=0, tiled=True),
        lax.all_gather(flat_weights[1], ("dp", "fsdp"), axis=0, tiled=True),
        lax.all_gather(flat_weights[2], ("dp", "fsdp"), axis=0, tiled=True),
        lax.all_gather(flat_weights[3], ("dp", "fsdp"), axis=0, tiled=True),
        lax.all_gather(flat_weights[4], ("dp", "fsdp"), axis=0, tiled=True),
        lax.all_gather(flat_weights[5], ("dp", "fsdp"), axis=0, tiled=True),
        lax.all_gather(flat_weights[6], ("dp", "fsdp"), axis=0, tiled=True),
        lax.all_gather(flat_weights[7], ("dp", "fsdp"), axis=0, tiled=True),
        lax.all_gather(flat_weights[8], ("dp", "fsdp"), axis=0, tiled=True),
    )
    gain_one, query_w, key_w, value_w, out_w, gain_two, gate_w, up_w, down_w = unpack(
        regathered, model_width
    )
    grad_hidden = dot_back(incoming, down_w)
    grad_gate = (
        grad_hidden * up_pre * sigmoid_gate * (1.0 + gate_pre * (1.0 - sigmoid_gate))
    ).astype(jnp.bfloat16)
    grad_up = (grad_hidden * gate_act).astype(jnp.bfloat16)
    grad_normed_two = dot_back(grad_gate, gate_w) + dot_back(grad_up, up_w)
    grad_gain_two = jnp.sum(grad_normed_two * unit_two, axis=0)
    grad_middle = incoming.astype(jnp.float32) + norm_back(
        grad_normed_two, gain_two, unit_two, inverse_two
    )
    ff_entries = [
        ("gain", grad_gain_two),
        ("mat", normed_two, grad_gate),
        ("mat", normed_two, grad_up),
        ("mat", hidden, incoming),
    ]
    grad_branch = grad_middle.astype(jnp.bfloat16)
    grad_attended = dot_back(grad_branch, out_w).astype(jnp.bfloat16)
    grad_att_blk = grad_attended.reshape(block_count, WINDOW, head_count, HEAD)
    probs = jnp.exp(masked_scores(query_blk, key_blk, key_mask) - log_total)
    grad_probs = jnp.einsum(
        "bahd,bchd->bhac", grad_att_blk, value_blk, preferred_element_type=jnp.float32
    )
    grad_scores = (
        probs * (grad_probs - jnp.sum(grad_probs * probs, axis=-1, keepdims=True))
    ).astype(jnp.bfloat16)
    grad_query = jnp.einsum(
        "bhac,bchd->bahd", grad_scores, key_blk, preferred_element_type=jnp.float32
    ) * HEAD ** (-0.5)
    grad_query = grad_query.reshape(tok_rows, model_width).astype(jnp.bfloat16)
    key_parts = jnp.einsum(
        "bhac,bahd->bchd", grad_scores, query_blk, preferred_element_type=jnp.float32
    ) * HEAD ** (-0.5)
    grad_key = fold_keys(key_parts, tok_rows, model_width).astype(jnp.bfloat16)
    value_parts = jnp.einsum(
        "bhac,bahd->bchd", probs_low, grad_att_blk, preferred_element_type=jnp.float32
    )
    grad_value = fold_keys(value_parts, tok_rows, model_width).astype(jnp.bfloat16)
    grad_normed_one = (
        dot_back(grad_query, query_w) + dot_back(grad_key, key_w) + dot_back(grad_value, value_w)
    )
    grad_gain_one = jnp.sum(grad_normed_one * unit_one, axis=0)
    grad_dealt = (grad_middle + norm_back(grad_normed_one, gain_one, unit_one, inverse_one)).astype(
        jnp.bfloat16
    )
    returned_out, returned_grad = (
        lax.all_to_all(result, "dp", split_axis=0, concat_axis=0, tiled=True),
        lax.all_to_all(grad_dealt, "dp", split_axis=0, concat_axis=0, tiled=True),
    )
    layer_out = returned_out[send_slot]
    input_grad = returned_grad[send_slot]
    attn_entries = [
        ("gain", grad_gain_one),
        ("mat", normed_one, grad_query),
        ("mat", normed_one, grad_key),
        ("mat", normed_one, grad_value),
        ("mat", attended, grad_branch),
    ]
    every_entry = attn_entries + ff_entries
    all_summed = lax.psum_scatter(
        term_maker(every_entry, pieces, lax.axis_size(("dp", "fsdp")) * 1),
        ("dp", "fsdp"),
        scatter_dimension=0,
        tiled=True,
    )
    all_spans = split_spans(all_summed, every_entry, pieces)
    (
        span_gain_one,
        span_query,
        span_key,
        span_value,
        span_out,
        span_gain_two,
        span_gate,
        span_up,
        span_down,
    ) = all_spans
    return (
        layer_out,
        input_grad,
        span_gain_one,
        span_query,
        span_key,
        span_value,
        span_out,
        span_gain_two,
        span_gate,
        span_up,
        span_down,
    )


MESH = pl.DeviceIdType.MESH
TP = 4
CORES = 2
PAD = 96
VMEM_BYTES = 62 * 2**20

QKV, GATE, UP, OUT, DOWN = range(5)
F32 = jnp.float32
BF16 = jnp.bfloat16


def remote(src, dst, send, recv, device):
    return pltpu.make_async_remote_copy(
        src_ref=src, dst_ref=dst, send_sem=send, recv_sem=recv, device_id=device, device_id_type=MESH
    )


def nn(a, b):
    return lax.dot_general(a, b, (((1,), (0,)), ((), ())), preferred_element_type=F32)


def nt(a, b):
    return lax.dot_general(a, b, (((1,), (1,)), ((), ())), preferred_element_type=F32)


def tn(a, b):
    return lax.dot_general(a, b, (((0,), (0,)), ((), ())), preferred_element_type=F32)


def row_of(tile):
    return jnp.concatenate([tile[k : k + 1] for k in range(tile.shape[0])], axis=1)


def tile_of(row):
    return jnp.concatenate(
        [row[:, k * 128 : (k + 1) * 128] for k in range(row.shape[1] // 128)], axis=0
    )


def block_kernel(
    sizes,
    tok,
    cot,
    deal,
    lens,
    gain1,
    gain2,
    wq,
    wk,
    wv,
    wo,
    wg,
    wu,
    wd,
    lout,
    igrad,
    ogain1,
    oq,
    ok,
    ov,
    oo,
    ogain2,
    og,
    ou,
    od,
    b,
    s,
):
    nd, zn, rows, width, hw, fw, share = sizes
    scol = b.own
    gains = b.gown
    heads = hw // HEAD
    toks = TP * rows
    per = rows // nd
    dp = lax.axis_index("dp")
    f = lax.axis_index("fsdp")
    other = 1 - f
    z = dp // TP
    c = dp % TP
    sib = (dp, other)
    row_dev = width // (nd * CORES)

    barrier = pltpu.get_barrier_semaphore()
    pl.semaphore_signal(barrier, inc=1, device_id=sib, device_id_type=MESH)

    @pl.loop(1, nd)
    def _(k):
        pl.semaphore_signal(
            barrier, inc=1, device_id=(lax.rem(dp + k, nd), f), device_id_type=MESH
        )

    me = dp * CORES + f
    chunks = share * CORES * TP * zn // 64
    lane = lax.broadcasted_iota(jnp.int32, (1, 128), 1)

    def turned(v, by):
        return pltpu.roll(v, by % 128, 1) if by % 128 else v

    def heads_in(w, t):
        n = w.shape[0]
        b.flat[:n] = w[...].astype(F32)
        per_row = width // 128
        cols = [b.flat[pl.ds(j, row_dev, stride=per_row), :] for j in range(per_row)]
        for cc in range(TP):
            for u in range(hw // 128):
                left, right = cols[4 * u + cc // 2], cols[4 * u + 2 + cc // 2]
                tile = jnp.where(
                    lane < HEAD, turned(left, HEAD * (cc % 2)), turned(right, HEAD * (1 - cc % 2))
                )
                at = t * hw + u * 128
                scol[QKV, cc, :, at : at + 128] = tile.astype(BF16)

    def heads_out(o, t):
        per_row = width // 128
        for j in range(per_row):
            cc, h = 2 * (j % 2), j // 2
            at = t * hw + (h // 2) * 128
            left = b.rcol[QKV, cc, :, at : at + 128].astype(F32)
            right = b.rcol[QKV, cc + 1, :, at : at + 128].astype(F32)
            tile = jnp.where(
                lane < HEAD, turned(left, HEAD * (h % 2)), turned(right, HEAD * (1 - h % 2))
            )
            o[pl.ds(j, row_dev, stride=per_row), :] = tile

    def spans(cc, odd):
        total = share * CORES * TP * zn
        for k in range(CORES * zn):
            src = total * odd + share * (CORES * TP * (k // CORES) + CORES * cc + k % CORES)
            dst, left = PAD * k, share
            while left:
                n = min(left, 128 - src % 128, 128 - dst % 128)
                yield src, dst, n
                src, dst, left = src + n, dst + n, left - n

    def hidden_in(w, piece):
        n = w.shape[0]
        b.flat[:n] = w[...].astype(F32)
        for cc in range(TP):
            for odd in range(2):
                tiles_of = [jnp.zeros((row_dev // 2, 128), F32) for _ in range(fw // 128)]
                for src, dst, ln in spans(cc, odd):
                    v = b.flat[pl.ds(src // 128, row_dev // 2, stride=chunks), :]
                    at = dst % 128
                    keep = (lane >= at) & (lane < at + ln)
                    tiles_of[dst // 128] = jnp.where(
                        keep, turned(v, dst - src), tiles_of[dst // 128]
                    )
                for u, v in enumerate(tiles_of):
                    b.pairs[u, pl.ds(odd, row_dev // 2, stride=2), :] = v
            for u in range(fw // 128):
                scol[piece, cc, :, u * 128 : (u + 1) * 128] = b.pairs[u].astype(BF16)

    def hidden_out(o, piece):
        todo = [[] for _ in range(chunks)]
        for cc in range(TP):
            for u in range(fw // 128):
                b.wide[cc, u] = b.rcol[piece, cc, :, u * 128 : (u + 1) * 128].astype(F32)
            for odd in range(2):
                for src, dst, ln in spans(cc, odd):
                    todo[src // 128].append((src, dst, ln, cc, odd))
        for j in range(chunks):
            tile = jnp.zeros((row_dev // 2, 128), F32)
            for src, dst, ln, cc, odd in todo[j]:
                v = b.wide[cc, dst // 128, pl.ds(odd, row_dev // 2, stride=2), :]
                at = src % 128
                keep = (lane >= at) & (lane < at + ln)
                tile = jnp.where(keep, turned(v, src - dst), tile)
            o[pl.ds(j, row_dev // 2, stride=chunks), :] = tile

    def rows_in(w, out, n):
        count = w.shape[0]
        per_row = width // 128
        b.flat[:count] = w[...].astype(F32)
        if count < n * per_row:
            b.flat[count : n * per_row] = jnp.zeros((n * per_row - count, 128), F32)
        for j in range(per_row):
            out[:, j * 128 : (j + 1) * 128] = b.flat[pl.ds(j, n, stride=per_row), :].astype(BF16)

    def rows_out(o, v):
        per_row = width // 128
        n = o.shape[0] // per_row
        for j in range(per_row):
            o[pl.ds(j, n, stride=per_row), :] = v[:n, j * 128 : (j + 1) * 128]

    def all_peers(src, dst, send, recv, start=True):
        @pl.loop(1, nd)
        def _(k):
            to = lax.rem(dp + k, nd)
            remote(src(to), dst.at[dp], send.at[k], recv.at[k], (to, f)).start()

    def all_peers_recv(src, dst, send, recv):
        @pl.loop(1, nd)
        def _(k):
            at = lax.rem(dp + (nd - k), nd)
            remote(src(at), dst.at[at], send.at[k], recv.at[k], (at, f)).wait_recv()

    def all_peers_sent(src, dst, send, recv):
        @pl.loop(1, nd)
        def _(k):
            to = lax.rem(dp + k, nd)
            remote(src(to), dst.at[dp], send.at[k], recv.at[k], (to, f)).wait_send()

    cx = c % 2
    cy = c // 2

    def plane(k):
        xx = 1 - cx if k % 2 else cx
        yy = 1 - cy if k // 2 else cy
        cc = yy * 2 + xx
        return cc, (z * TP + cc, f)

    def gather_start(buf, send, recv):
        for k in range(1, TP):
            _, dev = plane(k)
            remote(buf.at[c], buf.at[c], send.at[k], recv.at[k], dev).start()

    def gather_recv(buf, send, recv):
        for k in range(1, TP):
            cc, dev = plane(k)
            remote(buf.at[c], buf.at[cc], send.at[k], recv.at[k], dev).wait_recv()

    def gather_sent(buf, send, recv):
        for k in range(1, TP):
            _, dev = plane(k)
            remote(buf.at[c], buf.at[c], send.at[k], recv.at[k], dev).wait_send()

    tiles = 4
    tw = width // tiles

    def swap(src, dst, send, recv, k):
        cc, dev = plane(k)
        return remote(src.at[cc], dst.at[c], send.at[k], recv.at[k], dev)

    def swap_recv(src, dst, send, recv, k):
        cc, dev = plane(k)
        remote(src.at[cc], dst.at[cc], send.at[k], recv.at[k], dev).wait_recv()

    half = rows // 2
    low, high = pl.ds(0, half), pl.ds(half, half)

    def rows_part(buf):
        def get(at, part):
            return buf.at[at] if part is None else buf.at[at, (low, high)[part]]

        return get

    def relay_refs(get, send, recv, k, at):
        ref = get(at, (1, None, None, 0)[k])
        return remote(ref, ref, send.at[k], recv.at[k], plane((1, 1, 2, 2)[k])[1])

    def relay(get, send, recv, k):
        return relay_refs(get, send, recv, k, (plane(2)[0], c, c, plane(1)[0])[k])

    def relay_wait(get, send, recv, k):
        relay_refs(get, send, recv, k, plane((3, 1, 2, 3)[k])[0]).wait_recv()

    def relay_start(get, send, recv):
        relay(get, send, recv, 1).start()
        relay(get, send, recv, 2).start()

    def relay_pass(get, send, recv):
        relay_wait(get, send, recv, 1)
        relay(get, send, recv, 3).start()
        relay_wait(get, send, recv, 2)
        relay(get, send, recv, 0).start()

    def relay_done(get, send, recv):
        relay_wait(get, send, recv, 3)
        relay_wait(get, send, recv, 0)

    def halves(src, land, send, recv, k):
        at = plane(3)[0]
        part = src.at[at, low] if k else src.at[at, high]
        return remote(part, land.at[k // 3], send.at[k], recv.at[k], plane(1 if k else 2)[1])

    def side(src, dst, send, recv, k):
        cc, dev = plane(k)
        return remote(src.at[cc], dst.at[k - 1], send.at[k], recv.at[k], dev)

    def reduce_start(src, land, send, recv):
        halves(src, land, send, recv, 3).start()
        halves(src, land, send, recv, 0).start()

    def reduce_side(src, dst, land, send, recv, k):
        cc = plane(k)[0]
        if k == 1:
            halves(src, land, send, recv, 0).wait_recv()
            src[cc, half:] = (src[cc, half:].astype(F32) + land[0].astype(F32)).astype(BF16)
        else:
            halves(src, land, send, recv, 3).wait_recv()
            src[cc, :half] = (src[cc, :half].astype(F32) + land[1].astype(F32)).astype(BF16)
        side(src, dst, send, recv, k).start()

    def reduce_sum(src, dst, send, recv):
        total = src[c].astype(F32)
        for k in (1, 2):
            side(src, dst, send, recv, k).wait_recv()
            total = total + dst[k - 1].astype(F32)
        return total

    def block(piece, at, core):
        if piece == OUT:
            return b.wout.at[c, at, core]
        if piece == DOWN:
            return b.wdown.at[at, core]
        return b.wcol.at[piece, at, :, core]

    def hop(piece, at, slot, to):
        return remote(
            block(piece, at, f),
            block(piece, at, f),
            s.z_s.at[piece, slot],
            s.z_r.at[piece, at],
            (to * TP + c, f),
        )

    def mirror(piece, at, core):
        return remote(
            block(piece, at, core),
            block(piece, at, core),
            s.b_s.at[piece, at],
            s.b_r.at[piece, at],
            sib,
        )

    own_hops = ((1, 0), (-1, 1), (2, 2), (-2, 3))

    def reaches(by):
        return z + by < zn if by > 0 else z + by >= 0

    def line_start(piece):
        for by, slot in own_hops:

            @pl.when(reaches(by))
            def _():
                hop(piece, z, slot, z + by).start()

        mirror(piece, z, f).start()

    def line_pass(piece):
        for at_z, at, slot, to in ((zn - 2, 0, 4, zn - 1), (1, zn - 1, 5, 0)):

            @pl.when(z == at_z)
            def _():
                hop(piece, at, slot, z).wait_recv()
                hop(piece, at, slot, to).start()

    def line_take(piece):
        for d in range(1, zn):
            for by, passer in ((-d, zn - 2), (d, 1)):

                @pl.when(reaches(by) & ((z != passer) if d == zn - 2 else True))
                def _():
                    hop(piece, z + by, 0, z).wait_recv()

                @pl.when(reaches(by))
                def _():
                    mirror(piece, z + by, f).start()

    def line_done(piece):
        for at in range(zn):
            mirror(piece, at, other).wait_recv()

    def line_sent(piece):
        for by, slot in own_hops:

            @pl.when(reaches(by))
            def _():
                hop(piece, z, slot, z + by).wait_send()

        for at_z, at, slot, to in ((zn - 2, 0, 4, zn - 1), (1, zn - 1, 5, 0)):

            @pl.when(z == at_z)
            def _():
                hop(piece, at, slot, to).wait_send()

        for at in range(zn):
            mirror(piece, at, f).wait_send()

    def spread(piece, k):
        cc, dev = plane(k)
        return remote(
            scol.at[piece, cc],
            b.wcol.at[piece, z, c, f],
            s.s1_s.at[piece, k],
            s.s1_r.at[piece, k],
            dev,
        )

    def spread_recv(piece):
        for k in range(1, TP):
            cc, dev = plane(k)
            remote(
                scol.at[piece, cc],
                b.wcol.at[piece, z, cc, f],
                s.s1_s.at[piece, k],
                s.s1_r.at[piece, k],
                dev,
            ).wait_recv()

    slot = ((deal[...] >> _log2(rows * CORES)) * per) + (deal[...] & (per - 1))
    pick = (lax.broadcasted_iota(jnp.int32, (rows, rows), 0) == slot).astype(BF16)
    b.pick[...] = pick
    b.tsend[...] = nn(pick, tok[...]).reshape(nd, per, width).astype(BF16)
    b.csend[...] = nn(pick, cot[...]).reshape(nd, per, width).astype(BF16)

    gw = width // 128
    heads_in(wq, 0)
    heads_in(wk, 1)
    heads_in(wv, 2)
    spot = lax.broadcasted_iota(jnp.int32, (gw, 128), 0) == (me * row_dev) // 128
    spot = spot & ((lane // row_dev) == me % (128 // row_dev))

    def gain_tile(gain):
        g = gain[...].astype(F32)
        return jnp.where(spot, jnp.concatenate([g] * (128 // row_dev), axis=1), 0.0)

    gains[...] = jnp.concatenate([gain_tile(gain1), gain_tile(gain2)], axis=0).astype(BF16)
    pl.semaphore_wait(barrier, nd)

    all_peers(lambda to: gains, b.grecv, s.g_s, s.g_r)
    all_peers(lambda to: b.tsend.at[to], b.trecv, s.t_s, s.t_r)
    for k in range(1, TP):
        spread(QKV, k).start()
    b.wcol[QKV, z, c, f] = scol[QKV, c]
    b.trecv[dp] = b.tsend[dp]
    b.crecv[dp] = b.csend[dp]
    b.grecv[dp] = gains[...]
    ri = lax.broadcasted_iota(jnp.int32, (rows, rows), 0)
    ci = lax.broadcasted_iota(jnp.int32, (rows, rows), 1)
    seg_r = jnp.zeros((rows, rows), jnp.int32)
    seg_c = jnp.zeros((rows, rows), jnp.int32)
    bound = jnp.int32(0)
    for k in range(lens.shape[1]):
        bound = bound + lens[0, k]
        seg_r = seg_r + (ri >= bound).astype(jnp.int32)
        seg_c = seg_c + (ci >= bound).astype(jnp.int32)
    allowed = (seg_r == seg_c) & (ri >= ci) & (ri - ci < WINDOW)
    b.mask[c] = allowed.astype(F32).astype(BF16)
    gather_start(b.mask, s.m_s, s.m_r)
    rows_in(wo, b.wout.at[c, z, f], row_dev)

    all_peers_recv(lambda at: gains, b.grecv, s.g_s, s.g_r)
    gain_sum = jnp.sum(b.grecv[...].astype(F32), axis=0)
    b.gpart[f] = gain_sum.astype(BF16)
    gmirror = remote(b.gpart.at[f], b.gpart.at[f], s.gb_s, s.gb_r, sib)
    gmirror.start()

    spread_recv(QKV)
    line_start(QKV)
    line_start(OUT)
    for piece, w in ((GATE, wg), (UP, wu)):
        hidden_in(w, piece)
        for k in range(1, TP):
            spread(piece, k).start()
        b.wcol[piece, z, c, f] = scol[piece, c]
    rows_in(wd, b.wdown.at[z, f], PAD)

    all_peers_recv(lambda at: b.tsend.at[at], b.trecv, s.t_s, s.t_r)
    all_peers(lambda to: b.csend.at[to], b.crecv, s.c_s, s.c_r)
    remote(b.gpart.at[other], b.gpart.at[other], s.gb_s, s.gb_r, sib).wait_recv()
    gain_tile = b.gpart[0].astype(F32) + b.gpart[1].astype(F32)
    b.gain[0:1] = row_of(gain_tile[0:gw])
    b.gain[1:2] = row_of(gain_tile[gw : 2 * gw])

    x = b.trecv[...].astype(F32).reshape(rows, width)
    unit = x * lax.rsqrt(jnp.mean(x * x, axis=1, keepdims=True) + EPSILON)
    b.n1[c] = (unit * b.gain[0:1]).astype(BF16)
    n1_way = (rows_part(b.n1), s.a_s.at[0], s.a_r.at[0])
    call_way = (rows_part(b.call), s.a_s.at[1], s.a_r.at[1])
    n2_way = (rows_part(b.n2), s.a_s.at[2], s.a_r.at[2])
    gb_way = (rows_part(b.gb), s.a_s.at[3], s.a_r.at[3])
    relay_start(*n1_way)
    line_pass(QKV)
    spread_recv(GATE)
    line_start(GATE)
    relay_pass(*n1_way)
    spread_recv(UP)
    line_pass(OUT)
    line_take(QKV)
    gather_recv(b.mask, s.m_s, s.m_r)
    line_start(UP)
    line_done(QKV)
    scale = HEAD ** (-0.5)

    def out_part(at, part):
        return b.wout.at[at, :, f] if part is None else b.wout.at[at, pl.ds(part * (zn // 2), zn // 2), f]

    out_way = (out_part, s.o_s, s.o_r)

    def out_mirror(k, core):
        rows_of = b.wout.at[plane(k)[0], :, core]
        return remote(rows_of, rows_of, s.om_s.at[k], s.om_r.at[k], sib)

    def attend(k):
        i = plane(k)[0]
        if k == 3:
            relay_done(*n1_way)
        w = b.wcol[QKV].reshape(width, fw)
        b.qkv[i] = nn(b.n1[i], w).astype(BF16)
        blk = b.qkv[i]
        allow = b.mask[i].astype(F32) > 0.5
        outs = []
        for h in range(heads):
            q = blk[:, h * HEAD : (h + 1) * HEAD]
            key = blk[:, hw + h * HEAD : hw + (h + 1) * HEAD]
            v = blk[:, 2 * hw + h * HEAD : 2 * hw + (h + 1) * HEAD]
            scores = jnp.where(allow, nt(q, key) * scale, -1e30)
            e = jnp.exp(scores - jnp.max(scores, axis=1, keepdims=True))
            p = e / jnp.sum(e, axis=1, keepdims=True)
            b.probs[i, h] = p
            outs.append(nn(p.astype(BF16), v))
        b.att[i] = jnp.concatenate(outs, axis=1).astype(BF16)
        if k:
            swap(b.att, b.attall, s.x_s.at[0], s.x_r.at[0], k).start()
        else:
            b.attall[c] = b.att[c]

    attend(1)
    line_take(OUT)
    relay_start(*out_way)
    attend(2)
    attend(3)
    line_pass(GATE)
    attend(0)
    line_start(DOWN)
    relay_pass(*out_way)
    all_peers_recv(lambda at: b.csend.at[at], b.crecv, s.c_s, s.c_r)
    b.call[c] = b.crecv[...].reshape(rows, width)
    for k in (1, 2):
        out_mirror(k, f).start()
    line_done(OUT)
    line_pass(UP)
    relay_done(*out_way)
    out_mirror(3, f).start()
    for k in range(1, TP):
        swap_recv(b.att, b.attall, s.x_s.at[0], s.x_r.at[0], k)
        out_mirror(k, other).wait_recv()
    middle = b.trecv[...].astype(F32).reshape(rows, width)
    for i in range(TP):
        middle = middle + nn(b.attall[i], b.wout[i].reshape(hw, width))
    b.middle[...] = middle
    unit = middle * lax.rsqrt(jnp.mean(middle * middle, axis=1, keepdims=True) + EPSILON)
    b.n2[c] = (unit * b.gain[1:2]).astype(BF16)
    relay_start(*n2_way)
    line_take(GATE)
    relay_pass(*n2_way)
    relay_start(*call_way)
    line_take(UP)
    line_done(GATE)
    line_done(UP)

    def feed(k):
        i = plane(k)[0]
        if k == 3:
            relay_done(*n2_way)
        gate = nn(b.n2[i], b.wcol[GATE].reshape(width, fw))
        up = nn(b.n2[i], b.wcol[UP].reshape(width, fw))
        b.gate[i] = gate
        b.up[i] = up
        b.hid[i] = (gate * jax.nn.sigmoid(gate) * up).astype(BF16)

    feed(0)
    feed(1)
    feed(2)
    relay_pass(*call_way)
    feed(3)
    line_pass(DOWN)

    def presum(piece, src, dst):
        return remote(src, dst, s.p_s.at[piece], s.p_r.at[piece], sib)

    def part_of(piece):
        if piece == OUT:
            return b.gout.at[:, f], b.cout, b.sout, b.eout
        if piece == DOWN:
            return b.gdown.at[:, f], b.cdown, b.sdown, b.edown
        return b.gcol.at[piece, :, :, f], b.ccol.at[piece], b.scol.at[piece], b.ecol.at[piece]

    def half_of(piece):
        if piece == OUT:
            return b.gout.at[:, other]
        if piece == DOWN:
            return b.gdown.at[:, other]
        return b.gcol.at[piece, :, :, other]

    edge = (z == 0) | (z == zn - 1)

    def travel(piece, at, slot, send, to):
        _, _, part, land = part_of(piece)
        return remote(
            part.at[at], land.at[slot], s.e_s.at[piece, send], s.e_r.at[piece, slot], (to * TP + c, f)
        )

    inner = 1 + z // (zn - 1)
    end = (z - 1) * (zn - 1)

    def edge_send(piece, k):
        at, slot = ((zn - 1 - z, 3), (zn - 1 - inner, 2), (inner, 0))[k]
        return travel(piece, at, slot, slot, inner)

    def inner_send(piece, k):
        to, slot = ((end, 0), (zn - 1 - end, 1), (zn - 1 - z, 1))[k]
        return travel(piece, to, slot, k, to)

    def sum_start(piece):
        mine, came, part, _ = part_of(piece)
        presum(piece, half_of(piece), came).wait_recv()

        @pl.loop(0, zn)
        def _(j):
            part[j] = (mine[j].astype(F32) + came[j].astype(F32)).astype(BF16)

        @pl.when(edge)
        def _():
            for k in range(3):
                edge_send(piece, k).start()

        @pl.when(jnp.logical_not(edge))
        def _():
            inner_send(piece, 0).start()

    def sum_middle(piece):
        _, _, part, land = part_of(piece)

        @pl.when(jnp.logical_not(edge))
        def _():
            for k, slot, at in ((1, 3, zn - 1 - end), (2, 2, zn - 1 - z)):
                travel(piece, at, slot, slot, z).wait_recv()
                part[at] = (part[at].astype(F32) + land[slot].astype(F32)).astype(BF16)
                inner_send(piece, k).start()

    def sum_end(piece):
        _, _, part, land = part_of(piece)
        for slot in (0, 1):
            travel(piece, z, slot, slot, z).wait_recv()
        return part[z].astype(F32) + land[0].astype(F32) + land[1].astype(F32)

    def sum_sent(piece):
        @pl.when(edge)
        def _():
            for k in range(3):
                edge_send(piece, k).wait_send()

        @pl.when(jnp.logical_not(edge))
        def _():
            for k in range(3):
                inner_send(piece, k).wait_send()

        presum(piece, half_of(piece), part_of(piece)[1]).wait_send()

    def col_grad(piece, act, grad):
        @pl.loop(0, zn)
        def _(j):
            a = act[:, :, pl.ds(pl.multiple_of(j * tw, tw), tw)].reshape(toks, tw)
            g = tn(a, grad[...].reshape(toks, fw))
            b.gcol[piece, j] = g.reshape(TP, CORES, row_dev, fw).astype(BF16)

        presum(piece, half_of(piece), b.ccol.at[piece]).start()

    def home(piece, k):
        cc, dev = plane(k)
        return remote(
            b.tcol.at[piece, cc], b.rcol.at[piece, c], s.h2_s.at[piece, k], s.h2_r.at[piece, k], dev
        )

    def col_end(piece):
        b.tcol[piece] = sum_end(piece).astype(BF16)
        for k in range(1, TP):
            home(piece, k).start()
        b.rcol[piece, c] = b.tcol[piece, c]

    def my_gain(tile):
        row = jnp.sum(jnp.where(spot, tile, 0.0), axis=0, keepdims=True)
        total = row[:, :row_dev]
        for k in range(1, 128 // row_dev):
            total = total + row[:, k * row_dev : (k + 1) * row_dev]
        return total

    def col_recv(piece):
        for k in range(1, TP):
            cc, dev = plane(k)
            remote(
                b.tcol.at[piece, cc], b.rcol.at[piece, cc], s.h2_s.at[piece, k], s.h2_r.at[piece, k], dev
            ).wait_recv()

    relay_done(*call_way)
    call = b.call[...].reshape(toks, width)
    span = 4 * PAD
    for j in range(fw // span):
        w = tn(b.hid[:, :, j * span : (j + 1) * span].reshape(toks, span), call)
        b.gdown[2 * j : 2 * j + 2] = w.reshape(2, CORES, PAD, width).astype(BF16)
    presum(DOWN, half_of(DOWN), b.cdown).start()
    sum_start(DOWN)
    line_take(DOWN)
    line_done(DOWN)

    def feed_back(k):
        i = plane(k)[0]
        gh = nt(b.call[i], b.wdown[...].reshape(fw, width))
        gate = b.gate[i]
        sg = jax.nn.sigmoid(gate)
        b.ggate[i] = (gh * b.up[i] * sg * (1.0 + gate * (1.0 - sg))).astype(BF16)
        b.gup[i] = (gh * gate * sg).astype(BF16)
        v = nt(b.ggate[i], b.wcol[GATE].reshape(width, fw))
        v = v + nt(b.gup[i], b.wcol[UP].reshape(width, fw))
        b.p[1][i] = v.astype(BF16)

    red1 = (b.p[1], b.q[1], b.land.at[1], s.x_s.at[1], s.x_r.at[1])
    red0 = (b.p[0], b.q[0], b.land.at[0], s.x_s.at[3], s.x_r.at[3])
    red2 = (b.p[2], b.q[2], b.land.at[2], s.x_s.at[4], s.x_r.at[4])

    def red_start(red):
        reduce_start(red[0], red[2], red[3], red[4])

    def red_sum(red):
        return reduce_sum(red[0], red[1], red[3], red[4])

    feed_back(3)
    red_start(red1)
    feed_back(1)
    reduce_side(*red1, 1)
    feed_back(2)
    reduce_side(*red1, 2)
    feed_back(0)
    col_grad(GATE, b.n2, b.ggate)
    sum_middle(DOWN)
    col_grad(UP, b.n2, b.gup)
    sum_start(GATE)

    def feed_out(k):
        i = plane(k)[0]
        b.p[0][i] = nn(b.hid[i], b.wdown[...].reshape(fw, width)).astype(BF16)

    for k in (3, 1, 2, 0):
        feed_out(k)
    sum_start(UP)

    gn = red_sum(red1)
    red_start(red0)
    middle = b.middle[...]
    inv = lax.rsqrt(jnp.mean(middle * middle, axis=1, keepdims=True) + EPSILON)
    unit = middle * inv
    b.ggain[1:2] = jnp.sum(gn * unit, axis=0, keepdims=True)
    a = gn * b.gain[1:2]
    gm = b.call[c].astype(F32) + inv * (a - unit * jnp.mean(a * unit, axis=1, keepdims=True))
    b.gmid[...] = gm
    gb = gm.astype(BF16)
    b.gb[c] = gb
    for k in (3, 1, 2, 0):
        i = plane(k)[0]
        b.gasend[i] = nt(gb, b.wout[i].reshape(hw, width)).astype(BF16)
        if k:
            swap(b.gasend, b.ga, s.x_s.at[2], s.x_r.at[2], k).start()
        else:
            b.ga[c] = b.gasend[c]
    reduce_side(*red0, 1)
    reduce_side(*red0, 2)
    sum_middle(GATE)

    def attend_back(k):
        i = plane(k)[0]
        if k:
            swap_recv(b.gasend, b.ga, s.x_s.at[2], s.x_r.at[2], k)
        blk = b.qkv[i]
        gab = b.ga[i]
        gq, gk, gv = [], [], []
        for h in range(heads):
            q = blk[:, h * HEAD : (h + 1) * HEAD]
            key = blk[:, hw + h * HEAD : hw + (h + 1) * HEAD]
            v = blk[:, 2 * hw + h * HEAD : 2 * hw + (h + 1) * HEAD]
            ga = gab[:, h * HEAD : (h + 1) * HEAD]
            p = b.probs[i, h]
            gp = nt(ga, v)
            gs = (p * (gp - jnp.sum(p * gp, axis=1, keepdims=True))).astype(BF16)
            gq.append(nn(gs, key) * scale)
            gk.append(tn(gs, q) * scale)
            gv.append(tn(p.astype(BF16), ga))
        b.gqkv[i] = jnp.concatenate(gq + gk + gv, axis=1).astype(BF16)
        b.p[2][i] = nt(b.gqkv[i], b.wcol[QKV].reshape(width, fw)).astype(BF16)

    attend_back(3)
    red_start(red2)
    relay_start(*gb_way)
    attend_back(1)
    reduce_side(*red2, 1)
    attend_back(2)
    reduce_side(*red2, 2)
    attend_back(0)
    col_grad(QKV, b.n1, b.gqkv)
    sum_middle(UP)
    sum_start(QKV)
    relay_pass(*gb_way)
    rows_out(od, sum_end(DOWN))


    gn = red_sum(red2)
    x = b.trecv[...].astype(F32).reshape(rows, width)
    inv = lax.rsqrt(jnp.mean(x * x, axis=1, keepdims=True) + EPSILON)
    unit = x * inv
    b.ggain[0:1] = jnp.sum(gn * unit, axis=0, keepdims=True)
    a = gn * b.gain[0:1]
    gx = b.gmid[...] + inv * (a - unit * jnp.mean(a * unit, axis=1, keepdims=True))
    b.isend[...] = gx.reshape(nd, per, width).astype(BF16)
    all_peers(lambda to: b.isend.at[to], b.irecv, s.i_s, s.i_r)
    b.irecv[dp] = b.isend[dp]
    b.hsend[...] = jnp.concatenate([tile_of(b.ggain[0:1]), tile_of(b.ggain[1:2])], axis=0)
    all_peers(lambda to: b.hsend, b.hrecv, s.h_s, s.h_r)
    b.hrecv[dp] = b.hsend[...]

    res = b.middle[...] + red_sum(red0)
    b.lsend[...] = res.reshape(nd, per, width).astype(BF16)
    all_peers(lambda to: b.lsend.at[to], b.lrecv, s.l_s, s.l_r)
    b.lrecv[dp] = b.lsend[dp]
    relay_done(*gb_way)
    gb_all = b.gb[...].reshape(toks, width)
    b.gout[...] = (
        tn(b.att[...].reshape(toks, hw), gb_all).reshape(zn, CORES, row_dev, width).astype(BF16)
    )
    presum(OUT, half_of(OUT), b.cout).start()
    sum_middle(QKV)
    sum_start(OUT)

    col_end(GATE)
    all_peers_recv(lambda at: b.lsend.at[at], b.lrecv, s.l_s, s.l_r)
    pick = b.pick[...]
    lout[...] = tn(pick, b.lrecv[...].reshape(rows, width)).astype(BF16)
    sum_middle(OUT)
    col_end(UP)
    all_peers_recv(lambda at: b.hsend, b.hrecv, s.h_s, s.h_r)
    b.hpart[f] = jnp.sum(b.hrecv[...], axis=0)
    hmirror = remote(b.hpart.at[f], b.hpart.at[f], s.hb_s, s.hb_r, sib)
    hmirror.start()
    all_peers_recv(lambda at: b.isend.at[at], b.irecv, s.i_s, s.i_r)
    igrad[...] = tn(pick, b.irecv[...].reshape(rows, width)).astype(BF16)
    remote(b.hpart.at[other], b.hpart.at[other], s.hb_s, s.hb_r, sib).wait_recv()
    gain_sum = b.hpart[0] + b.hpart[1]
    ogain1[...] = my_gain(gain_sum[:gw])
    ogain2[...] = my_gain(gain_sum[gw:])
    col_recv(GATE)
    hidden_out(og, GATE)
    col_end(QKV)
    col_recv(UP)
    hidden_out(ou, UP)
    rows_out(oo, sum_end(OUT))
    col_recv(QKV)
    heads_out(oq, 0)
    heads_out(ok, 1)
    heads_out(ov, 2)

    gmirror.wait_send()
    hmirror.wait_send()
    all_peers_sent(lambda to: gains, b.grecv, s.g_s, s.g_r)
    all_peers_sent(lambda to: b.tsend.at[to], b.trecv, s.t_s, s.t_r)
    all_peers_sent(lambda to: b.csend.at[to], b.crecv, s.c_s, s.c_r)
    all_peers_sent(lambda to: b.lsend.at[to], b.lrecv, s.l_s, s.l_r)
    all_peers_sent(lambda to: b.isend.at[to], b.irecv, s.i_s, s.i_r)
    all_peers_sent(lambda to: b.hsend, b.hrecv, s.h_s, s.h_r)
    gather_sent(b.mask, s.m_s, s.m_r)
    for k in range(TP):
        for way in (n1_way, call_way, n2_way, gb_way, out_way):
            relay(*way, k).wait_send()
    for src, dst, land, send, recv in (red0, red1, red2):
        for k in (3, 0):
            halves(src, land, send, recv, k).wait_send()
        for k in (1, 2):
            side(src, dst, send, recv, k).wait_send()
    for k in range(1, TP):
        swap(b.att, b.attall, s.x_s.at[0], s.x_r.at[0], k).wait_send()
        swap(b.gasend, b.ga, s.x_s.at[2], s.x_r.at[2], k).wait_send()
        out_mirror(k, f).wait_send()
        for piece in (QKV, GATE, UP):
            spread(piece, k).wait_send()
            home(piece, k).wait_send()
    for piece in (QKV, GATE, UP, OUT, DOWN):
        line_sent(piece)
        sum_sent(piece)


def _log2(n):
    return n.bit_length() - 1


def kernel_takes(dp_count, core_count, rows, width, hidden):
    pieces = dp_count * core_count
    zn = dp_count // TP
    return (
        core_count == CORES
        and dp_count % TP == 0
        and rows == 128
        and rows % dp_count == 0
        and rows // dp_count == 8
        and width == zn * 256
        and width // HEAD == dp_count
        and width // pieces == HEAD // CORES
        and hidden % pieces == 0
        and hidden // pieces <= PAD
        and PAD * CORES * zn % 256 == 0
        and zn == 4
    )


def planned(
    dp_count,
    tokens,
    dealing,
    lengths,
    norm1_gain,
    w_query,
    w_key,
    w_value,
    w_out,
    norm2_gain,
    w_gate,
    w_up,
    w_down,
    cotangent,
):
    nd = dp_count
    zn = nd // TP
    rows, width = tokens.shape
    pieces = nd * CORES
    row_dev = width // pieces
    hidden = w_gate.shape[0] * pieces // width
    unit = hidden // pieces
    hw = width // TP
    fw = PAD * CORES * zn
    gw = width // 128
    toks = TP * rows
    per = rows // nd
    V = pltpu.VMEM
    bufs = dict(
        pick=V((rows, rows), BF16),
        own=V((3, TP, row_dev, fw), BF16),
        gown=V((2 * gw, 128), BF16),
        flat=V((PAD * width // 128, 128), F32),
        pairs=V((fw // 128, row_dev, 128), F32),
        wide=V((TP, fw // 128, row_dev, 128), F32),
        tsend=V((nd, per, width), BF16),
        trecv=V((nd, per, width), BF16),
        csend=V((nd, per, width), BF16),
        crecv=V((nd, per, width), BF16),
        lsend=V((nd, per, width), BF16),
        lrecv=V((nd, per, width), BF16),
        isend=V((nd, per, width), BF16),
        irecv=V((nd, per, width), BF16),
        grecv=V((nd, 2 * gw, 128), BF16),
        gpart=V((CORES, 2 * gw, 128), BF16),
        gain=V((8, width), F32),
        ggain=V((8, width), F32),
        hsend=V((2 * gw, 128), F32),
        hrecv=V((nd, 2 * gw, 128), F32),
        hpart=V((CORES, 2 * gw, 128), F32),
        mask=V((TP, rows, rows), BF16),
        wcol=V((3, zn, TP, CORES, row_dev, fw), BF16),
        wout=V((TP, zn, CORES, row_dev, width), BF16),
        wdown=V((zn, CORES, PAD, width), BF16),
        n1=V((TP, rows, width), BF16),
        n2=V((TP, rows, width), BF16),
        call=V((TP, rows, width), BF16),
        gb=V((TP, rows, width), BF16),
        qkv=V((TP, rows, 3 * hw), BF16),
        probs=V((TP, hw // HEAD, rows, rows), F32),
        att=V((TP, rows, hw), BF16),
        attall=V((TP, rows, hw), BF16),
        gasend=V((TP, rows, hw), BF16),
        middle=V((rows, width), F32),
        gmid=V((rows, width), F32),
        gate=V((TP, rows, fw), F32),
        up=V((TP, rows, fw), F32),
        hid=V((TP, rows, fw), BF16),
        ggate=V((TP, rows, fw), BF16),
        gup=V((TP, rows, fw), BF16),
        ga=V((TP, rows, hw), BF16),
        gqkv=V((TP, rows, 3 * hw), BF16),
        gcol=V((3, zn, TP, CORES, row_dev, fw), BF16),
        ccol=V((3, zn, TP, row_dev, fw), BF16),
        scol=V((3, zn, TP, row_dev, fw), BF16),
        ecol=V((3, 4, TP, row_dev, fw), BF16),
        tcol=V((3, TP, row_dev, fw), BF16),
        rcol=V((3, TP, row_dev, fw), BF16),
        gout=V((zn, CORES, row_dev, width), BF16),
        cout=V((zn, row_dev, width), BF16),
        sout=V((zn, row_dev, width), BF16),
        eout=V((4, row_dev, width), BF16),
        gdown=V((zn, CORES, PAD, width), BF16),
        cdown=V((zn, PAD, width), BF16),
        sdown=V((zn, PAD, width), BF16),
        edown=V((4, PAD, width), BF16),
    )
    bufs.update(
        p=[V((TP, rows, width), BF16) for _ in range(3)],
        q=[V((2, rows, width), BF16) for _ in range(3)],
        land=V((3, 2, rows // 2, width), BF16),
    )
    S = pltpu.SemaphoreType.DMA
    each = S((nd,))
    sems = dict(
        g_s=each,
        g_r=each,
        t_s=each,
        t_r=each,
        c_s=each,
        c_r=each,
        l_s=each,
        l_r=each,
        i_s=each,
        i_r=each,
        h_s=each,
        h_r=each,
        gb_s=S(()),
        gb_r=S(()),
        hb_s=S(()),
        hb_r=S(()),
        m_s=S((TP,)),
        m_r=S((TP,)),
        s1_s=S((3, TP)),
        s1_r=S((3, TP)),
        z_s=S((5, 2 * zn)),
        z_r=S((5, zn)),
        b_s=S((5, zn)),
        b_r=S((5, zn)),
        a_s=S((4, TP)),
        a_r=S((4, TP)),
        o_s=S((TP,)),
        o_r=S((TP,)),
        om_s=S((TP,)),
        om_r=S((TP,)),
        x_s=S((5, TP)),
        x_r=S((5, TP)),
        p_s=S((5,)),
        p_r=S((5,)),
        e_s=S((5, 4)),
        e_r=S((5, 4)),
        h2_s=S((3, TP)),
        h2_r=S((3, TP)),
    )
    n_io = 13 + 11
    spaces, shape_of = jax.tree.flatten((bufs, sems))

    def entry(*refs):
        io, rest = refs[:n_io], refs[n_io:]
        b, s = jax.tree.unflatten(shape_of, rest)
        block_kernel((nd, zn, rows, width, hw, fw, unit), *io, SimpleNamespace(**b), SimpleNamespace(**s))

    vm = pl.BlockSpec(memory_space=pltpu.VMEM)
    sm = pl.BlockSpec(memory_space=pltpu.SMEM)
    head_span = jax.ShapeDtypeStruct((row_dev * width // 128, 128), F32)
    hidden_span = jax.ShapeDtypeStruct((unit * width // 128, 128), F32)
    gain_span = jax.ShapeDtypeStruct((1, row_dev), F32)
    row_block = jax.ShapeDtypeStruct((rows, width), BF16)

    def lanes(v):
        return v.reshape(-1, 128)

    outs = pl.pallas_call(
        entry,
        out_shape=(row_block, row_block, gain_span)
        + (head_span,) * 4
        + (gain_span,)
        + (hidden_span,) * 3,
        in_specs=[vm, vm, vm, sm] + [vm] * 9,
        out_specs=(vm,) * 11,
        scratch_shapes=spaces,
        compiler_params=pltpu.CompilerParams(
            collective_id=0, has_side_effects=True, vmem_limit_bytes=VMEM_BYTES
        ),
        name="block_fwd_bwd",
    )(
        tokens,
        cotangent,
        dealing.reshape(1, rows),
        lengths,
        norm1_gain.reshape(1, row_dev),
        norm2_gain.reshape(1, row_dev),
        lanes(w_query),
        lanes(w_key),
        lanes(w_value),
        lanes(w_out),
        lanes(w_gate),
        lanes(w_up),
        lanes(w_down),
    )
    whole = pl.BlockSpec(memory_space=pl.ANY)

    def hand_over(*refs):
        n = len(refs) // 2
        copies = [pltpu.make_async_copy(refs[i], refs[n + i], refs[-1].at[i]) for i in range(n)]
        for cp in copies:
            cp.start()
        for cp in copies:
            cp.wait()

    outs = pl.pallas_call(
        hand_over,
        out_shape=tuple(jax.ShapeDtypeStruct(v.shape, v.dtype) for v in outs),
        in_specs=[vm] * len(outs),
        out_specs=(whole,) * len(outs),
        scratch_shapes=[S((len(outs),))],
        name="hand_over",
    )(*outs)
    return tuple(outs[:2]) + tuple(v.reshape(-1) for v in outs[2:])


def dispatch(dp_count, core_count, *args):
    tokens, w_gate = args[0], args[9]
    rows, width = tokens.shape
    hidden = w_gate.shape[0] * dp_count * core_count // width
    if kernel_takes(dp_count, core_count, rows, width, hidden):
        return planned(dp_count, *args)
    return body(*args)


def solution(mesh):
    in_specs = (
        P(("dp", "fsdp"), None),
        P(("dp", "fsdp")),
        P(("dp", "fsdp"), None),
        P(("dp", "fsdp")),
        P(("dp", "fsdp")),
        P(("dp", "fsdp")),
        P(("dp", "fsdp")),
        P(("dp", "fsdp")),
        P(("dp", "fsdp")),
        P(("dp", "fsdp")),
        P(("dp", "fsdp")),
        P(("dp", "fsdp")),
        P(("dp", "fsdp"), None),
    )
    out_specs = (
        P(("dp", "fsdp"), None),
        P(("dp", "fsdp"), None),
        P(("dp", "fsdp")),
        P(("dp", "fsdp")),
        P(("dp", "fsdp")),
        P(("dp", "fsdp")),
        P(("dp", "fsdp")),
        P(("dp", "fsdp")),
        P(("dp", "fsdp")),
        P(("dp", "fsdp")),
        P(("dp", "fsdp")),
    )
    return jax.shard_map(
        functools.partial(dispatch, mesh.shape["dp"], mesh.shape["fsdp"]),
         mesh=mesh, in_specs=in_specs, out_specs=out_specs, check_vma=False)
```
